32 devices in a mesh: dp: 16 (over z, x, core), tensor: 2 (over y).
Axes of the slice: x: 2, y: 2, z: 4, core: 2. Of those that a mesh axis runs over, the one named last changes fastest.
Arguments:
- inputs: bfloat16 [16384, 1024], P(('dp', 'tensor')), may hold values from -6 to 6
- lengths: int32 [32], P('dp'), may hold values from 128 to 512, as said below
- w_qkv: bfloat16 [1024, 3, 1024], P(None, None, 'tensor'), may hold values from -0.1875 to 0.1875
- b_qv: bfloat16 [2, 1024], P(None, 'tensor'), may hold values from -3 to 3
- w_out: bfloat16 [1024, 1024], P('tensor'), may hold values from -1.5 to 1.5
- b_out: bfloat16 [1024], replicated, may hold values from -3 to 3
- gain_one: bfloat16 [1024], replicated, may hold values from 0.5 to 1.5
- shift_one: bfloat16 [1024], replicated, may hold values from -3 to 3
- w_in: bfloat16 [1024, 4096], P(None, 'tensor'), may hold values from -0.1875 to 0.1875
- b_in: bfloat16 [4096], P('tensor'), may hold values from -3 to 3
- w_down: bfloat16 [4096, 1024], P('tensor'), may hold values from -0.09375 to 0.09375
- b_down: bfloat16 [1024], replicated, may hold values from -3 to 3
- gain_two: bfloat16 [1024], replicated, may hold values from 0.5 to 1.5
- shift_two: bfloat16 [1024], replicated, may hold values from -3 to 3
- cotangent: bfloat16 [16384, 1024], P(('dp', 'tensor')), may hold values from -6 to 6
Outputs:
- output: bfloat16 [16384, 1024], P(('dp', 'tensor'))
- grad_inputs: bfloat16 [16384, 1024], P(('dp', 'tensor'))
- grad_w_qkv: float32 [1024, 3, 1024], P(None, None, 'tensor')
- grad_b_qv: float32 [2, 1024], P(None, 'tensor')
- grad_w_out: float32 [1024, 1024], P('tensor')
- grad_b_out: float32 [1024], replicated
- grad_gain_one: float32 [1024], replicated
- grad_shift_one: float32 [1024], replicated
- grad_w_in: float32 [1024, 4096], P(None, 'tensor')
- grad_b_in: float32 [4096], P('tensor')
- grad_w_down: float32 [4096, 1024], P('tensor')
- grad_b_down: float32 [1024], replicated
- grad_gain_two: float32 [1024], replicated
- grad_shift_two: float32 [1024], replicated
The draws below stay inside these ranges and needn't reach their ends.
Inputs may be any that keep to these rules, and one draw needn't show every extreme that they name: `lengths`: each sequence's count of valid token slots; slots at or past it are padding. Some sequence has exactly 512 and some exactly 128.
All inputs are finite; a program needn't handle non-finite values.
Results may differ from the reference program's by a relative error of at most 0.02.
Values may be sent and summed in bfloat16 or wider, within the bound.
A program may use at most 128 MiB of HBM per device.

```python
import jax
import jax.numpy as jnp
from jax import lax

D = 1024
FF = 4096
HEADS = 16
HEAD = 64
SEQ = 512
LEAST = 128
SEQ_DEV = 2
SEQS = 32
TOKENS = 16384
N_DP = 16


def draw_lengths(key, part):
    key_base = jax.random.fold_in(key, 11)
    key_top = jax.random.fold_in(key, 12)
    key_low = jax.random.fold_in(key, 13)
    drawn = jax.random.randint(key_base, (SEQS,), LEAST, SEQ + 1)
    top_at = jax.random.randint(key_top, (), 0, SEQS)
    low_at = (top_at + 1 + jax.random.randint(key_low, (), 0, SEQS - 1)) % SEQS
    places = jnp.arange(SEQS)
    drawn = jnp.where(places == top_at, SEQ, drawn)
    drawn = jnp.where(places == low_at, LEAST, drawn)
    return drawn.astype(jnp.int32)


def block_scale(rng, shape, cuts, low, largest):
    gain = 1.0
    for axis_at, shards_of in cuts:
        steps = jax.random.uniform(jax.random.fold_in(jax.random.fold_in(rng, 6), axis_at), (shards_of,), jnp.float32, low / len(cuts), largest / len(cuts))
        gain = gain * jnp.repeat(jnp.exp(steps), shape[axis_at] // shards_of).reshape((-1,) + (1,) * (len(shape) - 1 - axis_at))
    return gain


def bell_draw(own_key, shape, scale, most, split=(), held_as=jnp.bfloat16):
    loudness = block_scale(own_key, shape, split, -0.22, 0.18) if split else 1.0
    values = jax.random.normal(own_key, shape, jnp.float32) * scale * loudness
    return jnp.minimum(jnp.maximum(values, -most), most).astype(held_as)


def setup_inputs(seed: int = 0) -> dict:
    keys = jax.random.split(jax.random.key(seed), 16)
    return {
        "inputs": bell_draw(keys[0], (TOKENS, D), 1.0, 6.0, ((0, 32),)),
        "lengths": draw_lengths(jax.random.fold_in(keys[15], 71), 0),
        "w_qkv": bell_draw(keys[2], (D, 3, D), D ** -0.5, 0.1875, ((2, 2),)),
        "b_qv": bell_draw(keys[3], (2, D), 0.5, 3.0, ((1, 2),)),
        "w_out": bell_draw(keys[4], (D, D), (D // 64) ** -0.5, 1.5, ((0, 2),)),
        "b_out": bell_draw(keys[5], (D,), 0.5, 3.0),
        "gain_one": jnp.clip(1.0 + 0.1 * jax.random.normal(keys[6], (D,), jnp.float32), 0.5, 1.5).astype(jnp.bfloat16),
        "shift_one": bell_draw(keys[7], (D,), 0.5, 3.0),
        "w_in": bell_draw(keys[8], (D, FF), D ** -0.5, 0.1875, ((1, 2),)),
        "b_in": bell_draw(keys[9], (FF,), 0.5, 3.0, ((0, 2),)),
        "w_down": bell_draw(keys[10], (FF, D), FF ** -0.5, 0.09375, ((0, 2),)),
        "b_down": bell_draw(keys[11], (D,), 0.5, 3.0),
        "gain_two": jnp.clip(1.0 + 0.1 * jax.random.normal(keys[12], (D,), jnp.float32), 0.5, 1.5).astype(jnp.bfloat16),
        "shift_two": bell_draw(keys[13], (D,), 0.5, 3.0),
        "cotangent": bell_draw(keys[14], (TOKENS, D), 1.0, 6.0, ((0, 32),)),
    }


EPSILON = 1e-12
PRECISE = lax.Precision.HIGHEST

@jax.custom_vjp
def low(v):
    return lax.optimization_barrier(v.astype(jnp.bfloat16)).astype(jnp.float32)

@jax.custom_vjp
def low_back(v):
    return v

def low_keep(v):
    return (low(v), None)

def low_pass(kept, grad):
    return (grad,)

def back_keep(v):
    return (v, None)

def back_low(kept, grad):
    return (low(grad),)
low.defvjp(low_keep, low_pass)
low_back.defvjp(back_keep, back_low)

def layer_norm(values, gain_vec, shift_vec):
    center = values - lax.optimization_barrier(jnp.mean(values, axis=-1, keepdims=True))
    spread = lax.optimization_barrier(jnp.mean(center * center, axis=-1, keepdims=True))
    return center * lax.rsqrt(spread + EPSILON) * gain_vec + shift_vec

def attend(queries, key_rows, value_rows, length):
    score_scale = HEAD ** (-0.5)
    scores = jnp.einsum('qhe,khe->hqk', queries, key_rows, precision=PRECISE)
    places = jnp.arange(SEQ)
    scores = jnp.where((places < length)[None, None, :], scores * score_scale, -1000000000.0)
    scores = low_back(scores)
    probability = low(jax.nn.softmax(scores, axis=-1))
    return jnp.einsum('hqk,khe->qhe', probability, value_rows, precision=PRECISE)

def group_forward(weights, tokens_group, lengths_group):
    w_qkv, b_qv, w_out, b_out, gain_one, shift_one, w_in, b_in, w_down, b_down, gain_two, shift_two = weights
    bias_three = jnp.stack([b_qv[0], jnp.zeros_like(b_qv[0]), b_qv[1]])
    projected = jnp.einsum('td,dcf->tcf', tokens_group, w_qkv, precision=PRECISE) + bias_three
    projected = low(low_back(projected))
    shaped = projected.reshape(SEQ_DEV, SEQ, 3, HEADS, HEAD)
    context = jax.vmap(jax.checkpoint(attend))(shaped[:, :, 0], shaped[:, :, 1], shaped[:, :, 2], lengths_group)
    context = low(low_back(context.reshape(SEQ_DEV * SEQ, D)))
    branch = low_back(jnp.dot(context, w_out, precision=PRECISE) + b_out)
    normed = layer_norm(tokens_group + branch, gain_one, shift_one)
    hidden = low_back(jnp.dot(low(normed), w_in, precision=PRECISE) + b_in)
    active = low(jax.nn.gelu(hidden, approximate=False))
    second = low_back(jnp.dot(active, w_down, precision=PRECISE) + b_down)
    return layer_norm(normed + second, gain_two, shift_two)

def reference(inputs, lengths, w_qkv, b_qv, w_out, b_out, gain_one, shift_one, w_in, b_in, w_down, b_down, gain_two, shift_two, cotangent):
    weights = tuple((weight.astype(jnp.float32) for weight in (w_qkv, b_qv, w_out, b_out, gain_one, shift_one, w_in, b_in, w_down, b_down, gain_two, shift_two)))
    blocks = inputs.astype(jnp.float32).reshape(N_DP, SEQ_DEV * SEQ, D)
    groups = lengths.reshape(N_DP, SEQ_DEV)
    places = jnp.arange(SEQ)
    valid_rows = (places[None, None, :] < groups[:, :, None]).astype(jnp.float32).reshape(N_DP, SEQ_DEV * SEQ, 1)
    seed_grad = cotangent.astype(jnp.float32).reshape(N_DP, SEQ_DEV * SEQ, D) * valid_rows
    step_forward = jax.checkpoint(group_forward)

    def forward(blocks_in, weights_in):

        def advance(carried, element):
            return (carried, step_forward(weights_in, element[0], element[1]))
        _, result = lax.scan(advance, jnp.zeros((), jnp.float32), (blocks_in, groups))
        return result
    result, pullback = jax.vjp(forward, blocks, weights)
    grad_blocks, grads = pullback(seed_grad)
    return (result.reshape(TOKENS, D).astype(jnp.bfloat16), grad_blocks.reshape(TOKENS, D).astype(jnp.bfloat16), grads[0], grads[1], grads[2], grads[3], grads[4], grads[5], grads[6], grads[7], grads[8], grads[9], grads[10], grads[11])
```

```python
import functools

import jax
import jax.numpy as jnp
from jax import lax
from jax.experimental import pallas as pl
from jax.experimental.pallas import tpu as pltpu
from jax.sharding import PartitionSpec as P

MESH = pl.DeviceIdType.MESH
N_Z, N_X = 4, 2
TILE = 512


def place():
    dp = lax.axis_index("dp")
    return dp // (2 * N_X), (dp // 2) % N_X, dp % 2, lax.axis_index("tensor")


def at(z, x, c, y):
    return ((z * N_X + x) * 2 + c, y)


def greet(peers):
    barrier = pltpu.get_barrier_semaphore()
    for peer in peers:
        pl.semaphore_signal(barrier, inc=1, device_id=peer, device_id_type=MESH)
    pl.semaphore_wait(barrier, len(peers))


def copy_to(src, dst, send_sem, recv_sem, peer):
    return pltpu.make_async_remote_copy(
        src_ref=src, dst_ref=dst, send_sem=send_sem, recv_sem=recv_sem,
        device_id=peer, device_id_type=MESH,
    )


def gather_kernel(*refs):
    count = (len(refs) - 2) // 2
    mine, other = refs[:count], refs[count : 2 * count]
    send, recv = refs[2 * count :]
    count = count - 1
    z, x, c, y = place()
    zb = z % 2
    to_y, to_x, to_z, to_c = at(z, x, c, 1 - y), at(z, 1 - x, c, y), at(z + 1 - 2 * zb, x, c, y), at(z, x, 1 - c, y)
    greet([to_y, to_x, to_z, to_c])

    def rows(n, core, group, first, parts):
        size = mine[n].shape[0] // 16
        return pl.ds(pl.multiple_of(core * 8 * size + group * 4 * size + first * size, 8), parts * size)

    def message(n, kind):
        pair_a, pair_b = (0, 2 * zb, 2), (1, 2 * x, 2)
        one_a, one_b = (0, 2 * zb + x, 1), (1, 2 * x + zb, 1)
        far_a, far_b = (0, 2 * (1 - zb), 2), (1, 2 * (1 - x), 2)
        what, peer = [
            (one_a, to_y), (one_b, to_y), (one_a, to_x), (one_b, to_z),
            (pair_a, to_z), (pair_b, to_x), (pair_a, to_c), (pair_b, to_c), (far_a, to_c), (far_b, to_c),
        ][kind]
        source = (mine if kind < 2 else other)[n]
        span = rows(n, c, *what)
        return copy_to(source.at[span], other[n].at[span], send.at[n, kind], recv.at[n, kind], peer)

    bias = copy_to(mine[count], other[count], send.at[count, 0], recv.at[count, 0], to_y)
    bias.start()
    for n in range(count):
        message(n, 0).start()
        message(n, 1).start()

    def stage(n, step):
        if step == 0:
            message(n, 0).wait_recv(); message(n, 2).start()
            message(n, 1).wait_recv(); message(n, 3).start()
        if step == 1:
            message(n, 2).wait_recv(); message(n, 4).start(); message(n, 6).start()
            message(n, 3).wait_recv(); message(n, 5).start(); message(n, 7).start()
        if step == 2:
            message(n, 4).wait_recv(); message(n, 8).start()
            message(n, 5).wait_recv(); message(n, 9).start()
        if step == 3:
            for kind in (6, 7, 8, 9):
                message(n, kind).wait_recv()
            for kind in range(10):
                message(n, kind).wait_send()

    for t in range(count + 3):
        for step in range(4):
            if 0 <= t - step < count:
                stage(t - step, step)
    bias.wait()


def gather(arrays, collective_id):
    count = len(arrays)
    return pl.pallas_call(
        gather_kernel,
        out_shape=[jax.ShapeDtypeStruct(a.shape, a.dtype) for a in arrays],
        in_specs=[pl.BlockSpec(memory_space=pl.ANY)] * count,
        out_specs=[pl.BlockSpec(memory_space=pl.ANY)] * count,
        scratch_shapes=[pltpu.SemaphoreType.DMA((count, 10)), pltpu.SemaphoreType.DMA((count, 10))],
        compiler_params=pltpu.CompilerParams(collective_id=collective_id, has_side_effects=True),
    )(*arrays)


MESSAGES = 12


def reduce_kernel(count, own_hbm, oth_hbm, small_in, out_hbm, small_out,
                  own, oth, r1, ry, rx, rz, agc, stage_buf, small, s0, s1, s2, s3, s4,
                  load_sem, send, recv, out_sem, small_send, small_recv):
    z, x, c, y = place()
    to_c, to_y, to_x = at(z, x, 1 - c, y), at(z, x, c, 1 - y), at(z, 1 - x, c, y)
    z_of = [(z + d) % N_Z for d in (1, 2, 3)]
    to_z = [at(v, x, c, y) for v in z_of]
    for k in range(2):
        pltpu.make_async_copy(own_hbm.at[pl.ds(k * count // 2, count // 2)], own.at[pl.ds(k * count // 2, count // 2)], load_sem.at[0, k]).start()
        pltpu.make_async_copy(oth_hbm.at[pl.ds(k * count // 2, count // 2)], oth.at[pl.ds(k * count // 2, count // 2)], load_sem.at[1, k]).start()
    small[...] = small_in[...]
    greet([to_c, to_y, to_x] + to_z)
    half, quarter, part = TILE // 2, TILE // 4, TILE // 16
    c_rows = pl.ds(pl.multiple_of(c * half, half), half)
    cn_rows = pl.ds(pl.multiple_of((1 - c) * half, half), half)
    x_rows = pl.ds(pl.multiple_of(c * half + x * quarter, quarter), quarter)
    xn_rows = pl.ds(pl.multiple_of(c * half + (1 - x) * quarter, quarter), quarter)

    def z_rows(v):
        return pl.ds(pl.multiple_of(c * half + x * quarter + v * part, part), part)

    def message(k, kind):
        if kind == 0: src, dst, peer = own.at[k, cn_rows], r1.at[k, 0], to_c
        if kind == 1: src, dst, peer = oth.at[k, cn_rows], r1.at[k, 1], to_c
        if kind == 2: src, dst, peer = oth.at[k, c_rows], ry.at[k], to_y
        if kind == 3: src, dst, peer = own.at[k, xn_rows], rx.at[k], to_x
        if 4 <= kind < 7: src, dst, peer = own.at[k, z_rows(z_of[kind - 4])], rz.at[k, kind - 4], to_z[kind - 4]
        if 7 <= kind < 10: src, dst, peer = oth.at[k, z_rows(z)], oth.at[k, z_rows(z)], to_z[kind - 7]
        if kind == 10: src, dst, peer = oth.at[k, x_rows], oth.at[k, x_rows], to_x
        if kind == 11: src, dst, peer = oth.at[k, c_rows], agc.at[k], to_c
        return copy_to(src, dst, send.at[k, kind], recv.at[k, kind], peer)

    def add_into(dst, src, n):
        def body(i, _):
            r = pl.ds(pl.multiple_of(i * 64, 64), 64)
            dst[r, :] = dst[r, :] + src[r, :]
            return 0
        lax.fori_loop(0, n // 64, body, 0)

    def wait(k, kinds):
        for kind in kinds:
            message(k, kind).wait()

    def out_copy(k, which):
        rows = c_rows if which == 0 else cn_rows
        return pltpu.make_async_copy(stage_buf.at[which, k % 2], out_hbm.at[k, rows], out_sem.at[which, k % 2])

    def widen(k, which):
        src = oth.at[k, c_rows] if which == 0 else agc.at[k]
        @pl.when(k >= 2)
        def _():
            out_copy(k - 2, which).wait()
        def body(i, _):
            r = pl.ds(pl.multiple_of(i * 64, 64), 64)
            stage_buf[which, k % 2, r, :] = src[r, :].astype(jnp.float32)
            return 0
        lax.fori_loop(0, half // 64, body, 0)
        out_copy(k, which).start()

    def step(k, s):
        if s == 0:
            for b in range(2):
                @pl.when(k == b * count // 2)
                def _():
                    pltpu.make_async_copy(own_hbm.at[pl.ds(b * count // 2, count // 2)], own.at[pl.ds(b * count // 2, count // 2)], load_sem.at[0, b]).wait()
                    pltpu.make_async_copy(oth_hbm.at[pl.ds(b * count // 2, count // 2)], oth.at[pl.ds(b * count // 2, count // 2)], load_sem.at[1, b]).wait()
            message(k, 0).start(); message(k, 1).start()
        if s == 1:
            wait(k, (0, 1))
            add_into(oth.at[k, c_rows], r1.at[k, 1], half)
            message(k, 2).start()
            add_into(own.at[k, c_rows], r1.at[k, 0], half)
        if s == 2:
            wait(k, (2,))
            add_into(own.at[k, c_rows], ry.at[k], half)
            message(k, 3).start()
        if s == 3:
            wait(k, (3,))
            add_into(own.at[k, x_rows], rx.at[k], quarter)
            for kind in (4, 5, 6): message(k, kind).start()
        if s == 4:
            wait(k, (4, 5, 6))
            total = own[k, z_rows(z), :].astype(jnp.float32)
            for d in range(3):
                total = total + rz[k, d].astype(jnp.float32)
            oth[k, z_rows(z), :] = total.astype(jnp.bfloat16)
            for kind in (7, 8, 9): message(k, kind).start()
        if s == 5:
            wait(k, (7, 8, 9))
            message(k, 10).start()
        if s == 6:
            wait(k, (10,))
            message(k, 11).start()
            widen(k, 0)
        if s == 7:
            wait(k, (11,))
            widen(k, 1)

    zp, zq = at(z + 1 - 2 * (z % 2), x, c, y), at((z + 2) % 4, x, c, y)
    def small_messages(i):
        ss, rr = small_send, small_recv
        if i == 0: return [copy_to(small, s0, ss.at[0], rr.at[0], to_c)]
        if i == 1: return [copy_to(small.at[pl.ds(0, 8)], s1.at[pl.ds(0, 8)], ss.at[1], rr.at[1], to_y),
                           copy_to(small.at[pl.ds(16, 8)], s1.at[pl.ds(8, 8)], ss.at[2], rr.at[2], to_y)]
        if i == 2: return [copy_to(small.at[pl.ds(0, 16)], s2, ss.at[3], rr.at[3], to_x)]
        if i == 3: return [copy_to(small.at[pl.ds(0, 16)], s3, ss.at[4], rr.at[4], zp)]
        if i == 4: return [copy_to(small.at[pl.ds(0, 16)], s4, ss.at[5], rr.at[5], zq)]
    def small_start(i):
        for m in small_messages(i): m.start()
    def small_finish(i):
        for m in small_messages(i): m.wait()
        if i == 0: small[...] = small[...] + s0[...]
        else: small[pl.ds(0, 16), :] = small[pl.ds(0, 16), :] + (s1, s2, s3, s4)[i - 1][...]

    def loop(t, _):
        for s in range(7, -1, -1):
            @pl.when((t >= s) & (t - s < count))
            def _():
                step(t - s, s)
        for i in range(6):
            @pl.when(t == i + 1)
            def _():
                if i > 0: small_finish(i - 1)
                if i < 5: small_start(i)
        return 0
    lax.fori_loop(0, count + 7, loop, 0)
    small_out[...] = small[pl.ds(0, 16), :]
    for k in (count - 2, count - 1):
        for which in (0, 1):
            out_copy(k, which).wait()


def reduce(own, oth, small, collective_id):
    count = own.shape[0]
    h, bf = TILE // 2, jnp.bfloat16
    V = pltpu.VMEM
    dma = pltpu.SemaphoreType.DMA
    any_spec, vm = pl.BlockSpec(memory_space=pl.ANY), pl.BlockSpec(memory_space=pltpu.VMEM)
    return pl.pallas_call(
        functools.partial(reduce_kernel, count),
        out_shape=[jax.ShapeDtypeStruct(own.shape, jnp.float32), jax.ShapeDtypeStruct((16, 1024), jnp.float32)],
        in_specs=[any_spec, any_spec, vm],
        out_specs=[any_spec, vm],
        scratch_shapes=[
            V((count, TILE, TILE), bf), V((count, TILE, TILE), bf), V((count, 2, h, TILE), bf), V((count, h, TILE), bf),
            V((count, h // 2, TILE), bf), V((count, 3, h // 8, TILE), bf), V((count, h, TILE), bf),
            V((2, 2, h, TILE), jnp.float32), V((24, 1024), jnp.float32), V((24, 1024), jnp.float32),
            V((16, 1024), jnp.float32), V((16, 1024), jnp.float32), V((16, 1024), jnp.float32), V((16, 1024), jnp.float32),
            dma((2, 2)), dma((count, MESSAGES)), dma((count, MESSAGES)), dma((2, 2)), dma((6,)), dma((6,)),
        ],
        compiler_params=pltpu.CompilerParams(collective_id=collective_id, has_side_effects=True, vmem_limit_bytes=60 << 20),
    )(own, oth, small)

HEAD = 64
SEQ = 512
SEQ_DEV = 2


EPSILON = 1e-12
NEG_FILL = -1000000000.0


def gelu_exact(values):
    return jax.nn.gelu(values, approximate=False)


def norm_forward(values, gain_vec, shift_vec):
    center = values - jnp.mean(values, axis=-1, keepdims=True)
    spread = jnp.mean(center * center, axis=-1, keepdims=True)
    inverse = lax.rsqrt(spread + EPSILON)
    scaled = center * inverse
    return (scaled * gain_vec + shift_vec, scaled, inverse)


def norm_backward(grad_out, scaled, inverse, gain_vec):
    grad_scaled = grad_out * gain_vec
    mean_one = jnp.mean(grad_scaled, axis=-1, keepdims=True)
    mean_two = jnp.mean(grad_scaled * scaled, axis=-1, keepdims=True)
    grad_in = inverse * (grad_scaled - mean_one - scaled * mean_two)
    return (grad_in, jnp.sum(grad_out * scaled, axis=0), jnp.sum(grad_out, axis=0))


def masked_scores(queries, key_rows, length):
    score_scale = HEAD ** (-0.5)
    scores = (
        jnp.einsum("qhe,khe->hqk", queries, key_rows, preferred_element_type=jnp.float32)
        * score_scale
    )
    key_valid = (jnp.arange(SEQ) < length)[None, None, :]
    return jnp.where(key_valid, scores, NEG_FILL)


def attend_forward(element):
    queries, key_rows, value_rows, length = element
    scores = masked_scores(queries, key_rows, length)
    peak_score = jnp.max(scores, axis=-1, keepdims=True)
    shifted_exp = jnp.exp(scores - peak_score)
    denominator = jnp.sum(shifted_exp, axis=-1, keepdims=True)
    probability = (shifted_exp / denominator).astype(jnp.bfloat16)
    context = jnp.einsum(
        "hqk,khe->qhe", probability, value_rows, preferred_element_type=jnp.float32
    )
    return (context.astype(jnp.bfloat16), (peak_score + jnp.log(denominator))[..., 0])


def attend_backward(element):
    queries, key_rows, value_rows, length, log_total, grad_context = element
    score_scale = HEAD ** (-0.5)
    scores = masked_scores(queries, key_rows, length)
    probability = jnp.exp(scores - log_total[..., None])
    grad_prob = jnp.einsum(
        "qhe,khe->hqk", grad_context, value_rows, preferred_element_type=jnp.float32
    )
    grad_value = jnp.einsum(
        "hqk,qhe->khe",
        probability.astype(jnp.bfloat16),
        grad_context,
        preferred_element_type=jnp.float32,
    )
    grad_scores = probability * (
        grad_prob - jnp.sum(probability * grad_prob, axis=-1, keepdims=True)
    )
    grad_scores = grad_scores.astype(jnp.bfloat16)
    grad_query = (
        jnp.einsum("hqk,khe->qhe", grad_scores, key_rows, preferred_element_type=jnp.float32)
        * score_scale
    )
    grad_key = (
        jnp.einsum("hqk,qhe->khe", grad_scores, queries, preferred_element_type=jnp.float32)
        * score_scale
    )
    return jnp.stack([grad_query, grad_key, grad_value], axis=1).astype(jnp.bfloat16)


def row_mask(lengths, rows_dev):
    places = lax.axis_index("tensor") * rows_dev + jnp.arange(rows_dev)
    sequence_of = places // SEQ
    offset = places % SEQ
    matches = sequence_of[:, None] == jnp.arange(lengths.shape[0])[None, :]
    limit_rows = jnp.sum(jnp.where(matches, lengths[None, :], 0), axis=1)
    return (offset < limit_rows).astype(jnp.float32)[:, None]


def forward_pass(inputs, lengths, weights):
    (
        w_qkv,
        b_qv,
        w_out,
        b_out,
        gain_one,
        shift_one,
        w_in,
        b_in,
        w_down,
        b_down,
        gain_two,
        shift_two,
    ) = weights
    width_dev = w_qkv.shape[2]
    gathered = lax.all_gather(inputs, "tensor", axis=0, tiled=True)
    bias_three = jnp.stack([b_qv[0], jnp.zeros_like(b_qv[0]), b_qv[1]]).astype(jnp.float32)
    projected = (
        jnp.einsum("td,dcf->tcf", gathered, w_qkv, preferred_element_type=jnp.float32) + bias_three
    ).astype(jnp.bfloat16)
    shaped = projected.reshape(SEQ_DEV, SEQ, 3, width_dev // HEAD, HEAD)
    context, log_total = lax.map(
        attend_forward, (shaped[:, :, 0], shaped[:, :, 1], shaped[:, :, 2], lengths)
    )
    context = context.reshape(SEQ_DEV * SEQ, width_dev)
    segment = context
    branch = lax.psum_scatter(
        jnp.dot(segment, w_out, preferred_element_type=jnp.float32).astype(jnp.bfloat16),
        "tensor",
        scatter_dimension=0,
        tiled=True,
    ).astype(jnp.float32) + b_out.astype(jnp.float32)
    normed, scaled_one, inverse_one = norm_forward(
        inputs.astype(jnp.float32) + branch,
        gain_one.astype(jnp.float32),
        shift_one.astype(jnp.float32),
    )
    normed_all = lax.all_gather(normed.astype(jnp.bfloat16), "tensor", axis=0, tiled=True)
    hidden = jnp.dot(normed_all, w_in, preferred_element_type=jnp.float32) + b_in.astype(
        jnp.float32
    )
    active = gelu_exact(hidden).astype(jnp.bfloat16)
    segment = active
    second = lax.psum_scatter(
        jnp.dot(segment, w_down, preferred_element_type=jnp.float32).astype(jnp.bfloat16),
        "tensor",
        scatter_dimension=0,
        tiled=True,
    ).astype(jnp.float32) + b_down.astype(jnp.float32)
    output, scaled_two, inverse_two = norm_forward(
        normed + second, gain_two.astype(jnp.float32), shift_two.astype(jnp.float32)
    )
    return (
        gathered,
        projected,
        context,
        log_total,
        scaled_one,
        inverse_one,
        normed_all,
        hidden,
        active,
        scaled_two,
        inverse_two,
        output,
    )


def general(
    inputs,
    lengths,
    w_qkv,
    b_qv,
    w_out,
    b_out,
    gain_one,
    shift_one,
    w_in,
    b_in,
    w_down,
    b_down,
    gain_two,
    shift_two,
    cotangent,
):
    weights = (
        w_qkv,
        b_qv,
        w_out,
        b_out,
        gain_one,
        shift_one,
        w_in,
        b_in,
        w_down,
        b_down,
        gain_two,
        shift_two,
    )
    first_pass = forward_pass(inputs, lengths, weights)
    output = first_pass[11].astype(jnp.bfloat16)
    recorded = forward_pass(inputs, lengths, weights)
    (
        gathered,
        projected,
        context,
        log_total,
        scaled_one,
        inverse_one,
        normed_all,
        hidden,
        active,
        scaled_two,
        inverse_two,
        _,
    ) = recorded
    rows_dev = inputs.shape[0]
    width_dev = w_qkv.shape[2]
    grad_out = cotangent.astype(jnp.float32) * row_mask(lengths, rows_dev)
    grad_two, grad_gain_two, grad_shift_two = norm_backward(
        grad_out, scaled_two, inverse_two, gain_two.astype(jnp.float32)
    )
    grad_second = grad_two.astype(jnp.bfloat16)
    grad_b_down = jnp.sum(grad_second.astype(jnp.float32), axis=0)
    second_all = lax.all_gather(grad_second, "tensor", axis=0, tiled=True)
    grad_w_down = jnp.einsum("tf,td->fd", active, second_all, preferred_element_type=jnp.float32)
    grad_active = jnp.einsum("td,fd->tf", second_all, w_down, preferred_element_type=jnp.float32)
    _, gelu_pull = jax.vjp(gelu_exact, hidden)
    grad_hidden = gelu_pull(grad_active)[0].astype(jnp.bfloat16)
    grad_b_in = jnp.sum(grad_hidden.astype(jnp.float32), axis=0)
    grad_w_in = jnp.einsum("td,tf->df", normed_all, grad_hidden, preferred_element_type=jnp.float32)
    segment = grad_hidden
    grad_normed = grad_two + lax.psum_scatter(
        jnp.einsum("tf,df->td", segment, w_in, preferred_element_type=jnp.float32).astype(
            jnp.bfloat16
        ),
        "tensor",
        scatter_dimension=0,
        tiled=True,
    ).astype(jnp.float32)
    grad_first, grad_gain_one, grad_shift_one = norm_backward(
        grad_normed, scaled_one, inverse_one, gain_one.astype(jnp.float32)
    )
    grad_branch = grad_first.astype(jnp.bfloat16)
    grad_b_out = jnp.sum(grad_branch.astype(jnp.float32), axis=0)
    branch_all = lax.all_gather(grad_branch, "tensor", axis=0, tiled=True)
    grad_w_out = jnp.einsum("tf,td->fd", context, branch_all, preferred_element_type=jnp.float32)
    grad_context = jnp.einsum(
        "td,fd->tf", branch_all, w_out, preferred_element_type=jnp.float32
    ).astype(jnp.bfloat16)
    heads_dev = width_dev // HEAD
    shaped = projected.reshape(SEQ_DEV, SEQ, 3, heads_dev, HEAD)
    grad_shaped = grad_context.reshape(SEQ_DEV, SEQ, heads_dev, HEAD)
    grad_proj = lax.map(
        attend_backward,
        (shaped[:, :, 0], shaped[:, :, 1], shaped[:, :, 2], lengths, log_total, grad_shaped),
    )
    grad_proj = grad_proj.reshape(SEQ_DEV * SEQ, 3, width_dev)
    grad_w_qkv = jnp.einsum("td,tcf->dcf", gathered, grad_proj, preferred_element_type=jnp.float32)
    grad_b_qv = jnp.sum(grad_proj[:, 0::2].astype(jnp.float32), axis=0)
    segment = grad_proj
    grad_inputs = (
        grad_first
        + lax.psum_scatter(
            jnp.einsum("tcf,dcf->td", segment, w_qkv, preferred_element_type=jnp.float32).astype(
                jnp.bfloat16
            ),
            "tensor",
            scatter_dimension=0,
            tiled=True,
        ).astype(jnp.float32)
    ).astype(jnp.bfloat16)
    small_terms = jnp.stack(
        [grad_gain_one, grad_shift_one, grad_b_out, grad_gain_two, grad_shift_two, grad_b_down]
    )
    grad_w_qkv, grad_b_qv, grad_w_out, grad_w_in, grad_b_in, grad_w_down, small_terms = (
        lax.psum(grad_w_qkv.astype(jnp.bfloat16), "dp").astype(jnp.float32),
        lax.psum(grad_b_qv.astype(jnp.bfloat16), "dp").astype(jnp.float32),
        lax.psum(grad_w_out.astype(jnp.bfloat16), "dp").astype(jnp.float32),
        lax.psum(grad_w_in.astype(jnp.bfloat16), "dp").astype(jnp.float32),
        lax.psum(grad_b_in.astype(jnp.bfloat16), "dp").astype(jnp.float32),
        lax.psum(grad_w_down.astype(jnp.bfloat16), "dp").astype(jnp.float32),
        lax.psum(small_terms.astype(jnp.bfloat16), "dp").astype(jnp.float32),
    )
    small_sums = lax.psum(small_terms, "tensor")
    return (
        output,
        grad_inputs,
        grad_w_qkv,
        grad_b_qv,
        grad_w_out,
        small_sums[2],
        small_sums[0],
        small_sums[1],
        grad_w_in,
        grad_b_in,
        grad_w_down,
        small_sums[5],
        small_sums[3],
        small_sums[4],
    )


def split_by_sequence(
    inputs,
    lengths,
    w_qkv,
    b_qv,
    w_out,
    b_out,
    gain_one,
    shift_one,
    w_in,
    b_in,
    w_down,
    b_down,
    gain_two,
    shift_two,
    cotangent,
):
    f32, bf = jnp.float32, jnp.bfloat16
    rows, width = inputs.shape
    half_width, half_hidden = w_qkv.shape[2], w_in.shape[1]
    length = lengths[lax.axis_index("tensor")]
    wq = w_qkv.transpose(1, 0, 2).reshape(3 * width, half_width)
    bias = jnp.concatenate([b_qv, b_in.reshape(-1, half_width)], axis=0)
    bias = jnp.pad(bias, ((0, 16 - bias.shape[0]), (0, 0)))
    own = (wq, w_out, w_in, w_down, bias)
    halves = [own, gather(list(own), 1)]

    def dot(a, b, ca, cb):
        return lax.dot_general(a, b, (((ca,), (cb,)), ((), ())), preferred_element_type=f32)

    keys_valid = (jnp.arange(rows) < length)[None, None, :]
    saved = []
    branch = b_out.astype(f32)[None]
    for wq_h, wo_h, wi_h, wd_h, bias_h in halves:
        w3 = wq_h.reshape(3, width, half_width)
        q = (dot(inputs, w3[0], 1, 0) + bias_h[0].astype(f32)).astype(bf)
        k = dot(inputs, w3[1], 1, 0).astype(bf)
        v = (dot(inputs, w3[2], 1, 0) + bias_h[1].astype(f32)).astype(bf)
        q, k, v = (t.reshape(rows, -1, HEAD).transpose(1, 0, 2) for t in (q, k, v))
        s = jnp.einsum("hqe,hke->hqk", q, k, preferred_element_type=f32) * HEAD ** (-0.5)
        s = jnp.where(keys_valid, s, NEG_FILL)
        e = jnp.exp(s - jnp.max(s, axis=-1, keepdims=True))
        p = e / jnp.sum(e, axis=-1, keepdims=True)
        context = jnp.einsum("hqk,hke->hqe", p.astype(bf), v, preferred_element_type=f32).astype(bf)
        context = context.transpose(1, 0, 2).reshape(rows, half_width)
        branch = branch + dot(context, wo_h, 1, 0)
        saved.append((w3, q, k, v, p, context))
    normed, xhat1, rstd1 = norm_forward(inputs.astype(f32) + branch, gain_one.astype(f32), shift_one.astype(f32))
    normed_low = normed.astype(bf)
    second = b_down.astype(f32)[None]
    ffn = []
    for wq_h, wo_h, wi_h, wd_h, bias_h in halves:
        hidden = dot(normed_low, wi_h, 1, 0) + bias_h[2 : 2 + half_hidden // half_width].reshape(-1).astype(f32)
        active = gelu_exact(hidden).astype(bf)
        second = second + dot(active, wd_h, 1, 0)
        ffn.append((hidden, active))
    output, xhat2, rstd2 = norm_forward(normed + second, gain_two.astype(f32), shift_two.astype(f32))
    grad_out = cotangent.astype(f32) * (jnp.arange(rows) < length).astype(f32)[:, None]
    g_two, g_gain_two, g_shift_two = norm_backward(grad_out, xhat2, rstd2, gain_two.astype(f32))
    g_second = g_two.astype(bf)
    g_b_down = jnp.sum(g_second.astype(f32), axis=0)
    g_normed = g_two
    tiles = [[], []]
    smalls = [[], []]

    def tile(n, a):
        a = a.astype(bf)
        r, q = a.shape
        tiles[n].append(a.reshape(r // TILE, TILE, q // TILE, TILE).transpose(0, 2, 1, 3).reshape(-1, TILE, TILE))

    for n, (wq_h, wo_h, wi_h, wd_h, bias_h) in enumerate(halves):
        hidden, active = ffn[n]
        tile(n, dot(active, g_second, 0, 0))
        g_active = dot(g_second, wd_h, 1, 1)
        g_hidden = jax.vjp(gelu_exact, hidden)[1](g_active)[0].astype(bf)
        smalls[n].append(jnp.sum(g_hidden.astype(f32), axis=0))
        tile(n, dot(normed_low, g_hidden, 0, 0))
        g_normed = g_normed + dot(g_hidden, wi_h, 1, 1)
    g_first, g_gain_one, g_shift_one = norm_backward(g_normed, xhat1, rstd1, gain_one.astype(f32))
    g_branch = g_first.astype(bf)
    g_b_out = jnp.sum(g_branch.astype(f32), axis=0)
    g_inputs = g_first
    for n, (wq_h, wo_h, wi_h, wd_h, bias_h) in enumerate(halves):
        w3, q, k, v, p, context = saved[n]
        tile(n, dot(context, g_branch, 0, 0))
        g_context = dot(g_branch, wo_h, 1, 1).astype(bf)
        gc = g_context.reshape(rows, -1, HEAD).transpose(1, 0, 2)
        g_p = jnp.einsum("hqe,hke->hqk", gc, v, preferred_element_type=f32)
        g_v = jnp.einsum("hqk,hqe->hke", p.astype(bf), gc, preferred_element_type=f32)
        g_s = (p * (g_p - jnp.sum(p * g_p, axis=-1, keepdims=True))).astype(bf)
        g_q = jnp.einsum("hqk,hke->hqe", g_s, k, preferred_element_type=f32) * HEAD ** (-0.5)
        g_k = jnp.einsum("hqk,hqe->hke", g_s, q, preferred_element_type=f32) * HEAD ** (-0.5)
        for i, g in enumerate((g_q, g_k, g_v)):
            g = g.transpose(1, 0, 2).reshape(rows, half_width).astype(bf)
            tile(n, dot(inputs, g, 0, 0))
            g_inputs = g_inputs + dot(g, w3[i], 1, 1)
            if i != 1:
                smalls[n].append(jnp.sum(g.astype(f32), axis=0))
    shared = jnp.stack([g_gain_one, g_shift_one, g_b_out, g_gain_two, g_shift_two, g_b_down])
    pad = lambda a: jnp.pad(a, ((0, 8 - a.shape[0]), (0, 0)))
    pieces = [pad(jnp.concatenate([s.reshape(-1) for s in smalls[n]]).reshape(-1, width)) for n in (0, 1)]
    small = jnp.concatenate([pad(shared), pieces[0], pieces[1]], axis=0)
    sums, small_sums = reduce(jnp.concatenate(tiles[0]), jnp.concatenate(tiles[1]), small, 2)

    def untile(first, r, q):
        count = (r // TILE) * (q // TILE)
        a = sums[first : first + count].reshape(r // TILE, q // TILE, TILE, TILE)
        return a.transpose(0, 2, 1, 3).reshape(r, q), first + count

    at_tile = 0
    g_w_down, at_tile = untile(at_tile, half_hidden, width)
    g_w_in, at_tile = untile(at_tile, width, half_hidden)
    g_w_out, at_tile = untile(at_tile, half_width, width)
    g_w_qkv, at_tile = untile(at_tile, 3 * width, half_width)
    owned = small_sums[8:].reshape(-1)
    g_b_in = owned[:half_hidden]
    g_b_qv = owned[half_hidden : half_hidden + 2 * half_width].reshape(2, half_width)
    return (
        output.astype(bf),
        g_inputs.astype(bf),
        g_w_qkv.reshape(3, width, half_width).transpose(1, 0, 2),
        g_b_qv,
        g_w_out,
        small_sums[2],
        small_sums[0],
        small_sums[1],
        g_w_in,
        g_b_in,
        g_w_down,
        small_sums[5],
        small_sums[3],
        small_sums[4],
    )


def solution(mesh):
    small_mesh = mesh.shape["tensor"] == 2 and mesh.shape["dp"] == 4 * N_Z
    step = split_by_sequence if small_mesh else general
    in_specs = (
        P(("dp", "tensor"), None),
        P("dp"),
        P(None, None, "tensor"),
        P(None, "tensor"),
        P("tensor", None),
        P(),
        P(),
        P(),
        P(None, "tensor"),
        P("tensor"),
        P("tensor", None),
        P(),
        P(),
        P(),
        P(("dp", "tensor"), None),
    )
    out_specs = (
        P(("dp", "tensor"), None),
        P(("dp", "tensor"), None),
        P(None, None, "tensor"),
        P(None, "tensor"),
        P("tensor", None),
        P(),
        P(),
        P(),
        P(None, "tensor"),
        P("tensor"),
        P("tensor", None),
        P(),
        P(),
        P(),
    )
    return jax.shard_map(step, mesh=mesh, in_specs=in_specs, out_specs=out_specs, check_vma=False)
```

```python
import jax
import jax.numpy as jnp
from jax import lax
from jax.experimental import pallas as pl
from jax.experimental.pallas import tpu as pltpu
from jax.sharding import PartitionSpec as P

MESH = pl.DeviceIdType.MESH
N_Z, N_X = 4, 2
TILE = 512
MESSAGES = 12
VMEM_BYTES = 63 << 20

HEAD = 64
SEQ = 512
SEQ_DEV = 2


EPSILON = 1e-12
NEG_FILL = -1000000000.0


def gelu_exact(values):
    return jax.nn.gelu(values, approximate=False)


def norm_forward(values, gain_vec, shift_vec):
    center = values - jnp.mean(values, axis=-1, keepdims=True)
    spread = jnp.mean(center * center, axis=-1, keepdims=True)
    inverse = lax.rsqrt(spread + EPSILON)
    scaled = center * inverse
    return (scaled * gain_vec + shift_vec, scaled, inverse)


def norm_backward(grad_out, scaled, inverse, gain_vec):
    grad_scaled = grad_out * gain_vec
    mean_one = jnp.mean(grad_scaled, axis=-1, keepdims=True)
    mean_two = jnp.mean(grad_scaled * scaled, axis=-1, keepdims=True)
    grad_in = inverse * (grad_scaled - mean_one - scaled * mean_two)
    return (grad_in, jnp.sum(grad_out * scaled, axis=0), jnp.sum(grad_out, axis=0))


def masked_scores(queries, key_rows, length):
    score_scale = HEAD ** (-0.5)
    scores = (
        jnp.einsum("qhe,khe->hqk", queries, key_rows, preferred_element_type=jnp.float32)
        * score_scale
    )
    key_valid = (jnp.arange(SEQ) < length)[None, None, :]
    return jnp.where(key_valid, scores, NEG_FILL)


def attend_forward(element):
    queries, key_rows, value_rows, length = element
    scores = masked_scores(queries, key_rows, length)
    peak_score = jnp.max(scores, axis=-1, keepdims=True)
    shifted_exp = jnp.exp(scores - peak_score)
    denominator = jnp.sum(shifted_exp, axis=-1, keepdims=True)
    probability = (shifted_exp / denominator).astype(jnp.bfloat16)
    context = jnp.einsum(
        "hqk,khe->qhe", probability, value_rows, preferred_element_type=jnp.float32
    )
    return (context.astype(jnp.bfloat16), (peak_score + jnp.log(denominator))[..., 0])


def attend_backward(element):
    queries, key_rows, value_rows, length, log_total, grad_context = element
    score_scale = HEAD ** (-0.5)
    scores = masked_scores(queries, key_rows, length)
    probability = jnp.exp(scores - log_total[..., None])
    grad_prob = jnp.einsum(
        "qhe,khe->hqk", grad_context, value_rows, preferred_element_type=jnp.float32
    )
    grad_value = jnp.einsum(
        "hqk,qhe->khe",
        probability.astype(jnp.bfloat16),
        grad_context,
        preferred_element_type=jnp.float32,
    )
    grad_scores = probability * (
        grad_prob - jnp.sum(probability * grad_prob, axis=-1, keepdims=True)
    )
    grad_scores = grad_scores.astype(jnp.bfloat16)
    grad_query = (
        jnp.einsum("hqk,khe->qhe", grad_scores, key_rows, preferred_element_type=jnp.float32)
        * score_scale
    )
    grad_key = (
        jnp.einsum("hqk,qhe->khe", grad_scores, queries, preferred_element_type=jnp.float32)
        * score_scale
    )
    return jnp.stack([grad_query, grad_key, grad_value], axis=1).astype(jnp.bfloat16)


def row_mask(lengths, rows_dev):
    places = lax.axis_index("tensor") * rows_dev + jnp.arange(rows_dev)
    sequence_of = places // SEQ
    offset = places % SEQ
    matches = sequence_of[:, None] == jnp.arange(lengths.shape[0])[None, :]
    limit_rows = jnp.sum(jnp.where(matches, lengths[None, :], 0), axis=1)
    return (offset < limit_rows).astype(jnp.float32)[:, None]


def forward_pass(inputs, lengths, weights):
    (
        w_qkv,
        b_qv,
        w_out,
        b_out,
        gain_one,
        shift_one,
        w_in,
        b_in,
        w_down,
        b_down,
        gain_two,
        shift_two,
    ) = weights
    width_dev = w_qkv.shape[2]
    gathered = lax.all_gather(inputs, "tensor", axis=0, tiled=True)
    bias_three = jnp.stack([b_qv[0], jnp.zeros_like(b_qv[0]), b_qv[1]]).astype(jnp.float32)
    projected = (
        jnp.einsum("td,dcf->tcf", gathered, w_qkv, preferred_element_type=jnp.float32) + bias_three
    ).astype(jnp.bfloat16)
    shaped = projected.reshape(SEQ_DEV, SEQ, 3, width_dev // HEAD, HEAD)
    context, log_total = lax.map(
        attend_forward, (shaped[:, :, 0], shaped[:, :, 1], shaped[:, :, 2], lengths)
    )
    context = context.reshape(SEQ_DEV * SEQ, width_dev)
    segment = context
    branch = lax.psum_scatter(
        jnp.dot(segment, w_out, preferred_element_type=jnp.float32).astype(jnp.bfloat16),
        "tensor",
        scatter_dimension=0,
        tiled=True,
    ).astype(jnp.float32) + b_out.astype(jnp.float32)
    normed, scaled_one, inverse_one = norm_forward(
        inputs.astype(jnp.float32) + branch,
        gain_one.astype(jnp.float32),
        shift_one.astype(jnp.float32),
    )
    normed_all = lax.all_gather(normed.astype(jnp.bfloat16), "tensor", axis=0, tiled=True)
    hidden = jnp.dot(normed_all, w_in, preferred_element_type=jnp.float32) + b_in.astype(
        jnp.float32
    )
    active = gelu_exact(hidden).astype(jnp.bfloat16)
    segment = active
    second = lax.psum_scatter(
        jnp.dot(segment, w_down, preferred_element_type=jnp.float32).astype(jnp.bfloat16),
        "tensor",
        scatter_dimension=0,
        tiled=True,
    ).astype(jnp.float32) + b_down.astype(jnp.float32)
    output, scaled_two, inverse_two = norm_forward(
        normed + second, gain_two.astype(jnp.float32), shift_two.astype(jnp.float32)
    )
    return (
        gathered,
        projected,
        context,
        log_total,
        scaled_one,
        inverse_one,
        normed_all,
        hidden,
        active,
        scaled_two,
        inverse_two,
        output,
    )


def general(
    inputs,
    lengths,
    w_qkv,
    b_qv,
    w_out,
    b_out,
    gain_one,
    shift_one,
    w_in,
    b_in,
    w_down,
    b_down,
    gain_two,
    shift_two,
    cotangent,
):
    weights = (
        w_qkv,
        b_qv,
        w_out,
        b_out,
        gain_one,
        shift_one,
        w_in,
        b_in,
        w_down,
        b_down,
        gain_two,
        shift_two,
    )
    first_pass = forward_pass(inputs, lengths, weights)
    output = first_pass[11].astype(jnp.bfloat16)
    recorded = forward_pass(inputs, lengths, weights)
    (
        gathered,
        projected,
        context,
        log_total,
        scaled_one,
        inverse_one,
        normed_all,
        hidden,
        active,
        scaled_two,
        inverse_two,
        _,
    ) = recorded
    rows_dev = inputs.shape[0]
    width_dev = w_qkv.shape[2]
    grad_out = cotangent.astype(jnp.float32) * row_mask(lengths, rows_dev)
    grad_two, grad_gain_two, grad_shift_two = norm_backward(
        grad_out, scaled_two, inverse_two, gain_two.astype(jnp.float32)
    )
    grad_second = grad_two.astype(jnp.bfloat16)
    grad_b_down = jnp.sum(grad_second.astype(jnp.float32), axis=0)
    second_all = lax.all_gather(grad_second, "tensor", axis=0, tiled=True)
    grad_w_down = jnp.einsum("tf,td->fd", active, second_all, preferred_element_type=jnp.float32)
    grad_active = jnp.einsum("td,fd->tf", second_all, w_down, preferred_element_type=jnp.float32)
    _, gelu_pull = jax.vjp(gelu_exact, hidden)
    grad_hidden = gelu_pull(grad_active)[0].astype(jnp.bfloat16)
    grad_b_in = jnp.sum(grad_hidden.astype(jnp.float32), axis=0)
    grad_w_in = jnp.einsum("td,tf->df", normed_all, grad_hidden, preferred_element_type=jnp.float32)
    segment = grad_hidden
    grad_normed = grad_two + lax.psum_scatter(
        jnp.einsum("tf,df->td", segment, w_in, preferred_element_type=jnp.float32).astype(
            jnp.bfloat16
        ),
        "tensor",
        scatter_dimension=0,
        tiled=True,
    ).astype(jnp.float32)
    grad_first, grad_gain_one, grad_shift_one = norm_backward(
        grad_normed, scaled_one, inverse_one, gain_one.astype(jnp.float32)
    )
    grad_branch = grad_first.astype(jnp.bfloat16)
    grad_b_out = jnp.sum(grad_branch.astype(jnp.float32), axis=0)
    branch_all = lax.all_gather(grad_branch, "tensor", axis=0, tiled=True)
    grad_w_out = jnp.einsum("tf,td->fd", context, branch_all, preferred_element_type=jnp.float32)
    grad_context = jnp.einsum(
        "td,fd->tf", branch_all, w_out, preferred_element_type=jnp.float32
    ).astype(jnp.bfloat16)
    heads_dev = width_dev // HEAD
    shaped = projected.reshape(SEQ_DEV, SEQ, 3, heads_dev, HEAD)
    grad_shaped = grad_context.reshape(SEQ_DEV, SEQ, heads_dev, HEAD)
    grad_proj = lax.map(
        attend_backward,
        (shaped[:, :, 0], shaped[:, :, 1], shaped[:, :, 2], lengths, log_total, grad_shaped),
    )
    grad_proj = grad_proj.reshape(SEQ_DEV * SEQ, 3, width_dev)
    grad_w_qkv = jnp.einsum("td,tcf->dcf", gathered, grad_proj, preferred_element_type=jnp.float32)
    grad_b_qv = jnp.sum(grad_proj[:, 0::2].astype(jnp.float32), axis=0)
    segment = grad_proj
    grad_inputs = (
        grad_first
        + lax.psum_scatter(
            jnp.einsum("tcf,dcf->td", segment, w_qkv, preferred_element_type=jnp.float32).astype(
                jnp.bfloat16
            ),
            "tensor",
            scatter_dimension=0,
            tiled=True,
        ).astype(jnp.float32)
    ).astype(jnp.bfloat16)
    small_terms = jnp.stack(
        [grad_gain_one, grad_shift_one, grad_b_out, grad_gain_two, grad_shift_two, grad_b_down]
    )
    grad_w_qkv, grad_b_qv, grad_w_out, grad_w_in, grad_b_in, grad_w_down, small_terms = (
        lax.psum(grad_w_qkv.astype(jnp.bfloat16), "dp").astype(jnp.float32),
        lax.psum(grad_b_qv.astype(jnp.bfloat16), "dp").astype(jnp.float32),
        lax.psum(grad_w_out.astype(jnp.bfloat16), "dp").astype(jnp.float32),
        lax.psum(grad_w_in.astype(jnp.bfloat16), "dp").astype(jnp.float32),
        lax.psum(grad_b_in.astype(jnp.bfloat16), "dp").astype(jnp.float32),
        lax.psum(grad_w_down.astype(jnp.bfloat16), "dp").astype(jnp.float32),
        lax.psum(small_terms.astype(jnp.bfloat16), "dp").astype(jnp.float32),
    )
    small_sums = lax.psum(small_terms, "tensor")
    return (
        output,
        grad_inputs,
        grad_w_qkv,
        grad_b_qv,
        grad_w_out,
        small_sums[2],
        small_sums[0],
        small_sums[1],
        grad_w_in,
        grad_b_in,
        grad_w_down,
        small_sums[5],
        small_sums[3],
        small_sums[4],
    )


def place():
    dp = lax.axis_index("dp")
    return dp // (2 * N_X), (dp // 2) % N_X, dp % 2, lax.axis_index("tensor")


def at(z, x, c, y):
    return ((z * N_X + x) * 2 + c, y)


def greet(peers):
    barrier = pltpu.get_barrier_semaphore()
    for peer in peers:
        pl.semaphore_signal(barrier, inc=1, device_id=peer, device_id_type=MESH)
    pl.semaphore_wait(barrier, len(peers))


def copy_to(src, dst, send_sem, recv_sem, peer):
    return pltpu.make_async_remote_copy(
        src_ref=src, dst_ref=dst, send_sem=send_sem, recv_sem=recv_sem,
        device_id=peer, device_id_type=MESH,
    )


CHUNKS = 24
RING = 4
BF, F32 = jnp.bfloat16, jnp.float32
ROWS_AT_ONCE = 32


def dot(a, b, ca, cb):
    return lax.dot_general(a, b, (((ca,), (cb,)), ((), ())), preferred_element_type=F32)


def span(index, size):
    return pl.ds(pl.multiple_of(index * size, size), size)


def layer_kernel(
    lengths, x_hbm, cot_hbm, wq_own, wo_own, wi_own, wd_own, vec, bias_own,
    out_hbm, gin_hbm, tiles_hbm, small_out, wq_oth, wo_oth, wi_oth, wd_oth, e_hbm,
    xv, nlow, gsec, gctx, ctx, qkv, inv, xhat, rs1, acc, u1, u2, own, oth, r1, ry, rx, rz,
    ring_a, ring_b, bias_oth, small, s0, s1, s2, s3, s4,
    load_sem, a_sem, b_sem, e_sem, o_sem, t_sem, g_send, g_recv, send, recv, small_send, small_recv,
):
    z, x, c, y = place()
    zb = z % 2
    z_of = [(z + d) % N_Z for d in (1, 2, 3)]
    to_c, to_y, to_x = at(z, x, 1 - c, y), at(z, x, c, 1 - y), at(z, 1 - x, c, y)
    to_z = [at(v, x, c, y) for v in z_of]
    to_zp, to_zq = at(z + 1 - 2 * zb, x, c, y), at((z + 2) % N_Z, x, c, y)
    seq, width = xv.shape
    half_w = width // 2

    load_x = pltpu.make_async_copy(x_hbm, xv, load_sem.at[0])
    load_cot = pltpu.make_async_copy(cot_hbm, gsec, load_sem.at[1])
    load_x.start()
    load_cot.start()

    def fetch_qkv(h, i):
        source = (wq_own, wq_oth)[h]
        return pltpu.make_async_copy(source.at[i], ring_b.at[i], b_sem.at[i])

    def fetch_out(h):
        return pltpu.make_async_copy((wo_own, wo_oth)[h], ring_a.at[h], a_sem.at[h])

    def fetch_in(h, f, slot):
        return pltpu.make_async_copy((wi_own, wi_oth)[h].at[:, span(f, TILE)], ring_b.at[slot], b_sem.at[slot])

    def fetch_down(h, f, slot):
        return pltpu.make_async_copy((wd_own, wd_oth)[h].at[span(f, TILE)], ring_a.at[slot], a_sem.at[slot])

    for i in range(3):
        fetch_qkv(0, i).start()
    fetch_out(0).start()

    greet([to_c, to_y, to_x] + to_z)

    cut = wi_own.shape[1] // 2
    deep = wd_own.shape[0] // 2
    arrays = [(wq_own.at[i], wq_oth.at[i]) for i in range(3)] + [(wo_own, wo_oth)]
    for j in range(2):
        arrays.append((wi_own.at[:, j * cut : (j + 1) * cut], wi_oth.at[:, j * cut : (j + 1) * cut]))
        arrays.append((wd_own.at[j * deep : (j + 1) * deep], wd_oth.at[j * deep : (j + 1) * deep]))
    count = len(arrays)

    def gather_message(n, kind):
        size = arrays[n][0].shape[0] // 16
        pair_a, pair_b = (0, 2 * zb, 2), (1, 2 * x, 2)
        one_a, one_b = (0, 2 * zb + x, 1), (1, 2 * x + zb, 1)
        far_a, far_b = (0, 2 * (1 - zb), 2), (1, 2 * (1 - x), 2)
        (group, first, parts), peer = [
            (one_a, to_y), (one_b, to_y), (one_a, to_x), (one_b, to_zp),
            (pair_a, to_zp), (pair_b, to_x), (pair_a, to_c), (pair_b, to_c), (far_a, to_c), (far_b, to_c),
        ][kind]
        rows = pl.ds(pl.multiple_of(c * 8 * size + group * 4 * size + first * size, 16), parts * size)
        source = arrays[n][0 if kind < 2 else 1]
        return copy_to(source.at[rows], arrays[n][1].at[rows], g_send.at[n, kind], g_recv.at[n, kind], peer)

    def gather_stage(n, step):
        if step == 0:
            gather_message(n, 0).wait_recv()
            gather_message(n, 2).start()
            gather_message(n, 1).wait_recv()
            gather_message(n, 3).start()
        if step == 1:
            gather_message(n, 2).wait_recv()
            gather_message(n, 4).start()
            gather_message(n, 6).start()
            gather_message(n, 3).wait_recv()
            gather_message(n, 5).start()
            gather_message(n, 7).start()
        if step == 2:
            gather_message(n, 4).wait_recv()
            gather_message(n, 8).start()
            gather_message(n, 5).wait_recv()
            gather_message(n, 9).start()
        if step == 3:
            for kind in (6, 7, 8, 9):
                gather_message(n, kind).wait_recv()
            for kind in range(10):
                gather_message(n, kind).wait_send()

    def progress(slot):
        for step in range(4):
            if 0 <= slot - step < count:
                gather_stage(slot - step, step)

    send_bias = copy_to(bias_own, bias_oth, g_send.at[count, 0], g_recv.at[count, 0], to_y)
    send_bias.start()
    for n in range(count):
        gather_message(n, 0).start()
        gather_message(n, 1).start()

    length = lengths[y]
    key_fill = jnp.where(lax.broadcasted_iota(jnp.int32, (1, seq), 1) < length, 0.0, NEG_FILL)
    low_lanes = lax.broadcasted_iota(jnp.int32, (1, 128), 1) < HEAD
    one, zero = jnp.ones((), BF), jnp.zeros((), BF)
    scale = HEAD ** (-0.5)
    pairs = half_w // 128

    def project(h):
        bias = (bias_own, bias_oth)[h]
        for i in range(3):
            fetch_qkv(h, i).wait()
            value = dot(xv[...], ring_b[i], 1, 0)
            if i == 0:
                qkv[h, 0] = (value + bias[0:1, :]).astype(BF) * jnp.asarray(scale, BF)
            if i == 1:
                qkv[h, 1] = value.astype(BF)
            if i == 2:
                qkv[h, 2] = (value + bias[1:2, :]).astype(BF)

    def attend(h, p, e_ref):
        lanes = span(p, 128)
        q2, k2, v2 = qkv[h, 0, :, lanes], qkv[h, 1, :, lanes], qkv[h, 2, :, lanes]
        parts = []
        for head in range(2):
            mine = low_lanes if head == 0 else jnp.logical_not(low_lanes)
            scores = dot(jnp.where(mine, q2, zero), k2, 1, 1) + key_fill
            peak = jnp.max(scores, axis=-1, keepdims=True)
            e = jnp.exp(scores - peak).astype(BF)
            e_ref[2 * p + head] = e
            parts.append(dot(e, jnp.where(mine, v2, one), 1, 0))
        total = pltpu.roll(jnp.where(low_lanes, parts[1], parts[0]), HEAD, 1)
        inverse = 1.0 / total
        inv[h, :, lanes] = inverse
        ctx[:, span(h * pairs + p, 128)] = (jnp.where(low_lanes, parts[0], parts[1]) * inverse).astype(BF)

    def attend_half(h, slots):
        def body(p, _):
            attend(h, p, (u1, u2)[h])
            for at_pair, slot in slots:
                @pl.when(p == at_pair)
                def _():
                    progress(slot)
            return 0
        lax.fori_loop(0, pairs, body, 0)

    def e_copy(h, back):
        ref, buf = e_hbm.at[pl.ds(h * 8, 8)], (u1 if back else (u1, u2)[h])
        return pltpu.make_async_copy(ref, buf, e_sem.at[h]) if back else pltpu.make_async_copy(buf, ref, e_sem.at[h])

    load_x.wait()
    project(0)
    attend_half(0, ((1, 0), (3, 1)))
    e_copy(0, False).start()
    fetch_out(0).wait()
    acc[...] = dot(ctx[:, :half_w], ring_a[0], 1, 0)
    for slot in (2, 3):
        progress(slot)
    send_bias.wait()
    fetch_qkv(1, 0).start()
    progress(4)
    fetch_qkv(1, 1).start()
    progress(5)
    fetch_qkv(1, 2).start()
    project(1)
    attend_half(1, ((2, 6),))
    e_copy(1, False).start()
    fetch_out(1).start()
    for f in range(2):
        fetch_in(0, f, f).start()
    fetch_down(0, 0, 0).start()
    fetch_out(1).wait()
    acc[...] += dot(ctx[:, half_w:], ring_a[1], 1, 0)
    progress(7)

    def blocks(body):
        def run(b, _):
            body(span(b, ROWS_AT_ONCE), b)
            return 0
        lax.fori_loop(0, seq // ROWS_AT_ONCE, run, 0)

    def mean(v):
        return jnp.sum(v, axis=-1, keepdims=True) * (1.0 / width)

    small[...] = jnp.zeros_like(small)
    b_out, gain1, shift1 = vec[0:1, :], vec[1:2, :], vec[2:3, :]
    b_down, gain2, shift2 = vec[3:4, :], vec[4:5, :], vec[5:6, :]

    def norm_one(r, b):
        v = xv[r, :].astype(F32) + (acc[r, :] + b_out)
        center = v - mean(v)
        inverse = lax.rsqrt(mean(center * center) + EPSILON)
        hat = center * inverse
        xhat[r, :] = hat
        rs1[r, :] = jnp.broadcast_to(inverse, (ROWS_AT_ONCE, 128))
        nlow[r, :] = (hat * gain1 + shift1).astype(BF)
    blocks(norm_one)
    acc[...] = jnp.zeros_like(acc)
    e_copy(0, False).wait()
    e_copy(1, False).wait()

    def hidden_half(h, slots):
        bias = (bias_own, bias_oth)[h]
        def body(f, _):
            t = h * 4 + f
            b_slot, a_slot = t % 3, t % 2
            @pl.when(f + 2 < 4)
            def _():
                fetch_in(h, f + 2, (t + 2) % 3).start()
            @pl.when(f + 1 < 4)
            def _():
                fetch_down(h, f + 1, (t + 1) % 2).start()
            fetch_in(h, f, b_slot).wait()
            hidden = dot(nlow[...], ring_b[b_slot], 1, 0) + bias[pl.ds(2 + f, 1), :]
            cdf = 0.5 + 0.5 * lax.erf(hidden * 0.7071067811865476)
            u1[t] = (hidden * cdf).astype(BF)
            u2[t] = (cdf + hidden * (jnp.exp(hidden * hidden * -0.5) * 0.3989422804014327)).astype(BF)
            fetch_down(h, f, a_slot).wait()
            acc[...] += dot(u1[t], ring_a[a_slot], 1, 0)
            for at_tile, slot in slots:
                @pl.when(f == at_tile)
                def _():
                    progress(slot)
            return 0
        lax.fori_loop(0, 4, body, 0)

    hidden_half(0, ((0, 8), (2, 9)))
    for g in range(2):
        fetch_in(1, g, (4 + g) % 3).start()
    fetch_down(1, 0, 0).start()
    hidden_half(1, ((0, 10),))

    load_cot.wait()
    valid_limit = lengths[y]

    def norm_two(r, b):
        normed = xhat[r, :] * gain1 + shift1
        v = normed + (acc[r, :] + b_down)
        center = v - mean(v)
        inverse = lax.rsqrt(mean(center * center) + EPSILON)
        hat = center * inverse
        gctx[r, :] = (hat * gain2 + shift2).astype(BF)
        position = b * ROWS_AT_ONCE + lax.broadcasted_iota(jnp.int32, (ROWS_AT_ONCE, 1), 0)
        g_out = jnp.where(position < valid_limit, gsec[r, :].astype(F32), 0.0)
        scaled = g_out * gain2
        g_two = inverse * (scaled - mean(scaled) - hat * mean(scaled * hat))
        low = g_two.astype(BF)
        acc[r, :] = g_two
        gsec[r, :] = low
        small[3:4, :] += jnp.sum(g_out * hat, axis=0, keepdims=True)
        small[4:5, :] += jnp.sum(g_out, axis=0, keepdims=True)
        small[5:6, :] += jnp.sum(low.astype(F32), axis=0, keepdims=True)
    blocks(norm_two)
    out_copy = pltpu.make_async_copy(gctx, out_hbm, o_sem.at[0])
    gin_copy = pltpu.make_async_copy(nlow, gin_hbm, o_sem.at[1])
    out_copy.start()

    half, quarter, part = TILE // 2, TILE // 4, TILE // 16
    c_rows = span(c, half)
    cn_rows = span(1 - c, half)
    x_rows = pl.ds(pl.multiple_of(c * half + x * quarter, quarter), quarter)
    xn_rows = pl.ds(pl.multiple_of(c * half + (1 - x) * quarter, quarter), quarter)

    def z_rows(v):
        return pl.ds(pl.multiple_of(c * half + x * quarter + v * part, part), part)

    def message(k, kind):
        slot = k % RING
        if kind == 0: src, dst, peer = own.at[k, cn_rows], r1.at[slot, 0], to_c
        if kind == 1: src, dst, peer = oth.at[k, cn_rows], r1.at[slot, 1], to_c
        if kind == 2: src, dst, peer = oth.at[k, c_rows], ry.at[slot], to_y
        if kind == 3: src, dst, peer = own.at[k, xn_rows], rx.at[slot], to_x
        if 4 <= kind < 7: src, dst, peer = own.at[k, z_rows(z_of[kind - 4])], rz.at[slot, kind - 4], to_z[kind - 4]
        if 7 <= kind < 10: src, dst, peer = oth.at[k, z_rows(z)], oth.at[k, z_rows(z)], to_z[kind - 7]
        if kind == 10: src, dst, peer = oth.at[k, x_rows], oth.at[k, x_rows], to_x
        if kind == 11: src, dst, peer = oth.at[k, c_rows], tiles_hbm.at[k, c_rows], to_c
        return copy_to(src, dst, send.at[slot, kind], recv.at[slot, kind], peer)

    def tile_copy(k):
        return pltpu.make_async_copy(oth.at[k, c_rows], tiles_hbm.at[k, c_rows], t_sem.at[k % RING])

    def add_into(dst, src, n):
        def body(i, _):
            r = span(i, 64)
            dst[r, :] = dst[r, :] + src[r, :]
            return 0
        lax.fori_loop(0, n // 64, body, 0)

    def wait(k, kinds):
        for kind in kinds:
            message(k, kind).wait()

    def reduce_stage(k, s):
        slot = k % RING
        if s == 0:
            message(k, 0).start()
            message(k, 1).start()
        if s == 1:
            wait(k, (0, 1))
            add_into(oth.at[k, c_rows], r1.at[slot, 1], half)
            message(k, 2).start()
            add_into(own.at[k, c_rows], r1.at[slot, 0], half)
        if s == 2:
            wait(k, (2,))
            add_into(own.at[k, c_rows], ry.at[slot], half)
            message(k, 3).start()
        if s == 3:
            wait(k, (3,))
            add_into(own.at[k, x_rows], rx.at[slot], quarter)
            for kind in (4, 5, 6):
                message(k, kind).start()
        if s == 4:
            wait(k, (4, 5, 6))
            total = own[k, z_rows(z), :].astype(F32)
            for d in range(3):
                total = total + rz[slot, d].astype(F32)
            oth[k, z_rows(z), :] = total.astype(BF)
            for kind in (7, 8, 9):
                message(k, kind).start()
        if s == 5:
            wait(k, (7, 8, 9))
            message(k, 10).start()
        if s == 6:
            wait(k, (10,))
            message(k, 11).start()
            tile_copy(k).start()
        if s == 7:
            wait(k, (11,))
            tile_copy(k).wait()

    def reduce_step(t):
        for s in range(8):
            @pl.when((t >= s) & (t - s < CHUNKS))
            def _():
                reduce_stage(t - s, s)

    def small_messages(i):
        if i == 0:
            return [copy_to(small, s0, small_send.at[0], small_recv.at[0], to_c)]
        if i == 1:
            return [
                copy_to(small.at[pl.ds(0, 8)], s1.at[pl.ds(0, 8)], small_send.at[1], small_recv.at[1], to_y),
                copy_to(small.at[pl.ds(16, 8)], s1.at[pl.ds(8, 8)], small_send.at[2], small_recv.at[2], to_y),
            ]
        got, peer = ((s2, to_x), (s3, to_zp), (s4, to_zq))[i - 2]
        return [copy_to(small.at[pl.ds(0, 16)], got, small_send.at[i + 1], small_recv.at[i + 1], peer)]

    def small_step(i):
        if i > 0:
            for m in small_messages(i - 1):
                m.wait()
            if i == 1:
                small[...] = small[...] + s0[...]
            else:
                small[0:16, :] = small[0:16, :] + (s1, s2, s3, s4)[i - 2][...]
        if i < 5:
            for m in small_messages(i):
                m.start()

    def fetch_ffn(t, start):
        for h in range(2):
            @pl.when((t >= 4 * h) & (t < 4 * h + 4))
            def _():
                b, a = fetch_in(h, t - 4 * h, t % 3), fetch_down(h, t - 4 * h, t % 2)
                if start:
                    b.start()
                    a.start()
                else:
                    b.wait()
                    a.wait()

    def down_tiles(k):
        g = gsec[:, span(k % 2, TILE)]
        own[k] = dot(u1[k // 2], g, 0, 0).astype(BF)
        oth[k] = dot(u1[4 + k // 2], g, 0, 0).astype(BF)

    def hidden_back(t):
        fetch_ffn(t, False)
        g_active = dot(gsec[...], ring_a[t % 2], 1, 1)
        g_hidden = (g_active * u2[t].astype(F32)).astype(BF)
        u2[t] = g_hidden
        total = jnp.sum(g_hidden.astype(F32), axis=0, keepdims=True)
        small[pl.ds(9 + 8 * (t // 4) + (t % 4) // 2, 1), span(t % 2, TILE)] = total
        acc[...] += dot(g_hidden, ring_b[t % 3], 1, 1)

    def in_tiles(k):
        j = k - 8
        a = nlow[:, span(j % 2, TILE)]
        own[k] = dot(a, u2[j // 2], 0, 0).astype(BF)
        oth[k] = dot(a, u2[4 + j // 2], 0, 0).astype(BF)

    def norm_one_back(r, b):
        g_normed, hat = acc[r, :], xhat[r, :]
        scaled = g_normed * gain1
        g_first = rs1[r, 0:1] * (scaled - mean(scaled) - hat * mean(scaled * hat))
        low = g_first.astype(BF)
        acc[r, :] = g_first
        gsec[r, :] = low
        small[0:1, :] += jnp.sum(g_normed * hat, axis=0, keepdims=True)
        small[1:2, :] += jnp.sum(g_normed, axis=0, keepdims=True)
        small[2:3, :] += jnp.sum(low.astype(F32), axis=0, keepdims=True)

    def attend_back(h, p):
        lanes = span(p, 128)
        wide = span(h * pairs + p, 128)
        q2, k2, v2 = qkv[h, 0, :, lanes], qkv[h, 1, :, lanes], qkv[h, 2, :, lanes]
        g = gctx[:, wide].astype(F32) * inv[h, :, lanes]
        low = g.astype(BF)
        less = pltpu.roll(-(g * ctx[:, wide].astype(F32)), HEAD, 1).astype(BF)
        g_q, g_k, g_v = [], [], []
        for head in range(2):
            mine = low_lanes if head == 0 else jnp.logical_not(low_lanes)
            e = u1[2 * p + head]
            g_scores = (dot(jnp.where(mine, low, less), jnp.where(mine, v2, one), 1, 1) * e.astype(F32)).astype(BF)
            g_q.append(dot(g_scores, k2, 1, 0))
            rows = slice(head * HEAD, head * HEAD + HEAD)
            g_k.append(dot(q2, g_scores, 0, 0)[rows])
            g_v.append(dot(low, e, 0, 0)[rows])
        qkv[h, 0, :, lanes] = (jnp.where(low_lanes, g_q[0], g_q[1]) * scale).astype(BF)
        qkv[h, 1, :, lanes] = jnp.concatenate(g_k, axis=0).T.astype(BF)
        qkv[h, 2, :, lanes] = jnp.concatenate(g_v, axis=0).T.astype(BF)

    fetch_ffn(0, True)

    def iteration(t, _):
        @pl.when(t < 8)
        def _():
            down_tiles(t)
        @pl.when((t >= 8) & (t < 16))
        def _():
            in_tiles(t)
        @pl.when((t >= 16) & (t < 18))
        def _():
            g = gsec[:, span(t - 16, TILE)]
            own[t] = dot(ctx[:, :half_w], g, 0, 0).astype(BF)
            oth[t] = dot(ctx[:, half_w:], g, 0, 0).astype(BF)
        @pl.when((t >= 18) & (t < 24))
        def _():
            j = t - 18
            a = xv[:, span(j % 2, TILE)]
            own[t] = dot(a, qkv[0, j // 2], 0, 0).astype(BF)
            oth[t] = dot(a, qkv[1, j // 2], 0, 0).astype(BF)
        reduce_step(t)
        @pl.when(t < 8)
        def _():
            @pl.when(t < 7)
            def _():
                fetch_ffn(t + 1, True)
            hidden_back(t)
        @pl.when(t == 8)
        def _():
            e_copy(0, True).start()
            fetch_out(0).start()
            fetch_out(1).start()
            blocks(norm_one_back)
        @pl.when(t == 9)
        def _():
            out_copy.wait()
            for h in range(2):
                fetch_out(h).wait()
                gctx[:, h * half_w : (h + 1) * half_w] = dot(gsec[...], ring_a[h], 1, 1).astype(BF)
            e_copy(0, True).wait()
        for first, h in ((10, 0), (13, 1)):
            @pl.when((t >= first) & (t < first + 2))
            def _():
                def body(p, _):
                    attend_back(h, 2 * (t - first) + p)
                    return 0
                lax.fori_loop(0, 2, body, 0)
            @pl.when(t == first + 1)
            def _():
                if h == 0:
                    e_copy(1, True).start()
                for i in (0, 2):
                    total = jnp.sum(qkv[h, i].astype(F32), axis=0, keepdims=True)
                    small[8 + 8 * h : 9 + 8 * h, (i // 2) * TILE : (i // 2 + 1) * TILE] = total
        @pl.when(t == 12)
        def _():
            e_copy(1, True).wait()
        for h in range(2):
            first = 15 + 2 * h
            @pl.when(t == first)
            def _():
                for i in range(3):
                    fetch_qkv(h, i).start()
            @pl.when(t == first + 1)
            def _():
                for i in range(3):
                    fetch_qkv(h, i).wait()
                    acc[...] += dot(qkv[h, i], ring_b[i], 1, 1)
        @pl.when(t == 19)
        def _():
            def last(r, b):
                nlow[r, :] = acc[r, :].astype(BF)
            blocks(last)
            gin_copy.start()
        for i in range(6):
            @pl.when(t == 16 + i)
            def _():
                small_step(i)
        return 0

    lax.fori_loop(0, CHUNKS + 7, iteration, 0)
    small_out[...] = small[0:16, :]
    gin_copy.wait()


def layer(lengths, inputs, cotangent, wq, w_out, w_in, w_down, vec, bias):
    seq, width = inputs.shape
    half = TILE // 2
    vm, dma = pltpu.VMEM, pltpu.SemaphoreType.DMA
    anywhere, inside = pl.BlockSpec(memory_space=pl.ANY), pl.BlockSpec(memory_space=pltpu.VMEM)
    like = lambda a: jax.ShapeDtypeStruct(a.shape, a.dtype)
    tile_shape = (TILE, TILE)
    return pl.pallas_call(
        layer_kernel,
        out_shape=[
            like(inputs), like(inputs), jax.ShapeDtypeStruct((CHUNKS,) + tile_shape, BF),
            jax.ShapeDtypeStruct((16, width), F32),
            like(wq), like(w_out), like(w_in), like(w_down),
            jax.ShapeDtypeStruct((16,) + tile_shape, BF),
        ],
        in_specs=[pl.BlockSpec(memory_space=pltpu.SMEM)] + [anywhere] * 6 + [inside] * 2,
        out_specs=[anywhere] * 3 + [inside] + [anywhere] * 5,
        scratch_shapes=[
            vm((seq, width), BF), vm((seq, width), BF), vm((seq, width), BF), vm((seq, width), BF), vm((seq, width), BF),
            vm((2, 3) + tile_shape, BF), vm((2,) + tile_shape, F32),
            vm((seq, width), F32), vm((seq, 128), F32), vm((seq, width), F32),
            vm((8,) + tile_shape, BF), vm((8,) + tile_shape, BF),
            vm((CHUNKS,) + tile_shape, BF), vm((CHUNKS,) + tile_shape, BF),
            vm((RING, 2, half, TILE), BF), vm((RING, half, TILE), BF),
            vm((RING, half // 2, TILE), BF), vm((RING, 3, half // 8, TILE), BF),
            vm((2, TILE, width), BF), vm((3, width, TILE), BF),
            vm(bias.shape, F32), vm((24, width), F32), vm((24, width), F32),
            vm((16, width), F32), vm((16, width), F32), vm((16, width), F32), vm((16, width), F32),
            dma((2,)), dma((2,)), dma((3,)), dma((2,)), dma((2,)), dma((RING,)),
            dma((9, 10)), dma((9, 10)), dma((RING, MESSAGES)), dma((RING, MESSAGES)), dma((6,)), dma((6,)),
        ],
        compiler_params=pltpu.CompilerParams(
            collective_id=1, has_side_effects=True, vmem_limit_bytes=VMEM_BYTES
        ),
    )(lengths, inputs, cotangent, wq, w_out, w_in, w_down, vec, bias)


def widen_kernel(tile, down, within, out, three):
    k = pl.program_id(0)
    value = tile[...].astype(F32)
    for ref, first, last in ((down, 0, 8), (within, 8, 16), (out, 16, 18), (three, 18, 24)):
        @pl.when((k >= first) & (k < last))
        def _():
            ref[...] = value


def widen(tiles, half_hidden, width, half_width):
    def within(first, last, place_of):
        def index(k):
            return place_of(jnp.clip(k, first, last - 1) - first)
        return index
    tile = (TILE, TILE)
    return pl.pallas_call(
        widen_kernel,
        grid=(CHUNKS,),
        out_shape=[
            jax.ShapeDtypeStruct((half_hidden, width), F32), jax.ShapeDtypeStruct((width, half_hidden), F32),
            jax.ShapeDtypeStruct((half_width, width), F32), jax.ShapeDtypeStruct((3, width, half_width), F32),
        ],
        in_specs=[pl.BlockSpec((None,) + tile, lambda k: (k, 0, 0))],
        out_specs=[
            pl.BlockSpec(tile, within(0, 8, lambda j: (j // 2, j % 2))),
            pl.BlockSpec(tile, within(8, 16, lambda j: (j % 2, j // 2))),
            pl.BlockSpec(tile, within(16, 18, lambda j: (0, j))),
            pl.BlockSpec((None,) + tile, within(18, 24, lambda j: (j // 2, j % 2, 0))),
        ],
    )(tiles)


def split_by_sequence(
    inputs, lengths, w_qkv, b_qv, w_out, b_out, gain_one, shift_one, w_in, b_in, w_down, b_down, gain_two, shift_two,
    cotangent,
):
    rows, width = inputs.shape
    half_width, half_hidden = w_qkv.shape[2], w_in.shape[1]
    wq = w_qkv.transpose(1, 0, 2)
    vec = jnp.stack([b_out, gain_one, shift_one, b_down, gain_two, shift_two]).astype(F32)
    bias = jnp.concatenate([b_qv, b_in.reshape(-1, half_width)], axis=0).astype(F32)
    output, grad_inputs, tiles, small = layer(lengths, inputs, cotangent, wq, w_out, w_in, w_down, vec, bias)[:4]
    g_w_down, g_w_in, g_w_out, g_w_qkv = widen(tiles, half_hidden, width, half_width)
    owned = small[8:].reshape(-1)
    return (
        output,
        grad_inputs,
        g_w_qkv.transpose(1, 0, 2),
        owned[: 2 * half_width].reshape(2, half_width),
        g_w_out,
        small[2],
        small[0],
        small[1],
        g_w_in,
        owned[2 * half_width : 2 * half_width + half_hidden],
        g_w_down,
        small[5],
        small[3],
        small[4],
    )


def solution(mesh):
    small_mesh = mesh.shape["tensor"] == 2 and mesh.shape["dp"] == 2 * N_X * N_Z
    step = split_by_sequence if small_mesh else general
    in_specs = (
        P(("dp", "tensor"), None),
        P("dp"),
        P(None, None, "tensor"),
        P(None, "tensor"),
        P("tensor", None),
        P(),
        P(),
        P(),
        P(None, "tensor"),
        P("tensor"),
        P("tensor", None),
        P(),
        P(),
        P(),
        P(("dp", "tensor"), None),
    )
    out_specs = (
        P(("dp", "tensor"), None),
        P(("dp", "tensor"), None),
        P(None, None, "tensor"),
        P(None, "tensor"),
        P("tensor", None),
        P(),
        P(),
        P(),
        P(None, "tensor"),
        P("tensor"),
        P("tensor", None),
        P(),
        P(),
        P(),
    )
    return jax.shard_map(step, mesh=mesh, in_specs=in_specs, out_specs=out_specs, check_vma=False)
```

```python
import jax
import jax.numpy as jnp
from jax import lax
from jax.experimental import pallas as pl
from jax.experimental.pallas import tpu as pltpu
from jax.sharding import PartitionSpec as P

MESH = pl.DeviceIdType.MESH
N_Z, N_X = 4, 2
TILE = 512
MESSAGES = 12
VMEM_BYTES = 63 << 20

HEAD = 64
SEQ = 512
SEQ_DEV = 2


EPSILON = 1e-12
NEG_FILL = -1000000000.0


def gelu_exact(values):
    return jax.nn.gelu(values, approximate=False)


def norm_forward(values, gain_vec, shift_vec):
    center = values - jnp.mean(values, axis=-1, keepdims=True)
    spread = jnp.mean(center * center, axis=-1, keepdims=True)
    inverse = lax.rsqrt(spread + EPSILON)
    scaled = center * inverse
    return (scaled * gain_vec + shift_vec, scaled, inverse)


def norm_backward(grad_out, scaled, inverse, gain_vec):
    grad_scaled = grad_out * gain_vec
    mean_one = jnp.mean(grad_scaled, axis=-1, keepdims=True)
    mean_two = jnp.mean(grad_scaled * scaled, axis=-1, keepdims=True)
    grad_in = inverse * (grad_scaled - mean_one - scaled * mean_two)
    return (grad_in, jnp.sum(grad_out * scaled, axis=0), jnp.sum(grad_out, axis=0))


def masked_scores(queries, key_rows, length):
    score_scale = HEAD ** (-0.5)
    scores = (
        jnp.einsum("qhe,khe->hqk", queries, key_rows, preferred_element_type=jnp.float32)
        * score_scale
    )
    key_valid = (jnp.arange(SEQ) < length)[None, None, :]
    return jnp.where(key_valid, scores, NEG_FILL)


def attend_forward(element):
    queries, key_rows, value_rows, length = element
    scores = masked_scores(queries, key_rows, length)
    peak_score = jnp.max(scores, axis=-1, keepdims=True)
    shifted_exp = jnp.exp(scores - peak_score)
    denominator = jnp.sum(shifted_exp, axis=-1, keepdims=True)
    probability = (shifted_exp / denominator).astype(jnp.bfloat16)
    context = jnp.einsum(
        "hqk,khe->qhe", probability, value_rows, preferred_element_type=jnp.float32
    )
    return (context.astype(jnp.bfloat16), (peak_score + jnp.log(denominator))[..., 0])


def attend_backward(element):
    queries, key_rows, value_rows, length, log_total, grad_context = element
    score_scale = HEAD ** (-0.5)
    scores = masked_scores(queries, key_rows, length)
    probability = jnp.exp(scores - log_total[..., None])
    grad_prob = jnp.einsum(
        "qhe,khe->hqk", grad_context, value_rows, preferred_element_type=jnp.float32
    )
    grad_value = jnp.einsum(
        "hqk,qhe->khe",
        probability.astype(jnp.bfloat16),
        grad_context,
        preferred_element_type=jnp.float32,
    )
    grad_scores = probability * (
        grad_prob - jnp.sum(probability * grad_prob, axis=-1, keepdims=True)
    )
    grad_scores = grad_scores.astype(jnp.bfloat16)
    grad_query = (
        jnp.einsum("hqk,khe->qhe", grad_scores, key_rows, preferred_element_type=jnp.float32)
        * score_scale
    )
    grad_key = (
        jnp.einsum("hqk,qhe->khe", grad_scores, queries, preferred_element_type=jnp.float32)
        * score_scale
    )
    return jnp.stack([grad_query, grad_key, grad_value], axis=1).astype(jnp.bfloat16)


def row_mask(lengths, rows_dev):
    places = lax.axis_index("tensor") * rows_dev + jnp.arange(rows_dev)
    sequence_of = places // SEQ
    offset = places % SEQ
    matches = sequence_of[:, None] == jnp.arange(lengths.shape[0])[None, :]
    limit_rows = jnp.sum(jnp.where(matches, lengths[None, :], 0), axis=1)
    return (offset < limit_rows).astype(jnp.float32)[:, None]


def forward_pass(inputs, lengths, weights):
    (
        w_qkv,
        b_qv,
        w_out,
        b_out,
        gain_one,
        shift_one,
        w_in,
        b_in,
        w_down,
        b_down,
        gain_two,
        shift_two,
    ) = weights
    width_dev = w_qkv.shape[2]
    gathered = lax.all_gather(inputs, "tensor", axis=0, tiled=True)
    bias_three = jnp.stack([b_qv[0], jnp.zeros_like(b_qv[0]), b_qv[1]]).astype(jnp.float32)
    projected = (
        jnp.einsum("td,dcf->tcf", gathered, w_qkv, preferred_element_type=jnp.float32) + bias_three
    ).astype(jnp.bfloat16)
    shaped = projected.reshape(SEQ_DEV, SEQ, 3, width_dev // HEAD, HEAD)
    context, log_total = lax.map(
        attend_forward, (shaped[:, :, 0], shaped[:, :, 1], shaped[:, :, 2], lengths)
    )
    context = context.reshape(SEQ_DEV * SEQ, width_dev)
    segment = context
    branch = lax.psum_scatter(
        jnp.dot(segment, w_out, preferred_element_type=jnp.float32).astype(jnp.bfloat16),
        "tensor",
        scatter_dimension=0,
        tiled=True,
    ).astype(jnp.float32) + b_out.astype(jnp.float32)
    normed, scaled_one, inverse_one = norm_forward(
        inputs.astype(jnp.float32) + branch,
        gain_one.astype(jnp.float32),
        shift_one.astype(jnp.float32),
    )
    normed_all = lax.all_gather(normed.astype(jnp.bfloat16), "tensor", axis=0, tiled=True)
    hidden = jnp.dot(normed_all, w_in, preferred_element_type=jnp.float32) + b_in.astype(
        jnp.float32
    )
    active = gelu_exact(hidden).astype(jnp.bfloat16)
    segment = active
    second = lax.psum_scatter(
        jnp.dot(segment, w_down, preferred_element_type=jnp.float32).astype(jnp.bfloat16),
        "tensor",
        scatter_dimension=0,
        tiled=True,
    ).astype(jnp.float32) + b_down.astype(jnp.float32)
    output, scaled_two, inverse_two = norm_forward(
        normed + second, gain_two.astype(jnp.float32), shift_two.astype(jnp.float32)
    )
    return (
        gathered,
        projected,
        context,
        log_total,
        scaled_one,
        inverse_one,
        normed_all,
        hidden,
        active,
        scaled_two,
        inverse_two,
        output,
    )


def general(
    inputs,
    lengths,
    w_qkv,
    b_qv,
    w_out,
    b_out,
    gain_one,
    shift_one,
    w_in,
    b_in,
    w_down,
    b_down,
    gain_two,
    shift_two,
    cotangent,
):
    weights = (
        w_qkv,
        b_qv,
        w_out,
        b_out,
        gain_one,
        shift_one,
        w_in,
        b_in,
        w_down,
        b_down,
        gain_two,
        shift_two,
    )
    first_pass = forward_pass(inputs, lengths, weights)
    output = first_pass[11].astype(jnp.bfloat16)
    recorded = forward_pass(inputs, lengths, weights)
    (
        gathered,
        projected,
        context,
        log_total,
        scaled_one,
        inverse_one,
        normed_all,
        hidden,
        active,
        scaled_two,
        inverse_two,
        _,
    ) = recorded
    rows_dev = inputs.shape[0]
    width_dev = w_qkv.shape[2]
    grad_out = cotangent.astype(jnp.float32) * row_mask(lengths, rows_dev)
    grad_two, grad_gain_two, grad_shift_two = norm_backward(
        grad_out, scaled_two, inverse_two, gain_two.astype(jnp.float32)
    )
    grad_second = grad_two.astype(jnp.bfloat16)
    grad_b_down = jnp.sum(grad_second.astype(jnp.float32), axis=0)
    second_all = lax.all_gather(grad_second, "tensor", axis=0, tiled=True)
    grad_w_down = jnp.einsum("tf,td->fd", active, second_all, preferred_element_type=jnp.float32)
    grad_active = jnp.einsum("td,fd->tf", second_all, w_down, preferred_element_type=jnp.float32)
    _, gelu_pull = jax.vjp(gelu_exact, hidden)
    grad_hidden = gelu_pull(grad_active)[0].astype(jnp.bfloat16)
    grad_b_in = jnp.sum(grad_hidden.astype(jnp.float32), axis=0)
    grad_w_in = jnp.einsum("td,tf->df", normed_all, grad_hidden, preferred_element_type=jnp.float32)
    segment = grad_hidden
    grad_normed = grad_two + lax.psum_scatter(
        jnp.einsum("tf,df->td", segment, w_in, preferred_element_type=jnp.float32).astype(
            jnp.bfloat16
        ),
        "tensor",
        scatter_dimension=0,
        tiled=True,
    ).astype(jnp.float32)
    grad_first, grad_gain_one, grad_shift_one = norm_backward(
        grad_normed, scaled_one, inverse_one, gain_one.astype(jnp.float32)
    )
    grad_branch = grad_first.astype(jnp.bfloat16)
    grad_b_out = jnp.sum(grad_branch.astype(jnp.float32), axis=0)
    branch_all = lax.all_gather(grad_branch, "tensor", axis=0, tiled=True)
    grad_w_out = jnp.einsum("tf,td->fd", context, branch_all, preferred_element_type=jnp.float32)
    grad_context = jnp.einsum(
        "td,fd->tf", branch_all, w_out, preferred_element_type=jnp.float32
    ).astype(jnp.bfloat16)
    heads_dev = width_dev // HEAD
    shaped = projected.reshape(SEQ_DEV, SEQ, 3, heads_dev, HEAD)
    grad_shaped = grad_context.reshape(SEQ_DEV, SEQ, heads_dev, HEAD)
    grad_proj = lax.map(
        attend_backward,
        (shaped[:, :, 0], shaped[:, :, 1], shaped[:, :, 2], lengths, log_total, grad_shaped),
    )
    grad_proj = grad_proj.reshape(SEQ_DEV * SEQ, 3, width_dev)
    grad_w_qkv = jnp.einsum("td,tcf->dcf", gathered, grad_proj, preferred_element_type=jnp.float32)
    grad_b_qv = jnp.sum(grad_proj[:, 0::2].astype(jnp.float32), axis=0)
    segment = grad_proj
    grad_inputs = (
        grad_first
        + lax.psum_scatter(
            jnp.einsum("tcf,dcf->td", segment, w_qkv, preferred_element_type=jnp.float32).astype(
                jnp.bfloat16
            ),
            "tensor",
            scatter_dimension=0,
            tiled=True,
        ).astype(jnp.float32)
    ).astype(jnp.bfloat16)
    small_terms = jnp.stack(
        [grad_gain_one, grad_shift_one, grad_b_out, grad_gain_two, grad_shift_two, grad_b_down]
    )
    grad_w_qkv, grad_b_qv, grad_w_out, grad_w_in, grad_b_in, grad_w_down, small_terms = (
        lax.psum(grad_w_qkv.astype(jnp.bfloat16), "dp").astype(jnp.float32),
        lax.psum(grad_b_qv.astype(jnp.bfloat16), "dp").astype(jnp.float32),
        lax.psum(grad_w_out.astype(jnp.bfloat16), "dp").astype(jnp.float32),
        lax.psum(grad_w_in.astype(jnp.bfloat16), "dp").astype(jnp.float32),
        lax.psum(grad_b_in.astype(jnp.bfloat16), "dp").astype(jnp.float32),
        lax.psum(grad_w_down.astype(jnp.bfloat16), "dp").astype(jnp.float32),
        lax.psum(small_terms.astype(jnp.bfloat16), "dp").astype(jnp.float32),
    )
    small_sums = lax.psum(small_terms, "tensor")
    return (
        output,
        grad_inputs,
        grad_w_qkv,
        grad_b_qv,
        grad_w_out,
        small_sums[2],
        small_sums[0],
        small_sums[1],
        grad_w_in,
        grad_b_in,
        grad_w_down,
        small_sums[5],
        small_sums[3],
        small_sums[4],
    )


def place():
    dp = lax.axis_index("dp")
    return dp // (2 * N_X), (dp // 2) % N_X, dp % 2, lax.axis_index("tensor")


def at(z, x, c, y):
    return ((z * N_X + x) * 2 + c, y)


def greet(peers):
    barrier = pltpu.get_barrier_semaphore()
    for peer in peers:
        pl.semaphore_signal(barrier, inc=1, device_id=peer, device_id_type=MESH)
    pl.semaphore_wait(barrier, len(peers))


def copy_to(src, dst, send_sem, recv_sem, peer):
    return pltpu.make_async_remote_copy(
        src_ref=src, dst_ref=dst, send_sem=send_sem, recv_sem=recv_sem,
        device_id=peer, device_id_type=MESH,
    )


CHUNKS = 24
RING = 4
BF, F32 = jnp.bfloat16, jnp.float32
ROWS_AT_ONCE = 64


def dot(a, b, ca, cb):
    return lax.dot_general(a, b, (((ca,), (cb,)), ((), ())), preferred_element_type=F32)


def span(index, size):
    return pl.ds(pl.multiple_of(index * size, size), size)


def tile_place(k):
    if k < 8:
        return 0, (slice(k // 2 * TILE, (k // 2 + 1) * TILE), slice(k % 2 * TILE, (k % 2 + 1) * TILE))
    if k < 16:
        k -= 8
        return 1, (slice(k % 2 * TILE, (k % 2 + 1) * TILE), slice(k // 2 * TILE, (k // 2 + 1) * TILE))
    if k < 18:
        k -= 16
        return 2, (slice(0, TILE), slice(k * TILE, (k + 1) * TILE))
    k -= 18
    return 3, (k // 2, slice(k % 2 * TILE, (k % 2 + 1) * TILE), slice(0, TILE))


def layer_kernel(
    lengths, x_hbm, cot_hbm, wq_own, wo_own, wi_own, wd_own, in1, in2, in3, in4, in5, in6, in_qv, in_hidden,
    out_hbm, gin_hbm, tiles_hbm, small_out, wq_oth, wo_oth, wi_oth, wd_oth, e_hbm,
    xv, nlow, gsec, gctx, ctx, qkv, inv, xhat, rs1, acc, u1, u2, own, oth, r1, ry, rx, rz,
    ring_a, ring_b, vec, bias_own, bias_oth, small, s0, s1, s2, s3, s4,
    load_sem, w_sem, a_sem, b_sem, e_sem, o_sem, t_sem, g_send, g_recv, send, recv, small_send, small_recv,
):
    z, x, c, y = place()
    zb = z % 2
    z_of = [(z + d) % N_Z for d in (1, 2, 3)]
    to_c, to_y, to_x = at(z, x, 1 - c, y), at(z, x, c, 1 - y), at(z, 1 - x, c, y)
    to_z = [at(v, x, c, y) for v in z_of]
    to_zp, to_zq = at(z + 1 - 2 * zb, x, c, y), at((z + 2) % N_Z, x, c, y)
    seq, width = xv.shape
    half_w = width // 2

    load_x = pltpu.make_async_copy(x_hbm, xv, load_sem.at[0])
    load_cot = pltpu.make_async_copy(cot_hbm, gsec, load_sem.at[1])
    load_x.start()
    load_cot.start()
    for row, ref in enumerate((in1, in2, in3, in4, in5, in6)):
        vec[row : row + 1, :] = ref[...].astype(F32).reshape(1, width)
    bias_own[0:2, :] = in_qv[...].astype(F32)
    bias_own[2:6, :] = in_hidden[...].astype(F32).reshape(4, TILE)

    def fetch_qkv(h, i):
        source = (wq_own, wq_oth)[h]
        return pltpu.make_async_copy(source.at[i], ring_b.at[i], b_sem.at[i])

    def fetch_out(h):
        return pltpu.make_async_copy((wo_own, wo_oth)[h], ring_a.at[h], a_sem.at[h])

    def fetch_in(h, f, slot):
        return pltpu.make_async_copy((wi_own, wi_oth)[h].at[:, span(f, TILE)], ring_b.at[slot], b_sem.at[slot])

    def fetch_down(h, f, slot):
        return pltpu.make_async_copy((wd_own, wd_oth)[h].at[span(f, TILE)], ring_a.at[slot], a_sem.at[slot])

    def weight_load(h, k):
        which, where = tile_place(k)
        source = ((wd_own, wi_own, wo_own, wq_own), (wd_oth, wi_oth, wo_oth, wq_oth))[h][which]
        return pltpu.make_async_copy(source.at[where], (own, oth)[h].at[k], w_sem.at[h, k])

    for k in (*range(18, 24), *range(8, 16), *range(0, 8), 16, 17):
        weight_load(0, k).start()

    greet([to_c, to_y, to_x] + to_z)

    cut = wi_own.shape[1] // 2
    deep = wd_own.shape[0] // 2
    arrays = [(wq_own.at[i], wq_oth.at[i]) for i in range(3)] + [(wo_own, wo_oth)]
    arrays += [(wi_own.at[:, j * cut : (j + 1) * cut], wi_oth.at[:, j * cut : (j + 1) * cut]) for j in range(2)]
    arrays += [(wd_own.at[j * deep : (j + 1) * deep], wd_oth.at[j * deep : (j + 1) * deep]) for j in range(2)]
    loads_of = [(18, 19), (20, 21), (22, 23), (16, 17), (8, 9, 10, 11), (12, 13, 14, 15), (0, 1, 2, 3), (4, 5, 6, 7)]
    count = len(arrays)

    def gather_message(n, kind):
        size = arrays[n][0].shape[0] // 2
        size_part = size // 8 - (8 if n >= 4 else 0)
        near_a, near_b = 2 * zb, 4 + 2 * x
        far_a, far_b = 2 * (1 - zb), 4 + 2 * (1 - x)
        one_a, one_b = 2 * zb + x, 4 + 2 * x + zb
        first, parts, peer = [
            (one_a, 1, to_y), (one_b, 1, to_y), (one_a, 1, to_x), (one_b, 1, to_zp),
            (near_a, 2, to_zp), (near_b, 2, to_x), (near_a, 2, to_c), (near_b, 2, to_c), (far_a, 2, to_c), (far_b, 2, to_c),
            (8, 0, to_y), (8, 0, to_c),
        ][kind]
        length_rows = parts * size_part if parts else size - 8 * size_part
        rows = pl.ds(pl.multiple_of(c * size + first * size_part, 8), length_rows)
        source = arrays[n][0 if kind in (0, 1, 10) else 1]
        return copy_to(source.at[rows], arrays[n][1].at[rows], g_send.at[n, kind], g_recv.at[n, kind], peer)

    def gather_stage(n, step):
        if step == 0:
            gather_message(n, 0).wait_recv()
            gather_message(n, 2).start()
            gather_message(n, 1).wait_recv()
            gather_message(n, 3).start()
        if step == 1:
            gather_message(n, 2).wait_recv()
            gather_message(n, 4).start()
            gather_message(n, 6).start()
            gather_message(n, 3).wait_recv()
            gather_message(n, 5).start()
            gather_message(n, 7).start()
        if step == 2:
            gather_message(n, 4).wait_recv()
            gather_message(n, 8).start()
            gather_message(n, 5).wait_recv()
            gather_message(n, 9).start()
            if n >= 4:
                gather_message(n, 10).wait_recv()
                gather_message(n, 11).start()
        if step == 3:
            kinds = range(12 if n >= 4 else 10)
            for kind in kinds:
                if kind >= 6 and kind != 10:
                    gather_message(n, kind).wait_recv()
            for k in loads_of[n]:
                weight_load(1, k).start()
            for kind in kinds:
                gather_message(n, kind).wait_send()

    def progress(slot):
        for step in range(4):
            if 0 <= slot - step < count:
                gather_stage(slot - step, step)

    send_bias = copy_to(bias_own, bias_oth, g_send.at[count, 0], g_recv.at[count, 0], to_y)
    send_bias.start()
    for n in (0, 1, 2, 3, 4, 5, -4, 6, -5, 7, -6, -7):
        for kind in (0, 1) if n >= 0 else (10,):
            gather_message(abs(n), kind).start()

    length = lengths[y]
    key_fill = jnp.where(lax.broadcasted_iota(jnp.int32, (1, seq), 1) < length, 0.0, NEG_FILL)
    low_lanes = lax.broadcasted_iota(jnp.int32, (1, 128), 1) < HEAD
    one, zero = jnp.ones((), BF), jnp.zeros((), BF)
    scale = HEAD ** (-0.5)
    pairs = half_w // 128

    def project(h):
        bias = (bias_own, bias_oth)[h]
        for i in range(3):
            for k in (18 + 2 * i, 19 + 2 * i):
                weight_load(h, k).wait()
            value = dot(xv[...], (own, oth)[h][18 + 2 * i : 20 + 2 * i].reshape(width, TILE), 1, 0)
            if i == 0:
                qkv[h, 0] = (value + bias[0:1, :]).astype(BF) * jnp.asarray(scale, BF)
            if i == 1:
                qkv[h, 1] = value.astype(BF)
            if i == 2:
                qkv[h, 2] = (value + bias[1:2, :]).astype(BF)

    def attend(h, p, e_ref):
        lanes = span(p, 128)
        q2, k2, v2 = qkv[h, 0, :, lanes], qkv[h, 1, :, lanes], qkv[h, 2, :, lanes]
        parts = []
        for head in range(2):
            mine = low_lanes if head == 0 else jnp.logical_not(low_lanes)
            scores = dot(jnp.where(mine, q2, zero), k2, 1, 1) + key_fill
            peak = jnp.max(scores, axis=-1, keepdims=True)
            e = jnp.exp(scores - peak).astype(BF)
            e_ref[2 * p + head] = e
            parts.append(dot(e, jnp.where(mine, v2, one), 1, 0))
        total = pltpu.roll(jnp.where(low_lanes, parts[1], parts[0]), HEAD, 1)
        inverse = 1.0 / total
        inv[h, :, lanes] = inverse
        ctx[:, span(h * pairs + p, 128)] = (jnp.where(low_lanes, parts[0], parts[1]) * inverse).astype(BF)

    def attend_half(h, slots):
        def body(p, _):
            attend(h, p, (u1, u2)[h])
            for at_pair, slot in slots:
                @pl.when(p == at_pair)
                def _():
                    progress(slot)
            return 0
        lax.fori_loop(0, pairs, body, 0)

    def e_copy(h, back):
        ref, buf = e_hbm.at[pl.ds(h * 8, 8)], (u1 if back else (u1, u2)[h])
        return pltpu.make_async_copy(ref, buf, e_sem.at[h]) if back else pltpu.make_async_copy(buf, ref, e_sem.at[h])

    def out_project(h):
        for d in range(2):
            weight_load(h, 16 + d).wait()
            term = dot(ctx[:, h * half_w : (h + 1) * half_w], (own, oth)[h][16 + d], 1, 0)
            lanes = slice(d * TILE, (d + 1) * TILE)
            acc[:, lanes] = term if h == 0 else acc[:, lanes] + term

    load_x.wait()
    project(0)
    attend_half(0, ((1, 0), (3, 1)))
    e_copy(0, False).start()
    out_project(0)
    for slot in (2, 3, 4, 5):
        progress(slot)
    send_bias.wait()
    project(1)
    attend_half(1, ((1, 6),))
    e_copy(1, False).start()
    out_project(1)
    progress(7)

    def blocks(body):
        def run(b, _):
            body(span(b, ROWS_AT_ONCE), b)
            return 0
        lax.fori_loop(0, seq // ROWS_AT_ONCE, run, 0)

    def mean(v):
        return jnp.sum(v, axis=-1, keepdims=True) * (1.0 / width)

    small[...] = jnp.zeros_like(small)
    b_out, gain1, shift1 = vec[0:1, :], vec[1:2, :], vec[2:3, :]
    b_down, gain2, shift2 = vec[3:4, :], vec[4:5, :], vec[5:6, :]

    def norm_one(r, b):
        v = xv[r, :].astype(F32) + (acc[r, :] + b_out)
        center = v - mean(v)
        inverse = lax.rsqrt(mean(center * center) + EPSILON)
        hat = center * inverse
        xhat[r, :] = hat
        rs1[r, :] = jnp.broadcast_to(inverse, (ROWS_AT_ONCE, 128))
        nlow[r, :] = (hat * gain1 + shift1).astype(BF)
    blocks(norm_one)
    e_copy(0, False).wait()
    e_copy(1, False).wait()

    def hidden_half(h, slots):
        bias, weights = (bias_own, bias_oth)[h], (own, oth)[h]
        for f in range(4):
            for k in (8 + 2 * f, 9 + 2 * f):
                weight_load(h, k).wait()
            hidden = dot(nlow[...], weights[8 + 2 * f : 10 + 2 * f].reshape(width, TILE), 1, 0) + bias[2 + f : 3 + f, :]
            cdf = 0.5 + 0.5 * lax.erf(hidden * 0.7071067811865476)
            u1[4 * h + f] = (hidden * cdf).astype(BF)
            u2[4 * h + f] = (cdf + hidden * (jnp.exp(hidden * hidden * -0.5) * 0.3989422804014327)).astype(BF)
            if f in slots:
                progress(slots[f])

    def down_half(h, tiles, clear=False):
        for f in tiles:
            for d in range(2):
                weight_load(h, 2 * f + d).wait()
                term = dot(u1[4 * h + f], (own, oth)[h][2 * f + d], 1, 0)
                lanes = slice(d * TILE, (d + 1) * TILE)
                acc[:, lanes] = term if clear and f == tiles[0] else acc[:, lanes] + term

    hidden_half(0, {2: 8})
    down_half(0, (0, 1, 2, 3), True)
    hidden_half(1, {1: 9})
    down_half(1, (0, 1))
    progress(10)
    down_half(1, (2, 3))

    load_cot.wait()
    valid_limit = lengths[y]

    def norm_two(r, b):
        normed = xhat[r, :] * gain1 + shift1
        v = normed + (acc[r, :] + b_down)
        center = v - mean(v)
        inverse = lax.rsqrt(mean(center * center) + EPSILON)
        hat = center * inverse
        gctx[r, :] = (hat * gain2 + shift2).astype(BF)
        position = b * ROWS_AT_ONCE + lax.broadcasted_iota(jnp.int32, (ROWS_AT_ONCE, 1), 0)
        g_out = jnp.where(position < valid_limit, gsec[r, :].astype(F32), 0.0)
        scaled = g_out * gain2
        g_two = inverse * (scaled - mean(scaled) - hat * mean(scaled * hat))
        low = g_two.astype(BF)
        acc[r, :] = g_two
        gsec[r, :] = low
        small[3:4, :] += jnp.sum(g_out * hat, axis=0, keepdims=True)
        small[4:5, :] += jnp.sum(g_out, axis=0, keepdims=True)
        small[5:6, :] += jnp.sum(low.astype(F32), axis=0, keepdims=True)
    blocks(norm_two)
    out_copy = pltpu.make_async_copy(gctx, out_hbm, o_sem.at[0])
    gin_copy = pltpu.make_async_copy(nlow, gin_hbm, o_sem.at[1])
    out_copy.start()

    half, quarter, part = TILE // 2, TILE // 4, TILE // 16
    c_rows = span(c, half)
    cn_rows = span(1 - c, half)
    x_rows = pl.ds(pl.multiple_of(c * half + x * quarter, quarter), quarter)
    xn_rows = pl.ds(pl.multiple_of(c * half + (1 - x) * quarter, quarter), quarter)

    def z_rows(v):
        return pl.ds(pl.multiple_of(c * half + x * quarter + v * part, part), part)

    def message(k, kind):
        slot = k % RING
        if kind == 0: src, dst, peer = own.at[k, cn_rows], r1.at[slot, 0], to_c
        if kind == 1: src, dst, peer = oth.at[k, cn_rows], r1.at[slot, 1], to_c
        if kind == 2: src, dst, peer = oth.at[k, c_rows], ry.at[slot], to_y
        if kind == 3: src, dst, peer = own.at[k, xn_rows], rx.at[slot], to_x
        if 4 <= kind < 7: src, dst, peer = own.at[k, z_rows(z_of[kind - 4])], rz.at[slot, kind - 4], to_z[kind - 4]
        if 7 <= kind < 10: src, dst, peer = oth.at[k, z_rows(z)], oth.at[k, z_rows(z)], to_z[kind - 7]
        if kind == 10: src, dst, peer = oth.at[k, x_rows], oth.at[k, x_rows], to_x
        if kind == 11: src, dst, peer = oth.at[k, c_rows], tiles_hbm.at[k, c_rows], to_c
        return copy_to(src, dst, send.at[slot, kind], recv.at[slot, kind], peer)

    def tile_copy(k):
        return pltpu.make_async_copy(oth.at[k, c_rows], tiles_hbm.at[k, c_rows], t_sem.at[k % RING])

    def add_into(dst, src, n):
        def body(i, _):
            r = span(i, 64)
            dst[r, :] = dst[r, :] + src[r, :]
            return 0
        lax.fori_loop(0, n // 64, body, 0)

    def wait(k, kinds):
        for kind in kinds:
            message(k, kind).wait()

    def reduce_stage(k, s):
        slot = k % RING
        if s == 0:
            message(k, 0).start()
            message(k, 1).start()
        if s == 1:
            wait(k, (0, 1))
            add_into(oth.at[k, c_rows], r1.at[slot, 1], half)
            message(k, 2).start()
            add_into(own.at[k, c_rows], r1.at[slot, 0], half)
        if s == 2:
            wait(k, (2,))
            add_into(own.at[k, c_rows], ry.at[slot], half)
            message(k, 3).start()
        if s == 3:
            wait(k, (3,))
            add_into(own.at[k, x_rows], rx.at[slot], quarter)
            for kind in (4, 5, 6):
                message(k, kind).start()
        if s == 4:
            wait(k, (4, 5, 6))
            total = own[k, z_rows(z), :].astype(F32)
            for d in range(3):
                total = total + rz[slot, d].astype(F32)
            oth[k, z_rows(z), :] = total.astype(BF)
            for kind in (7, 8, 9):
                message(k, kind).start()
        if s == 5:
            wait(k, (7, 8, 9))
            message(k, 10).start()
        if s == 6:
            wait(k, (10,))
            message(k, 11).start()
            tile_copy(k).start()
        if s == 7:
            wait(k, (11,))
            tile_copy(k).wait()

    def reduce_step(t):
        for s in range(8):
            @pl.when((t >= s) & (t - s < CHUNKS))
            def _():
                reduce_stage(t - s, s)

    def small_messages(i):
        if i == 0:
            return [copy_to(small, s0, small_send.at[0], small_recv.at[0], to_c)]
        if i == 1:
            return [
                copy_to(small.at[pl.ds(0, 8)], s1.at[pl.ds(0, 8)], small_send.at[1], small_recv.at[1], to_y),
                copy_to(small.at[pl.ds(16, 8)], s1.at[pl.ds(8, 8)], small_send.at[2], small_recv.at[2], to_y),
            ]
        got, peer = ((s2, to_x), (s3, to_zp), (s4, to_zq))[i - 2]
        return [copy_to(small.at[pl.ds(0, 16)], got, small_send.at[i + 1], small_recv.at[i + 1], peer)]

    def small_step(i):
        if i > 0:
            for m in small_messages(i - 1):
                m.wait()
            if i == 1:
                small[...] = small[...] + s0[...]
            else:
                small[0:16, :] = small[0:16, :] + (s1, s2, s3, s4)[i - 2][...]
        if i < 5:
            for m in small_messages(i):
                m.start()

    def fetch_ffn(t, start):
        for h in range(2):
            @pl.when((t >= 4 * h) & (t < 4 * h + 4))
            def _():
                b, a = fetch_in(h, t - 4 * h, t % 3), fetch_down(h, t - 4 * h, t % 2)
                if start:
                    b.start()
                    a.start()
                else:
                    b.wait()
                    a.wait()

    def down_tiles(k):
        g = gsec[:, span(k % 2, TILE)]
        own[k] = dot(u1[k // 2], g, 0, 0).astype(BF)
        oth[k] = dot(u1[4 + k // 2], g, 0, 0).astype(BF)

    def hidden_back(t):
        fetch_ffn(t, False)
        g_active = dot(gsec[...], ring_a[t % 2], 1, 1)
        g_hidden = (g_active * u2[t].astype(F32)).astype(BF)
        u2[t] = g_hidden
        total = jnp.sum(g_hidden.astype(F32), axis=0, keepdims=True)
        small[pl.ds(9 + 8 * (t // 4) + (t % 4) // 2, 1), span(t % 2, TILE)] = total
        acc[...] += dot(g_hidden, ring_b[t % 3], 1, 1)

    def in_tiles(k):
        j = k - 8
        a = nlow[:, span(j % 2, TILE)]
        own[k] = dot(a, u2[j // 2], 0, 0).astype(BF)
        oth[k] = dot(a, u2[4 + j // 2], 0, 0).astype(BF)

    def norm_one_back(r, b):
        g_normed, hat = acc[r, :], xhat[r, :]
        scaled = g_normed * gain1
        g_first = rs1[r, 0:1] * (scaled - mean(scaled) - hat * mean(scaled * hat))
        low = g_first.astype(BF)
        acc[r, :] = g_first
        gsec[r, :] = low
        small[0:1, :] += jnp.sum(g_normed * hat, axis=0, keepdims=True)
        small[1:2, :] += jnp.sum(g_normed, axis=0, keepdims=True)
        small[2:3, :] += jnp.sum(low.astype(F32), axis=0, keepdims=True)

    def attend_back(h, p):
        lanes = span(p, 128)
        wide = span(h * pairs + p, 128)
        q2, k2, v2 = qkv[h, 0, :, lanes], qkv[h, 1, :, lanes], qkv[h, 2, :, lanes]
        g = gctx[:, wide].astype(F32) * inv[h, :, lanes]
        low = g.astype(BF)
        less = pltpu.roll(-(g * ctx[:, wide].astype(F32)), HEAD, 1).astype(BF)
        g_q, g_k, g_v = [], [], []
        for head in range(2):
            mine = low_lanes if head == 0 else jnp.logical_not(low_lanes)
            e = u1[2 * p + head]
            g_scores = (dot(jnp.where(mine, low, less), jnp.where(mine, v2, one), 1, 1) * e.astype(F32)).astype(BF)
            g_q.append(dot(g_scores, k2, 1, 0))
            rows = slice(head * HEAD, head * HEAD + HEAD)
            g_k.append(dot(q2, g_scores, 0, 0)[rows])
            g_v.append(dot(low, e, 0, 0)[rows])
        qkv[h, 0, :, lanes] = (jnp.where(low_lanes, g_q[0], g_q[1]) * scale).astype(BF)
        qkv[h, 1, :, lanes] = jnp.concatenate(g_k, axis=0).T.astype(BF)
        qkv[h, 2, :, lanes] = jnp.concatenate(g_v, axis=0).T.astype(BF)

    fetch_ffn(0, True)

    def iteration(t, _):
        @pl.when(t < 8)
        def _():
            down_tiles(t)
        @pl.when((t >= 8) & (t < 16))
        def _():
            in_tiles(t)
        @pl.when((t >= 16) & (t < 18))
        def _():
            g = gsec[:, span(t - 16, TILE)]
            own[t] = dot(ctx[:, :half_w], g, 0, 0).astype(BF)
            oth[t] = dot(ctx[:, half_w:], g, 0, 0).astype(BF)
        @pl.when((t >= 18) & (t < 24))
        def _():
            j = t - 18
            a = xv[:, span(j % 2, TILE)]
            own[t] = dot(a, qkv[0, j // 2], 0, 0).astype(BF)
            oth[t] = dot(a, qkv[1, j // 2], 0, 0).astype(BF)
        reduce_step(t)
        @pl.when(t < 8)
        def _():
            @pl.when(t < 7)
            def _():
                fetch_ffn(t + 1, True)
            hidden_back(t)
        @pl.when(t == 8)
        def _():
            e_copy(0, True).start()
            fetch_out(0).start()
            fetch_out(1).start()
            blocks(norm_one_back)
        @pl.when(t == 9)
        def _():
            out_copy.wait()
            for h in range(2):
                fetch_out(h).wait()
                gctx[:, h * half_w : (h + 1) * half_w] = dot(gsec[...], ring_a[h], 1, 1).astype(BF)
            e_copy(0, True).wait()
        for first, h in ((10, 0), (13, 1)):
            @pl.when((t >= first) & (t < first + 2))
            def _():
                def body(p, _):
                    attend_back(h, 2 * (t - first) + p)
                    return 0
                lax.fori_loop(0, 2, body, 0)
            @pl.when(t == first + 1)
            def _():
                if h == 0:
                    e_copy(1, True).start()
                for i in (0, 2):
                    total = jnp.sum(qkv[h, i].astype(F32), axis=0, keepdims=True)
                    small[8 + 8 * h : 9 + 8 * h, (i // 2) * TILE : (i // 2 + 1) * TILE] = total
        @pl.when(t == 12)
        def _():
            e_copy(1, True).wait()
        for h in range(2):
            first = 15 + 2 * h
            @pl.when(t == first)
            def _():
                for i in range(3):
                    fetch_qkv(h, i).start()
            @pl.when(t == first + 1)
            def _():
                for i in range(3):
                    fetch_qkv(h, i).wait()
                    acc[...] += dot(qkv[h, i], ring_b[i], 1, 1)
        @pl.when(t == 19)
        def _():
            def last(r, b):
                nlow[r, :] = acc[r, :].astype(BF)
            blocks(last)
            gin_copy.start()
        for i in range(6):
            @pl.when(t == 16 + i)
            def _():
                small_step(i)
        return 0

    lax.fori_loop(0, CHUNKS + 7, iteration, 0)
    small_out[...] = small[0:16, :]
    gin_copy.wait()


def layer(lengths, inputs, cotangent, wq, w_out, w_in, w_down, vectors):
    seq, width = inputs.shape
    half = TILE // 2
    vm, dma = pltpu.VMEM, pltpu.SemaphoreType.DMA
    anywhere, inside = pl.BlockSpec(memory_space=pl.ANY), pl.BlockSpec(memory_space=pltpu.VMEM)
    like = lambda a: jax.ShapeDtypeStruct(a.shape, a.dtype)
    tile_shape = (TILE, TILE)
    return pl.pallas_call(
        layer_kernel,
        out_shape=[
            like(inputs), like(inputs), jax.ShapeDtypeStruct((CHUNKS,) + tile_shape, BF),
            jax.ShapeDtypeStruct((16, width), F32),
            like(wq), like(w_out), like(w_in), like(w_down),
            jax.ShapeDtypeStruct((16,) + tile_shape, BF),
        ],
        in_specs=[pl.BlockSpec(memory_space=pltpu.SMEM)] + [anywhere] * 6 + [inside] * 8,
        out_specs=[anywhere] * 3 + [inside] + [anywhere] * 5,
        scratch_shapes=[
            vm((seq, width), BF), vm((seq, width), BF), vm((seq, width), BF), vm((seq, width), BF), vm((seq, width), BF),
            vm((2, 3) + tile_shape, BF), vm((2,) + tile_shape, F32),
            vm((seq, width), F32), vm((seq, 128), F32), vm((seq, width), F32),
            vm((8,) + tile_shape, BF), vm((8,) + tile_shape, BF),
            vm((CHUNKS,) + tile_shape, BF), vm((CHUNKS,) + tile_shape, BF),
            vm((RING, 2, half, TILE), BF), vm((RING, half, TILE), BF),
            vm((RING, half // 2, TILE), BF), vm((RING, 3, half // 8, TILE), BF),
            vm((2, TILE, width), BF), vm((3, width, TILE), BF),
            vm((8, width), F32), vm((8, TILE), F32), vm((8, TILE), F32), vm((24, width), F32), vm((24, width), F32),
            vm((16, width), F32), vm((16, width), F32), vm((16, width), F32), vm((16, width), F32),
            dma((2,)), dma((2, CHUNKS)), dma((2,)), dma((3,)), dma((2,)), dma((2,)), dma((RING,)),
            dma((9, 12)), dma((9, 12)), dma((RING, MESSAGES)), dma((RING, MESSAGES)), dma((6,)), dma((6,)),
        ],
        compiler_params=pltpu.CompilerParams(
            collective_id=1, has_side_effects=True, vmem_limit_bytes=VMEM_BYTES
        ),
    )(lengths, inputs, cotangent, wq, w_out, w_in, w_down, *vectors)


def widen_kernel(
    tiles, out_in, gin_in, sums, down, within, out, three, out_out, gin_out,
    b_qv, b_out, gain1, shift1, b_in, b_down, gain2, shift2, low, wide, held, in_sem, out_sem, pass_sem,
):
    enter = [pltpu.make_async_copy(ref, held.at[i], pass_sem.at[i]) for i, ref in enumerate((out_in, gin_in))]
    leave = [pltpu.make_async_copy(held.at[i], ref, pass_sem.at[i]) for i, ref in enumerate((out_out, gin_out))]
    loads = [pltpu.make_async_copy(tiles.at[k], low.at[k], in_sem.at[k]) for k in range(CHUNKS)]
    for copy in loads[:RING] + enter + loads[RING:]:
        copy.start()
    width, half = sums.shape[1], b_qv.shape[1]
    for ref, row in ((gain1, 0), (shift1, 1), (b_out, 2), (gain2, 3), (shift2, 4), (b_down, 5)):
        ref[...] = sums[row, :]
    for i in range(2):
        b_qv[i : i + 1, :] = sums[8:9, i * half : (i + 1) * half]
        b_in[i * width : (i + 1) * width] = sums[9 + i, :]

    def store(k):
        which, where = tile_place(k)
        return pltpu.make_async_copy(wide.at[k % RING], (down, within, out, three)[which].at[where], out_sem.at[k % RING])

    stores = [store(k) for k in range(CHUNKS)]
    for k in range(CHUNKS):
        loads[k].wait()
        if k >= RING:
            stores[k - RING].wait()
        def body(i, _):
            r = span(i, 32)
            wide[k % RING, r, :] = low[k, r, :].astype(F32)
            return 0
        lax.fori_loop(0, TILE // 32, body, 0)
        stores[k].start()
        if k == RING:
            for into, back in zip(enter, leave):
                into.wait()
                back.start()
    for copy in stores[CHUNKS - RING :] + leave:
        copy.wait()


def widen(tiles, output, grad_inputs, sums, half_hidden, width, half_width):
    tile, vm, dma = (TILE, TILE), pltpu.VMEM, pltpu.SemaphoreType.DMA
    anywhere, inside = pl.BlockSpec(memory_space=pl.ANY), pl.BlockSpec(memory_space=pltpu.VMEM)
    wide = lambda *shape: jax.ShapeDtypeStruct(shape, F32)
    return pl.pallas_call(
        widen_kernel,
        out_shape=[
            wide(half_hidden, width), wide(width, half_hidden), wide(half_width, width), wide(3, width, half_width),
            jax.ShapeDtypeStruct(output.shape, output.dtype), jax.ShapeDtypeStruct(output.shape, output.dtype),
            wide(2, half_width), wide(width), wide(width), wide(width), wide(half_hidden), wide(width), wide(width), wide(width),
        ],
        in_specs=[anywhere] * 3 + [inside],
        out_specs=[anywhere] * 6 + [inside] * 8,
        scratch_shapes=[
            vm((CHUNKS,) + tile, BF), vm((RING,) + tile, F32), vm((2,) + output.shape, BF), dma((CHUNKS,)), dma((RING,)), dma((2,)),
        ],
        compiler_params=pltpu.CompilerParams(vmem_limit_bytes=60 << 20),
    )(tiles, output, grad_inputs, sums)


def split_by_sequence(
    inputs, lengths, w_qkv, b_qv, w_out, b_out, gain_one, shift_one, w_in, b_in, w_down, b_down, gain_two, shift_two,
    cotangent,
):
    rows, width = inputs.shape
    half_width, half_hidden = w_qkv.shape[2], w_in.shape[1]
    wq = w_qkv.transpose(1, 0, 2)
    vectors = (b_out, gain_one, shift_one, b_down, gain_two, shift_two, b_qv, b_in)
    made = layer(lengths, inputs, cotangent, wq, w_out, w_in, w_down, vectors)
    output, grad_inputs, tiles, sums = made[:4]
    (
        g_w_down, g_w_in, g_w_out, g_w_qkv, output, grad_inputs,
        g_b_qv, g_b_out, g_gain_one, g_shift_one, g_b_in, g_b_down, g_gain_two, g_shift_two,
    ) = widen(tiles, output, grad_inputs, sums, half_hidden, width, half_width)
    return (
        output, grad_inputs, g_w_qkv.transpose(1, 0, 2), g_b_qv, g_w_out, g_b_out, g_gain_one, g_shift_one,
        g_w_in, g_b_in, g_w_down, g_b_down, g_gain_two, g_shift_two,
    )


def solution(mesh):
    small_mesh = mesh.shape["tensor"] == 2 and mesh.shape["dp"] == 2 * N_X * N_Z
    step = split_by_sequence if small_mesh else general
    in_specs = (
        P(("dp", "tensor"), None),
        P("dp"),
        P(None, None, "tensor"),
        P(None, "tensor"),
        P("tensor", None),
        P(),
        P(),
        P(),
        P(None, "tensor"),
        P("tensor"),
        P("tensor", None),
        P(),
        P(),
        P(),
        P(("dp", "tensor"), None),
    )
    out_specs = (
        P(("dp", "tensor"), None),
        P(("dp", "tensor"), None),
        P(None, None, "tensor"),
        P(None, "tensor"),
        P("tensor", None),
        P(),
        P(),
        P(),
        P(None, "tensor"),
        P("tensor"),
        P("tensor", None),
        P(),
        P(),
        P(),
    )
    return jax.shard_map(step, mesh=mesh, in_specs=in_specs, out_specs=out_specs, check_vma=False)
```

```python
import jax
import jax.numpy as jnp
from jax import lax
from jax.experimental import pallas as pl
from jax.experimental.pallas import tpu as pltpu
from jax.sharding import PartitionSpec as P

MESH = pl.DeviceIdType.MESH
N_Z, N_X = 4, 2
TILE = 512
MESSAGES = 12
VMEM_BYTES = 63 << 20

HEAD = 64
SEQ = 512
SEQ_DEV = 2


EPSILON = 1e-12
NEG_FILL = -1000000000.0


def gelu_exact(values):
    return jax.nn.gelu(values, approximate=False)


def norm_forward(values, gain_vec, shift_vec):
    center = values - jnp.mean(values, axis=-1, keepdims=True)
    spread = jnp.mean(center * center, axis=-1, keepdims=True)
    inverse = lax.rsqrt(spread + EPSILON)
    scaled = center * inverse
    return (scaled * gain_vec + shift_vec, scaled, inverse)


def norm_backward(grad_out, scaled, inverse, gain_vec):
    grad_scaled = grad_out * gain_vec
    mean_one = jnp.mean(grad_scaled, axis=-1, keepdims=True)
    mean_two = jnp.mean(grad_scaled * scaled, axis=-1, keepdims=True)
    grad_in = inverse * (grad_scaled - mean_one - scaled * mean_two)
    return (grad_in, jnp.sum(grad_out * scaled, axis=0), jnp.sum(grad_out, axis=0))


def masked_scores(queries, key_rows, length):
    score_scale = HEAD ** (-0.5)
    scores = (
        jnp.einsum("qhe,khe->hqk", queries, key_rows, preferred_element_type=jnp.float32)
        * score_scale
    )
    key_valid = (jnp.arange(SEQ) < length)[None, None, :]
    return jnp.where(key_valid, scores, NEG_FILL)


def attend_forward(element):
    queries, key_rows, value_rows, length = element
    scores = masked_scores(queries, key_rows, length)
    peak_score = jnp.max(scores, axis=-1, keepdims=True)
    shifted_exp = jnp.exp(scores - peak_score)
    denominator = jnp.sum(shifted_exp, axis=-1, keepdims=True)
    probability = (shifted_exp / denominator).astype(jnp.bfloat16)
    context = jnp.einsum(
        "hqk,khe->qhe", probability, value_rows, preferred_element_type=jnp.float32
    )
    return (context.astype(jnp.bfloat16), (peak_score + jnp.log(denominator))[..., 0])


def attend_backward(element):
    queries, key_rows, value_rows, length, log_total, grad_context = element
    score_scale = HEAD ** (-0.5)
    scores = masked_scores(queries, key_rows, length)
    probability = jnp.exp(scores - log_total[..., None])
    grad_prob = jnp.einsum(
        "qhe,khe->hqk", grad_context, value_rows, preferred_element_type=jnp.float32
    )
    grad_value = jnp.einsum(
        "hqk,qhe->khe",
        probability.astype(jnp.bfloat16),
        grad_context,
        preferred_element_type=jnp.float32,
    )
    grad_scores = probability * (
        grad_prob - jnp.sum(probability * grad_prob, axis=-1, keepdims=True)
    )
    grad_scores = grad_scores.astype(jnp.bfloat16)
    grad_query = (
        jnp.einsum("hqk,khe->qhe", grad_scores, key_rows, preferred_element_type=jnp.float32)
        * score_scale
    )
    grad_key = (
        jnp.einsum("hqk,qhe->khe", grad_scores, queries, preferred_element_type=jnp.float32)
        * score_scale
    )
    return jnp.stack([grad_query, grad_key, grad_value], axis=1).astype(jnp.bfloat16)


def row_mask(lengths, rows_dev):
    places = lax.axis_index("tensor") * rows_dev + jnp.arange(rows_dev)
    sequence_of = places // SEQ
    offset = places % SEQ
    matches = sequence_of[:, None] == jnp.arange(lengths.shape[0])[None, :]
    limit_rows = jnp.sum(jnp.where(matches, lengths[None, :], 0), axis=1)
    return (offset < limit_rows).astype(jnp.float32)[:, None]


def forward_pass(inputs, lengths, weights):
    (
        w_qkv,
        b_qv,
        w_out,
        b_out,
        gain_one,
        shift_one,
        w_in,
        b_in,
        w_down,
        b_down,
        gain_two,
        shift_two,
    ) = weights
    width_dev = w_qkv.shape[2]
    gathered = lax.all_gather(inputs, "tensor", axis=0, tiled=True)
    bias_three = jnp.stack([b_qv[0], jnp.zeros_like(b_qv[0]), b_qv[1]]).astype(jnp.float32)
    projected = (
        jnp.einsum("td,dcf->tcf", gathered, w_qkv, preferred_element_type=jnp.float32) + bias_three
    ).astype(jnp.bfloat16)
    shaped = projected.reshape(SEQ_DEV, SEQ, 3, width_dev // HEAD, HEAD)
    context, log_total = lax.map(
        attend_forward, (shaped[:, :, 0], shaped[:, :, 1], shaped[:, :, 2], lengths)
    )
    context = context.reshape(SEQ_DEV * SEQ, width_dev)
    segment = context
    branch = lax.psum_scatter(
        jnp.dot(segment, w_out, preferred_element_type=jnp.float32).astype(jnp.bfloat16),
        "tensor",
        scatter_dimension=0,
        tiled=True,
    ).astype(jnp.float32) + b_out.astype(jnp.float32)
    normed, scaled_one, inverse_one = norm_forward(
        inputs.astype(jnp.float32) + branch,
        gain_one.astype(jnp.float32),
        shift_one.astype(jnp.float32),
    )
    normed_all = lax.all_gather(normed.astype(jnp.bfloat16), "tensor", axis=0, tiled=True)
    hidden = jnp.dot(normed_all, w_in, preferred_element_type=jnp.float32) + b_in.astype(
        jnp.float32
    )
    active = gelu_exact(hidden).astype(jnp.bfloat16)
    segment = active
    second = lax.psum_scatter(
        jnp.dot(segment, w_down, preferred_element_type=jnp.float32).astype(jnp.bfloat16),
        "tensor",
        scatter_dimension=0,
        tiled=True,
    ).astype(jnp.float32) + b_down.astype(jnp.float32)
    output, scaled_two, inverse_two = norm_forward(
        normed + second, gain_two.astype(jnp.float32), shift_two.astype(jnp.float32)
    )
    return (
        gathered,
        projected,
        context,
        log_total,
        scaled_one,
        inverse_one,
        normed_all,
        hidden,
        active,
        scaled_two,
        inverse_two,
        output,
    )


def general(
    inputs,
    lengths,
    w_qkv,
    b_qv,
    w_out,
    b_out,
    gain_one,
    shift_one,
    w_in,
    b_in,
    w_down,
    b_down,
    gain_two,
    shift_two,
    cotangent,
):
    weights = (
        w_qkv,
        b_qv,
        w_out,
        b_out,
        gain_one,
        shift_one,
        w_in,
        b_in,
        w_down,
        b_down,
        gain_two,
        shift_two,
    )
    first_pass = forward_pass(inputs, lengths, weights)
    output = first_pass[11].astype(jnp.bfloat16)
    recorded = forward_pass(inputs, lengths, weights)
    (
        gathered,
        projected,
        context,
        log_total,
        scaled_one,
        inverse_one,
        normed_all,
        hidden,
        active,
        scaled_two,
        inverse_two,
        _,
    ) = recorded
    rows_dev = inputs.shape[0]
    width_dev = w_qkv.shape[2]
    grad_out = cotangent.astype(jnp.float32) * row_mask(lengths, rows_dev)
    grad_two, grad_gain_two, grad_shift_two = norm_backward(
        grad_out, scaled_two, inverse_two, gain_two.astype(jnp.float32)
    )
    grad_second = grad_two.astype(jnp.bfloat16)
    grad_b_down = jnp.sum(grad_second.astype(jnp.float32), axis=0)
    second_all = lax.all_gather(grad_second, "tensor", axis=0, tiled=True)
    grad_w_down = jnp.einsum("tf,td->fd", active, second_all, preferred_element_type=jnp.float32)
    grad_active = jnp.einsum("td,fd->tf", second_all, w_down, preferred_element_type=jnp.float32)
    _, gelu_pull = jax.vjp(gelu_exact, hidden)
    grad_hidden = gelu_pull(grad_active)[0].astype(jnp.bfloat16)
    grad_b_in = jnp.sum(grad_hidden.astype(jnp.float32), axis=0)
    grad_w_in = jnp.einsum("td,tf->df", normed_all, grad_hidden, preferred_element_type=jnp.float32)
    segment = grad_hidden
    grad_normed = grad_two + lax.psum_scatter(
        jnp.einsum("tf,df->td", segment, w_in, preferred_element_type=jnp.float32).astype(
            jnp.bfloat16
        ),
        "tensor",
        scatter_dimension=0,
        tiled=True,
    ).astype(jnp.float32)
    grad_first, grad_gain_one, grad_shift_one = norm_backward(
        grad_normed, scaled_one, inverse_one, gain_one.astype(jnp.float32)
    )
    grad_branch = grad_first.astype(jnp.bfloat16)
    grad_b_out = jnp.sum(grad_branch.astype(jnp.float32), axis=0)
    branch_all = lax.all_gather(grad_branch, "tensor", axis=0, tiled=True)
    grad_w_out = jnp.einsum("tf,td->fd", context, branch_all, preferred_element_type=jnp.float32)
    grad_context = jnp.einsum(
        "td,fd->tf", branch_all, w_out, preferred_element_type=jnp.float32
    ).astype(jnp.bfloat16)
    heads_dev = width_dev // HEAD
    shaped = projected.reshape(SEQ_DEV, SEQ, 3, heads_dev, HEAD)
    grad_shaped = grad_context.reshape(SEQ_DEV, SEQ, heads_dev, HEAD)
    grad_proj = lax.map(
        attend_backward,
        (shaped[:, :, 0], shaped[:, :, 1], shaped[:, :, 2], lengths, log_total, grad_shaped),
    )
    grad_proj = grad_proj.reshape(SEQ_DEV * SEQ, 3, width_dev)
    grad_w_qkv = jnp.einsum("td,tcf->dcf", gathered, grad_proj, preferred_element_type=jnp.float32)
    grad_b_qv = jnp.sum(grad_proj[:, 0::2].astype(jnp.float32), axis=0)
    segment = grad_proj
    grad_inputs = (
        grad_first
        + lax.psum_scatter(
            jnp.einsum("tcf,dcf->td", segment, w_qkv, preferred_element_type=jnp.float32).astype(
                jnp.bfloat16
            ),
            "tensor",
            scatter_dimension=0,
            tiled=True,
        ).astype(jnp.float32)
    ).astype(jnp.bfloat16)
    small_terms = jnp.stack(
        [grad_gain_one, grad_shift_one, grad_b_out, grad_gain_two, grad_shift_two, grad_b_down]
    )
    grad_w_qkv, grad_b_qv, grad_w_out, grad_w_in, grad_b_in, grad_w_down, small_terms = (
        lax.psum(grad_w_qkv.astype(jnp.bfloat16), "dp").astype(jnp.float32),
        lax.psum(grad_b_qv.astype(jnp.bfloat16), "dp").astype(jnp.float32),
        lax.psum(grad_w_out.astype(jnp.bfloat16), "dp").astype(jnp.float32),
        lax.psum(grad_w_in.astype(jnp.bfloat16), "dp").astype(jnp.float32),
        lax.psum(grad_b_in.astype(jnp.bfloat16), "dp").astype(jnp.float32),
        lax.psum(grad_w_down.astype(jnp.bfloat16), "dp").astype(jnp.float32),
        lax.psum(small_terms.astype(jnp.bfloat16), "dp").astype(jnp.float32),
    )
    small_sums = lax.psum(small_terms, "tensor")
    return (
        output,
        grad_inputs,
        grad_w_qkv,
        grad_b_qv,
        grad_w_out,
        small_sums[2],
        small_sums[0],
        small_sums[1],
        grad_w_in,
        grad_b_in,
        grad_w_down,
        small_sums[5],
        small_sums[3],
        small_sums[4],
    )


def place():
    dp = lax.axis_index("dp")
    return dp // (2 * N_X), (dp // 2) % N_X, dp % 2, lax.axis_index("tensor")


def at(z, x, c, y):
    return ((z * N_X + x) * 2 + c, y)


def greet(peers):
    barrier = pltpu.get_barrier_semaphore()
    for peer in peers:
        pl.semaphore_signal(barrier, inc=1, device_id=peer, device_id_type=MESH)
    pl.semaphore_wait(barrier, len(peers))


def copy_to(src, dst, send_sem, recv_sem, peer):
    return pltpu.make_async_remote_copy(
        src_ref=src, dst_ref=dst, send_sem=send_sem, recv_sem=recv_sem,
        device_id=peer, device_id_type=MESH,
    )


CHUNKS = 24
RING = 4
BF, F32 = jnp.bfloat16, jnp.float32
ROWS_AT_ONCE = 64


def dot(a, b, ca, cb):
    return lax.dot_general(a, b, (((ca,), (cb,)), ((), ())), preferred_element_type=F32)


def span(index, size):
    return pl.ds(pl.multiple_of(index * size, size), size)


def tile_place(k):
    if k < 8:
        return 0, (slice(k // 2 * TILE, (k // 2 + 1) * TILE), slice(k % 2 * TILE, (k % 2 + 1) * TILE))
    if k < 16:
        k -= 8
        return 1, (slice(k % 2 * TILE, (k % 2 + 1) * TILE), slice(k // 2 * TILE, (k // 2 + 1) * TILE))
    if k < 18:
        k -= 16
        return 2, (slice(0, TILE), slice(k * TILE, (k + 1) * TILE))
    k -= 18
    return 3, (k // 2, slice(k % 2 * TILE, (k % 2 + 1) * TILE), slice(0, TILE))


def layer_kernel(
    lengths, x_hbm, cot_hbm, wq_own, wo_own, wi_own, wd_own, in1, in2, in3, in4, in5, in6, in_qv, in_hidden,
    out_ref, gin_ref, oth, small_out, wq_oth, wo_oth, wi_oth, wd_oth, e_hbm,
    xv, nlow, gsec, gctx, ctx, qkv, inv, xhat, rs1, acc, u1, u2, own, r1, ry, rx, rz,
    ring_a, ring_b, vec, bias_own, bias_oth, small, s0, s1, s2, s3, s4,
    load_sem, w_sem, a_sem, b_sem, e_sem, g_send, g_recv, send, recv, small_send, small_recv,
):
    z, x, c, y = place()
    zb = z % 2
    z_of = [(z + d) % N_Z for d in (1, 2, 3)]
    to_c, to_y, to_x = at(z, x, 1 - c, y), at(z, x, c, 1 - y), at(z, 1 - x, c, y)
    to_z = [at(v, x, c, y) for v in z_of]
    to_zp, to_zq = at(z + 1 - 2 * zb, x, c, y), at((z + 2) % N_Z, x, c, y)
    seq, width = xv.shape
    half_w = width // 2

    load_x = pltpu.make_async_copy(x_hbm, xv, load_sem.at[0])
    load_cot = pltpu.make_async_copy(cot_hbm, gsec, load_sem.at[1])
    load_x.start()
    load_cot.start()
    for row, ref in enumerate((in1, in2, in3, in4, in5, in6)):
        vec[row : row + 1, :] = ref[...].astype(F32).reshape(1, width)
    bias_own[0:2, :] = in_qv[...].astype(F32)
    bias_own[2:6, :] = in_hidden[...].astype(F32).reshape(4, TILE)

    def fetch_qkv(h, i):
        source = (wq_own, wq_oth)[h]
        return pltpu.make_async_copy(source.at[i], ring_b.at[i], b_sem.at[i])

    def fetch_out(h):
        return pltpu.make_async_copy((wo_own, wo_oth)[h], ring_a.at[h], a_sem.at[h])

    def fetch_in(h, f, slot):
        return pltpu.make_async_copy((wi_own, wi_oth)[h].at[:, span(f, TILE)], ring_b.at[slot], b_sem.at[slot])

    def fetch_down(h, f, slot):
        return pltpu.make_async_copy((wd_own, wd_oth)[h].at[span(f, TILE)], ring_a.at[slot], a_sem.at[slot])

    def weight_load(h, k):
        which, where = tile_place(k)
        source = ((wd_own, wi_own, wo_own, wq_own), (wd_oth, wi_oth, wo_oth, wq_oth))[h][which]
        return pltpu.make_async_copy(source.at[where], (own, oth)[h].at[k], w_sem.at[h, k])

    for k in (*range(18, 24), *range(8, 16), *range(0, 8), 16, 17):
        weight_load(0, k).start()

    greet([to_c, to_y, to_x] + to_z)

    cut = wi_own.shape[1] // 2
    deep = wd_own.shape[0] // 2
    arrays = [(wq_own.at[i], wq_oth.at[i]) for i in range(3)] + [(wo_own, wo_oth)]
    arrays += [(wi_own.at[:, j * cut : (j + 1) * cut], wi_oth.at[:, j * cut : (j + 1) * cut]) for j in range(2)]
    arrays += [(wd_own.at[j * deep : (j + 1) * deep], wd_oth.at[j * deep : (j + 1) * deep]) for j in range(2)]
    loads_of = [(18, 19), (20, 21), (22, 23), (16, 17), (8, 9, 10, 11), (12, 13, 14, 15), (0, 1, 2, 3), (4, 5, 6, 7)]
    count = len(arrays)

    def gather_message(n, kind):
        size = arrays[n][0].shape[0] // 2
        size_part = size // 8 - (8 if n >= 4 else 0)
        near_a, near_b = 2 * zb, 4 + 2 * x
        far_a, far_b = 2 * (1 - zb), 4 + 2 * (1 - x)
        one_a, one_b = 2 * zb + x, 4 + 2 * x + zb
        first, parts, peer = [
            (one_a, 1, to_y), (one_b, 1, to_y), (one_a, 1, to_x), (one_b, 1, to_zp),
            (near_a, 2, to_zp), (near_b, 2, to_x), (near_a, 2, to_c), (near_b, 2, to_c), (far_a, 2, to_c), (far_b, 2, to_c),
            (8, 0, to_y), (8, 0, to_c),
        ][kind]
        length_rows = parts * size_part if parts else size - 8 * size_part
        rows = pl.ds(pl.multiple_of(c * size + first * size_part, 8), length_rows)
        source = arrays[n][0 if kind in (0, 1, 10) else 1]
        return copy_to(source.at[rows], arrays[n][1].at[rows], g_send.at[n, kind], g_recv.at[n, kind], peer)

    def gather_stage(n, step):
        if step == 0:
            gather_message(n, 0).wait_recv()
            gather_message(n, 2).start()
            gather_message(n, 1).wait_recv()
            gather_message(n, 3).start()
        if step == 1:
            gather_message(n, 2).wait_recv()
            gather_message(n, 4).start()
            gather_message(n, 6).start()
            gather_message(n, 3).wait_recv()
            gather_message(n, 5).start()
            gather_message(n, 7).start()
        if step == 2:
            gather_message(n, 4).wait_recv()
            gather_message(n, 8).start()
            gather_message(n, 5).wait_recv()
            gather_message(n, 9).start()
            if n >= 4:
                gather_message(n, 10).wait_recv()
                gather_message(n, 11).start()
        if step == 3:
            kinds = range(12 if n >= 4 else 10)
            for kind in kinds:
                if kind >= 6 and kind != 10:
                    gather_message(n, kind).wait_recv()
            for k in loads_of[n]:
                weight_load(1, k).start()
            for kind in kinds:
                gather_message(n, kind).wait_send()

    def progress(slot):
        for step in range(4):
            if 0 <= slot - step < count:
                gather_stage(slot - step, step)

    send_bias = copy_to(bias_own, bias_oth, g_send.at[count, 0], g_recv.at[count, 0], to_y)
    send_bias.start()
    for n in (0, 1, 2, 3, 4, 5, -4, 6, -5, 7, -6, -7):
        for kind in (0, 1) if n >= 0 else (10,):
            gather_message(abs(n), kind).start()

    length = lengths[y]
    key_fill = jnp.where(lax.broadcasted_iota(jnp.int32, (1, seq), 1) < length, 0.0, NEG_FILL)
    low_lanes = lax.broadcasted_iota(jnp.int32, (1, 128), 1) < HEAD
    one, zero = jnp.ones((), BF), jnp.zeros((), BF)
    scale = HEAD ** (-0.5)
    pairs = half_w // 128

    def project(h):
        bias = (bias_own, bias_oth)[h]
        for i in range(3):
            for k in (18 + 2 * i, 19 + 2 * i):
                weight_load(h, k).wait()
            value = dot(xv[...], (own, oth)[h][18 + 2 * i : 20 + 2 * i].reshape(width, TILE), 1, 0)
            if i == 0:
                qkv[h, 0] = (value + bias[0:1, :]).astype(BF) * jnp.asarray(scale, BF)
            if i == 1:
                qkv[h, 1] = value.astype(BF)
            if i == 2:
                qkv[h, 2] = (value + bias[1:2, :]).astype(BF)

    def attend(h, p, e_ref):
        lanes = span(p, 128)
        q2, k2, v2 = qkv[h, 0, :, lanes], qkv[h, 1, :, lanes], qkv[h, 2, :, lanes]
        parts = []
        for head in range(2):
            mine = low_lanes if head == 0 else jnp.logical_not(low_lanes)
            scores = dot(jnp.where(mine, q2, zero), k2, 1, 1) + key_fill
            peak = jnp.max(scores, axis=-1, keepdims=True)
            e = jnp.exp(scores - peak).astype(BF)
            e_ref[2 * p + head] = e
            parts.append(dot(e, jnp.where(mine, v2, one), 1, 0))
        total = pltpu.roll(jnp.where(low_lanes, parts[1], parts[0]), HEAD, 1)
        inverse = 1.0 / total
        inv[h, :, lanes] = inverse
        ctx[:, span(h * pairs + p, 128)] = (jnp.where(low_lanes, parts[0], parts[1]) * inverse).astype(BF)

    def attend_half(h, slots):
        def body(p, _):
            attend(h, p, (u1, u2)[h])
            for at_pair, slot in slots:
                @pl.when(p == at_pair)
                def _():
                    progress(slot)
            return 0
        lax.fori_loop(0, pairs, body, 0)

    def e_copy(h, back):
        ref, buf = e_hbm.at[pl.ds(h * 8, 8)], (u1 if back else (u1, u2)[h])
        return pltpu.make_async_copy(ref, buf, e_sem.at[h]) if back else pltpu.make_async_copy(buf, ref, e_sem.at[h])

    def out_project(h):
        for d in range(2):
            weight_load(h, 16 + d).wait()
            term = dot(ctx[:, h * half_w : (h + 1) * half_w], (own, oth)[h][16 + d], 1, 0)
            lanes = slice(d * TILE, (d + 1) * TILE)
            acc[:, lanes] = term if h == 0 else acc[:, lanes] + term

    load_x.wait()
    project(0)
    attend_half(0, ((1, 0), (3, 1)))
    e_copy(0, False).start()
    out_project(0)
    for slot in (2, 3, 4, 5):
        progress(slot)
    send_bias.wait()
    project(1)
    attend_half(1, ((1, 6),))
    e_copy(1, False).start()
    out_project(1)

    def blocks(body):
        def run(b, _):
            body(span(b, ROWS_AT_ONCE), b)
            return 0
        lax.fori_loop(0, seq // ROWS_AT_ONCE, run, 0)

    def mean(v):
        return jnp.sum(v, axis=-1, keepdims=True) * (1.0 / width)

    small[...] = jnp.zeros_like(small)
    b_out, gain1, shift1 = vec[0:1, :], vec[1:2, :], vec[2:3, :]
    b_down, gain2, shift2 = vec[3:4, :], vec[4:5, :], vec[5:6, :]

    def norm_one(r, b):
        v = xv[r, :].astype(F32) + (acc[r, :] + b_out)
        center = v - mean(v)
        inverse = lax.rsqrt(mean(center * center) + EPSILON)
        hat = center * inverse
        xhat[r, :] = hat
        rs1[r, :] = jnp.broadcast_to(inverse, (ROWS_AT_ONCE, 128))
        nlow[r, :] = (hat * gain1 + shift1).astype(BF)
    blocks(norm_one)
    e_copy(0, False).wait()
    e_copy(1, False).wait()
    progress(7)

    def hidden_half(h, slots):
        bias, weights = (bias_own, bias_oth)[h], (own, oth)[h]
        for f in range(4):
            for k in (8 + 2 * f, 9 + 2 * f):
                weight_load(h, k).wait()
            hidden = dot(nlow[...], weights[8 + 2 * f : 10 + 2 * f].reshape(width, TILE), 1, 0) + bias[2 + f : 3 + f, :]
            cdf = 0.5 + 0.5 * lax.erf(hidden * 0.7071067811865476)
            u1[4 * h + f] = (hidden * cdf).astype(BF)
            u2[4 * h + f] = (cdf + hidden * (jnp.exp(hidden * hidden * -0.5) * 0.3989422804014327)).astype(BF)
            if f in slots:
                progress(slots[f])

    def down_half(h, tiles, clear=False):
        for f in tiles:
            for d in range(2):
                weight_load(h, 2 * f + d).wait()
                term = dot(u1[4 * h + f], (own, oth)[h][2 * f + d], 1, 0)
                lanes = slice(d * TILE, (d + 1) * TILE)
                acc[:, lanes] = term if clear and f == tiles[0] else acc[:, lanes] + term

    hidden_half(0, {})
    down_half(0, (0, 1), True)
    progress(8)
    down_half(0, (2, 3))
    hidden_half(1, {3: 9})
    down_half(1, (0, 1))
    progress(10)
    down_half(1, (2, 3))

    load_cot.wait()
    valid_limit = lengths[y]

    def norm_two(r, b):
        normed = xhat[r, :] * gain1 + shift1
        v = normed + (acc[r, :] + b_down)
        center = v - mean(v)
        inverse = lax.rsqrt(mean(center * center) + EPSILON)
        hat = center * inverse
        out_ref[r, :] = (hat * gain2 + shift2).astype(BF)
        position = b * ROWS_AT_ONCE + lax.broadcasted_iota(jnp.int32, (ROWS_AT_ONCE, 1), 0)
        g_out = jnp.where(position < valid_limit, gsec[r, :].astype(F32), 0.0)
        scaled = g_out * gain2
        g_two = inverse * (scaled - mean(scaled) - hat * mean(scaled * hat))
        low = g_two.astype(BF)
        acc[r, :] = g_two
        gsec[r, :] = low
        small[3:4, :] += jnp.sum(g_out * hat, axis=0, keepdims=True)
        small[4:5, :] += jnp.sum(g_out, axis=0, keepdims=True)
        small[5:6, :] += jnp.sum(low.astype(F32), axis=0, keepdims=True)
    blocks(norm_two)

    half, quarter, part = TILE // 2, TILE // 4, TILE // 16
    c_rows = span(c, half)
    cn_rows = span(1 - c, half)
    x_rows = pl.ds(pl.multiple_of(c * half + x * quarter, quarter), quarter)
    xn_rows = pl.ds(pl.multiple_of(c * half + (1 - x) * quarter, quarter), quarter)

    def z_rows(v):
        return pl.ds(pl.multiple_of(c * half + x * quarter + v * part, part), part)

    def message(k, kind):
        slot = k % RING
        if kind == 0: src, dst, peer = own.at[k, cn_rows], r1.at[slot, 0], to_c
        if kind == 1: src, dst, peer = oth.at[k, cn_rows], r1.at[slot, 1], to_c
        if kind == 2: src, dst, peer = oth.at[k, c_rows], ry.at[slot], to_y
        if kind == 3: src, dst, peer = own.at[k, xn_rows], rx.at[slot], to_x
        if 4 <= kind < 7: src, dst, peer = own.at[k, z_rows(z_of[kind - 4])], rz.at[slot, kind - 4], to_z[kind - 4]
        if 7 <= kind < 10: src, dst, peer = oth.at[k, z_rows(z)], oth.at[k, z_rows(z)], to_z[kind - 7]
        if kind == 10: src, dst, peer = oth.at[k, x_rows], oth.at[k, x_rows], to_x
        if kind == 11: src, dst, peer = oth.at[k, c_rows], oth.at[k, c_rows], to_c
        return copy_to(src, dst, send.at[slot, kind], recv.at[slot, kind], peer)

    def add_into(dst, src, n):
        def body(i, _):
            r = span(i, 64)
            dst[r, :] = dst[r, :] + src[r, :]
            return 0
        lax.fori_loop(0, n // 64, body, 0)

    def wait(k, kinds):
        for kind in kinds:
            message(k, kind).wait()

    def reduce_stage(k, s):
        slot = k % RING
        if s == 0:
            message(k, 0).start()
            message(k, 1).start()
        if s == 1:
            wait(k, (0, 1))
            add_into(oth.at[k, c_rows], r1.at[slot, 1], half)
            message(k, 2).start()
            add_into(own.at[k, c_rows], r1.at[slot, 0], half)
        if s == 2:
            wait(k, (2,))
            add_into(own.at[k, c_rows], ry.at[slot], half)
            message(k, 3).start()
        if s == 3:
            wait(k, (3,))
            add_into(own.at[k, x_rows], rx.at[slot], quarter)
            for kind in (4, 5, 6):
                message(k, kind).start()
        if s == 4:
            wait(k, (4, 5, 6))
            total = own[k, z_rows(z), :].astype(F32)
            for d in range(3):
                total = total + rz[slot, d].astype(F32)
            oth[k, z_rows(z), :] = total.astype(BF)
            for kind in (7, 8, 9):
                message(k, kind).start()
        if s == 5:
            wait(k, (7, 8, 9))
            message(k, 10).start()
        if s == 6:
            wait(k, (10,))
            message(k, 11).start()
        if s == 7:
            wait(k, (11,))

    def reduce_step(t):
        for s in range(8):
            @pl.when((t >= s) & (t - s < CHUNKS))
            def _():
                reduce_stage(t - s, s)

    def small_messages(i):
        if i == 0:
            return [copy_to(small, s0, small_send.at[0], small_recv.at[0], to_c)]
        if i == 1:
            return [
                copy_to(small.at[pl.ds(0, 8)], s1.at[pl.ds(0, 8)], small_send.at[1], small_recv.at[1], to_y),
                copy_to(small.at[pl.ds(16, 8)], s1.at[pl.ds(8, 8)], small_send.at[2], small_recv.at[2], to_y),
            ]
        got, peer = ((s2, to_x), (s3, to_zp), (s4, to_zq))[i - 2]
        return [copy_to(small.at[pl.ds(0, 16)], got, small_send.at[i + 1], small_recv.at[i + 1], peer)]

    def small_step(i):
        if i > 0:
            for m in small_messages(i - 1):
                m.wait()
            if i == 1:
                small[...] = small[...] + s0[...]
            else:
                small[0:16, :] = small[0:16, :] + (s1, s2, s3, s4)[i - 2][...]
        if i < 5:
            for m in small_messages(i):
                m.start()

    def fetch_ffn(t, start):
        for h in range(2):
            @pl.when((t >= 4 * h) & (t < 4 * h + 4))
            def _():
                b, a = fetch_in(h, t - 4 * h, t % 3), fetch_down(h, t - 4 * h, t % 2)
                if start:
                    b.start()
                    a.start()
                else:
                    b.wait()
                    a.wait()

    def down_tiles(k):
        g = gsec[:, span(k % 2, TILE)]
        own[k] = dot(u1[k // 2], g, 0, 0).astype(BF)
        oth[k] = dot(u1[4 + k // 2], g, 0, 0).astype(BF)

    def hidden_back(t):
        fetch_ffn(t, False)
        g_active = dot(gsec[...], ring_a[t % 2], 1, 1)
        g_hidden = (g_active * u2[t].astype(F32)).astype(BF)
        u2[t] = g_hidden
        total = jnp.sum(g_hidden.astype(F32), axis=0, keepdims=True)
        small[pl.ds(9 + 8 * (t // 4) + (t % 4) // 2, 1), span(t % 2, TILE)] = total
        acc[...] += dot(g_hidden, ring_b[t % 3], 1, 1)

    def in_tiles(k):
        j = k - 8
        a = nlow[:, span(j % 2, TILE)]
        own[k] = dot(a, u2[j // 2], 0, 0).astype(BF)
        oth[k] = dot(a, u2[4 + j // 2], 0, 0).astype(BF)

    def norm_one_back(r, b):
        g_normed, hat = acc[r, :], xhat[r, :]
        scaled = g_normed * gain1
        g_first = rs1[r, 0:1] * (scaled - mean(scaled) - hat * mean(scaled * hat))
        low = g_first.astype(BF)
        acc[r, :] = g_first
        gsec[r, :] = low
        small[0:1, :] += jnp.sum(g_normed * hat, axis=0, keepdims=True)
        small[1:2, :] += jnp.sum(g_normed, axis=0, keepdims=True)
        small[2:3, :] += jnp.sum(low.astype(F32), axis=0, keepdims=True)

    def attend_back(h, p):
        lanes = span(p, 128)
        wide = span(h * pairs + p, 128)
        q2, k2, v2 = qkv[h, 0, :, lanes], qkv[h, 1, :, lanes], qkv[h, 2, :, lanes]
        g = gctx[:, wide].astype(F32) * inv[h, :, lanes]
        low = g.astype(BF)
        less = pltpu.roll(-(g * ctx[:, wide].astype(F32)), HEAD, 1).astype(BF)
        g_q, g_k, g_v = [], [], []
        for head in range(2):
            mine = low_lanes if head == 0 else jnp.logical_not(low_lanes)
            e = u1[2 * p + head]
            g_scores = (dot(jnp.where(mine, low, less), jnp.where(mine, v2, one), 1, 1) * e.astype(F32)).astype(BF)
            g_q.append(dot(g_scores, k2, 1, 0))
            rows = slice(head * HEAD, head * HEAD + HEAD)
            g_k.append(dot(q2, g_scores, 0, 0)[rows])
            g_v.append(dot(low, e, 0, 0)[rows])
        qkv[h, 0, :, lanes] = (jnp.where(low_lanes, g_q[0], g_q[1]) * scale).astype(BF)
        qkv[h, 1, :, lanes] = jnp.concatenate(g_k, axis=0).T.astype(BF)
        qkv[h, 2, :, lanes] = jnp.concatenate(g_v, axis=0).T.astype(BF)

    fetch_ffn(0, True)

    def iteration(t, _):
        @pl.when(t < 8)
        def _():
            down_tiles(t)
        @pl.when((t >= 8) & (t < 16))
        def _():
            in_tiles(t)
        @pl.when((t >= 16) & (t < 18))
        def _():
            g = gsec[:, span(t - 16, TILE)]
            own[t] = dot(ctx[:, :half_w], g, 0, 0).astype(BF)
            oth[t] = dot(ctx[:, half_w:], g, 0, 0).astype(BF)
        @pl.when((t >= 18) & (t < 24))
        def _():
            j = t - 18
            a = xv[:, span(j % 2, TILE)]
            own[t] = dot(a, qkv[0, j // 2], 0, 0).astype(BF)
            oth[t] = dot(a, qkv[1, j // 2], 0, 0).astype(BF)
        reduce_step(t)
        @pl.when(t < 8)
        def _():
            @pl.when(t < 7)
            def _():
                fetch_ffn(t + 1, True)
            hidden_back(t)
        @pl.when(t == 8)
        def _():
            e_copy(0, True).start()
            fetch_out(0).start()
            fetch_out(1).start()
            blocks(norm_one_back)
        @pl.when(t == 9)
        def _():
            for h in range(2):
                fetch_out(h).wait()
                gctx[:, h * half_w : (h + 1) * half_w] = dot(gsec[...], ring_a[h], 1, 1).astype(BF)
            e_copy(0, True).wait()
        for first, h in ((10, 0), (13, 1)):
            @pl.when((t >= first) & (t < first + 2))
            def _():
                def body(p, _):
                    attend_back(h, 2 * (t - first) + p)
                    return 0
                lax.fori_loop(0, 2, body, 0)
            @pl.when(t == first + 1)
            def _():
                if h == 0:
                    e_copy(1, True).start()
                for i in (0, 2):
                    total = jnp.sum(qkv[h, i].astype(F32), axis=0, keepdims=True)
                    small[8 + 8 * h : 9 + 8 * h, (i // 2) * TILE : (i // 2 + 1) * TILE] = total
        @pl.when(t == 12)
        def _():
            e_copy(1, True).wait()
        for h in range(2):
            first = 15 + 2 * h
            @pl.when(t == first)
            def _():
                for i in range(3):
                    fetch_qkv(h, i).start()
            @pl.when(t == first + 1)
            def _():
                for i in range(3):
                    fetch_qkv(h, i).wait()
                    acc[...] += dot(qkv[h, i], ring_b[i], 1, 1)
        @pl.when(t == 19)
        def _():
            def last(r, b):
                gin_ref[r, :] = acc[r, :].astype(BF)
            blocks(last)
        for i in range(6):
            @pl.when(t == 16 + i)
            def _():
                small_step(i)
        return 0

    lax.fori_loop(0, CHUNKS + 7, iteration, 0)
    small_out[...] = small[0:16, :]


def layer(lengths, inputs, cotangent, wq, w_out, w_in, w_down, vectors):
    seq, width = inputs.shape
    half = TILE // 2
    vm, dma = pltpu.VMEM, pltpu.SemaphoreType.DMA
    anywhere, inside = pl.BlockSpec(memory_space=pl.ANY), pl.BlockSpec(memory_space=pltpu.VMEM)
    like = lambda a: jax.ShapeDtypeStruct(a.shape, a.dtype)
    tile_shape = (TILE, TILE)
    return pl.pallas_call(
        layer_kernel,
        out_shape=[
            pltpu.VMEM(inputs.shape, BF), pltpu.VMEM(inputs.shape, BF), pltpu.VMEM((CHUNKS,) + tile_shape, BF),
            pltpu.VMEM((16, width), F32),
            like(wq), like(w_out), like(w_in), like(w_down),
            jax.ShapeDtypeStruct((16,) + tile_shape, BF),
        ],
        in_specs=[pl.BlockSpec(memory_space=pltpu.SMEM)] + [anywhere] * 6 + [inside] * 8,
        out_specs=[inside] * 4 + [anywhere] * 5,
        scratch_shapes=[
            vm((seq, width), BF), vm((seq, width), BF), vm((seq, width), BF), vm((seq, width), BF), vm((seq, width), BF),
            vm((2, 3) + tile_shape, BF), vm((2,) + tile_shape, F32),
            vm((seq, width), F32), vm((seq, 128), F32), vm((seq, width), F32),
            vm((8,) + tile_shape, BF), vm((8,) + tile_shape, BF),
            vm((CHUNKS,) + tile_shape, BF),
            vm((RING, 2, half, TILE), BF), vm((RING, half, TILE), BF),
            vm((RING, half // 2, TILE), BF), vm((RING, 3, half // 8, TILE), BF),
            vm((2, TILE, width), BF), vm((3, width, TILE), BF),
            vm((8, width), F32), vm((8, TILE), F32), vm((8, TILE), F32), vm((24, width), F32), vm((24, width), F32),
            vm((16, width), F32), vm((16, width), F32), vm((16, width), F32), vm((16, width), F32),
            dma((2,)), dma((2, CHUNKS)), dma((2,)), dma((3,)), dma((2,)),
            dma((9, 12)), dma((9, 12)), dma((RING, MESSAGES)), dma((RING, MESSAGES)), dma((6,)), dma((6,)),
        ],
        compiler_params=pltpu.CompilerParams(
            collective_id=1, has_side_effects=True, vmem_limit_bytes=47 << 20
        ),
    )(lengths, inputs, cotangent, wq, w_out, w_in, w_down, *vectors)


def widen_kernel(
    tiles, out_in, gin_in, sums, down, within, out, three, out_out, gin_out,
    b_qv, b_out, gain1, shift1, b_in, b_down, gain2, shift2, wide, out_sem, pass_sem,
):
    leave = [pltpu.make_async_copy(ref, to, pass_sem.at[i]) for i, (ref, to) in enumerate(((out_in, out_out), (gin_in, gin_out)))]
    for copy in leave:
        copy.start()
    width, half = sums.shape[1], b_qv.shape[1]
    for ref, row in ((gain1, 0), (shift1, 1), (b_out, 2), (gain2, 3), (shift2, 4), (b_down, 5)):
        ref[...] = sums[row, :]
    for i in range(2):
        b_qv[i : i + 1, :] = sums[8:9, i * half : (i + 1) * half]
        b_in[i * width : (i + 1) * width] = sums[9 + i, :]

    def store(k):
        which, where = tile_place(k)
        return pltpu.make_async_copy(wide.at[k % RING], (down, within, out, three)[which].at[where], out_sem.at[k % RING])

    stores = [store(k) for k in range(CHUNKS)]
    for k in range(CHUNKS):
        if k >= RING:
            stores[k - RING].wait()
        def body(i, _):
            r = span(i, 32)
            wide[k % RING, r, :] = tiles[k, r, :].astype(F32)
            return 0
        lax.fori_loop(0, TILE // 32, body, 0)
        stores[k].start()
    for copy in stores[CHUNKS - RING :] + leave:
        copy.wait()


def widen(tiles, output, grad_inputs, sums, half_hidden, width, half_width):
    tile, vm, dma = (TILE, TILE), pltpu.VMEM, pltpu.SemaphoreType.DMA
    anywhere, inside = pl.BlockSpec(memory_space=pl.ANY), pl.BlockSpec(memory_space=pltpu.VMEM)
    wide = lambda *shape: jax.ShapeDtypeStruct(shape, F32)
    return pl.pallas_call(
        widen_kernel,
        out_shape=[
            wide(half_hidden, width), wide(width, half_hidden), wide(half_width, width), wide(3, width, half_width),
            jax.ShapeDtypeStruct(output.shape, output.dtype), jax.ShapeDtypeStruct(output.shape, output.dtype),
            wide(2, half_width), wide(width), wide(width), wide(width), wide(half_hidden), wide(width), wide(width), wide(width),
        ],
        in_specs=[inside] * 4,
        out_specs=[anywhere] * 6 + [inside] * 8,
        scratch_shapes=[
            vm((RING,) + tile, F32), dma((RING,)), dma((2,)),
        ],
        compiler_params=pltpu.CompilerParams(vmem_limit_bytes=16 << 20),
    )(tiles, output, grad_inputs, sums)


def split_by_sequence(
    inputs, lengths, w_qkv, b_qv, w_out, b_out, gain_one, shift_one, w_in, b_in, w_down, b_down, gain_two, shift_two,
    cotangent,
):
    rows, width = inputs.shape
    half_width, half_hidden = w_qkv.shape[2], w_in.shape[1]
    wq = w_qkv.transpose(1, 0, 2)
    vectors = (b_out, gain_one, shift_one, b_down, gain_two, shift_two, b_qv, b_in)
    made = layer(lengths, inputs, cotangent, wq, w_out, w_in, w_down, vectors)
    output, grad_inputs, tiles, sums = made[:4]
    (
        g_w_down, g_w_in, g_w_out, g_w_qkv, output, grad_inputs,
        g_b_qv, g_b_out, g_gain_one, g_shift_one, g_b_in, g_b_down, g_gain_two, g_shift_two,
    ) = widen(tiles, output, grad_inputs, sums, half_hidden, width, half_width)
    return (
        output, grad_inputs, g_w_qkv.transpose(1, 0, 2), g_b_qv, g_w_out, g_b_out, g_gain_one, g_shift_one,
        g_w_in, g_b_in, g_w_down, g_b_down, g_gain_two, g_shift_two,
    )


def solution(mesh):
    small_mesh = mesh.shape["tensor"] == 2 and mesh.shape["dp"] == 2 * N_X * N_Z
    step = split_by_sequence if small_mesh else general
    in_specs = (
        P(("dp", "tensor"), None),
        P("dp"),
        P(None, None, "tensor"),
        P(None, "tensor"),
        P("tensor", None),
        P(),
        P(),
        P(),
        P(None, "tensor"),
        P("tensor"),
        P("tensor", None),
        P(),
        P(),
        P(),
        P(("dp", "tensor"), None),
    )
    out_specs = (
        P(("dp", "tensor"), None),
        P(("dp", "tensor"), None),
        P(None, None, "tensor"),
        P(None, "tensor"),
        P("tensor", None),
        P(),
        P(),
        P(),
        P(None, "tensor"),
        P("tensor"),
        P("tensor", None),
        P(),
        P(),
        P(),
    )
    return jax.shard_map(step, mesh=mesh, in_specs=in_specs, out_specs=out_specs, check_vma=False)
```

```python
import jax
import jax.numpy as jnp
from jax import lax
from jax.experimental import pallas as pl
from jax.experimental.pallas import tpu as pltpu
from jax.sharding import PartitionSpec as P

MESH = pl.DeviceIdType.MESH
N_Z, N_X = 4, 2
TILE = 512
MESSAGES = 12
VMEM_BYTES = 63 << 20

HEAD = 64
SEQ = 512
SEQ_DEV = 2


EPSILON = 1e-12
NEG_FILL = -1000000000.0


def gelu_exact(values):
    return jax.nn.gelu(values, approximate=False)


def norm_forward(values, gain_vec, shift_vec):
    center = values - jnp.mean(values, axis=-1, keepdims=True)
    spread = jnp.mean(center * center, axis=-1, keepdims=True)
    inverse = lax.rsqrt(spread + EPSILON)
    scaled = center * inverse
    return (scaled * gain_vec + shift_vec, scaled, inverse)


def norm_backward(grad_out, scaled, inverse, gain_vec):
    grad_scaled = grad_out * gain_vec
    mean_one = jnp.mean(grad_scaled, axis=-1, keepdims=True)
    mean_two = jnp.mean(grad_scaled * scaled, axis=-1, keepdims=True)
    grad_in = inverse * (grad_scaled - mean_one - scaled * mean_two)
    return (grad_in, jnp.sum(grad_out * scaled, axis=0), jnp.sum(grad_out, axis=0))


def masked_scores(queries, key_rows, length):
    score_scale = HEAD ** (-0.5)
    scores = (
        jnp.einsum("qhe,khe->hqk", queries, key_rows, preferred_element_type=jnp.float32)
        * score_scale
    )
    key_valid = (jnp.arange(SEQ) < length)[None, None, :]
    return jnp.where(key_valid, scores, NEG_FILL)


def attend_forward(element):
    queries, key_rows, value_rows, length = element
    scores = masked_scores(queries, key_rows, length)
    peak_score = jnp.max(scores, axis=-1, keepdims=True)
    shifted_exp = jnp.exp(scores - peak_score)
    denominator = jnp.sum(shifted_exp, axis=-1, keepdims=True)
    probability = (shifted_exp / denominator).astype(jnp.bfloat16)
    context = jnp.einsum(
        "hqk,khe->qhe", probability, value_rows, preferred_element_type=jnp.float32
    )
    return (context.astype(jnp.bfloat16), (peak_score + jnp.log(denominator))[..., 0])


def attend_backward(element):
    queries, key_rows, value_rows, length, log_total, grad_context = element
    score_scale = HEAD ** (-0.5)
    scores = masked_scores(queries, key_rows, length)
    probability = jnp.exp(scores - log_total[..., None])
    grad_prob = jnp.einsum(
        "qhe,khe->hqk", grad_context, value_rows, preferred_element_type=jnp.float32
    )
    grad_value = jnp.einsum(
        "hqk,qhe->khe",
        probability.astype(jnp.bfloat16),
        grad_context,
        preferred_element_type=jnp.float32,
    )
    grad_scores = probability * (
        grad_prob - jnp.sum(probability * grad_prob, axis=-1, keepdims=True)
    )
    grad_scores = grad_scores.astype(jnp.bfloat16)
    grad_query = (
        jnp.einsum("hqk,khe->qhe", grad_scores, key_rows, preferred_element_type=jnp.float32)
        * score_scale
    )
    grad_key = (
        jnp.einsum("hqk,qhe->khe", grad_scores, queries, preferred_element_type=jnp.float32)
        * score_scale
    )
    return jnp.stack([grad_query, grad_key, grad_value], axis=1).astype(jnp.bfloat16)


def row_mask(lengths, rows_dev):
    places = lax.axis_index("tensor") * rows_dev + jnp.arange(rows_dev)
    sequence_of = places // SEQ
    offset = places % SEQ
    matches = sequence_of[:, None] == jnp.arange(lengths.shape[0])[None, :]
    limit_rows = jnp.sum(jnp.where(matches, lengths[None, :], 0), axis=1)
    return (offset < limit_rows).astype(jnp.float32)[:, None]


def forward_pass(inputs, lengths, weights):
    (
        w_qkv,
        b_qv,
        w_out,
        b_out,
        gain_one,
        shift_one,
        w_in,
        b_in,
        w_down,
        b_down,
        gain_two,
        shift_two,
    ) = weights
    width_dev = w_qkv.shape[2]
    gathered = lax.all_gather(inputs, "tensor", axis=0, tiled=True)
    bias_three = jnp.stack([b_qv[0], jnp.zeros_like(b_qv[0]), b_qv[1]]).astype(jnp.float32)
    projected = (
        jnp.einsum("td,dcf->tcf", gathered, w_qkv, preferred_element_type=jnp.float32) + bias_three
    ).astype(jnp.bfloat16)
    shaped = projected.reshape(SEQ_DEV, SEQ, 3, width_dev // HEAD, HEAD)
    context, log_total = lax.map(
        attend_forward, (shaped[:, :, 0], shaped[:, :, 1], shaped[:, :, 2], lengths)
    )
    context = context.reshape(SEQ_DEV * SEQ, width_dev)
    segment = context
    branch = lax.psum_scatter(
        jnp.dot(segment, w_out, preferred_element_type=jnp.float32).astype(jnp.bfloat16),
        "tensor",
        scatter_dimension=0,
        tiled=True,
    ).astype(jnp.float32) + b_out.astype(jnp.float32)
    normed, scaled_one, inverse_one = norm_forward(
        inputs.astype(jnp.float32) + branch,
        gain_one.astype(jnp.float32),
        shift_one.astype(jnp.float32),
    )
    normed_all = lax.all_gather(normed.astype(jnp.bfloat16), "tensor", axis=0, tiled=True)
    hidden = jnp.dot(normed_all, w_in, preferred_element_type=jnp.float32) + b_in.astype(
        jnp.float32
    )
    active = gelu_exact(hidden).astype(jnp.bfloat16)
    segment = active
    second = lax.psum_scatter(
        jnp.dot(segment, w_down, preferred_element_type=jnp.float32).astype(jnp.bfloat16),
        "tensor",
        scatter_dimension=0,
        tiled=True,
    ).astype(jnp.float32) + b_down.astype(jnp.float32)
    output, scaled_two, inverse_two = norm_forward(
        normed + second, gain_two.astype(jnp.float32), shift_two.astype(jnp.float32)
    )
    return (
        gathered,
        projected,
        context,
        log_total,
        scaled_one,
        inverse_one,
        normed_all,
        hidden,
        active,
        scaled_two,
        inverse_two,
        output,
    )


def general(
    inputs,
    lengths,
    w_qkv,
    b_qv,
    w_out,
    b_out,
    gain_one,
    shift_one,
    w_in,
    b_in,
    w_down,
    b_down,
    gain_two,
    shift_two,
    cotangent,
):
    weights = (
        w_qkv,
        b_qv,
        w_out,
        b_out,
        gain_one,
        shift_one,
        w_in,
        b_in,
        w_down,
        b_down,
        gain_two,
        shift_two,
    )
    first_pass = forward_pass(inputs, lengths, weights)
    output = first_pass[11].astype(jnp.bfloat16)
    recorded = forward_pass(inputs, lengths, weights)
    (
        gathered,
        projected,
        context,
        log_total,
        scaled_one,
        inverse_one,
        normed_all,
        hidden,
        active,
        scaled_two,
        inverse_two,
        _,
    ) = recorded
    rows_dev = inputs.shape[0]
    width_dev = w_qkv.shape[2]
    grad_out = cotangent.astype(jnp.float32) * row_mask(lengths, rows_dev)
    grad_two, grad_gain_two, grad_shift_two = norm_backward(
        grad_out, scaled_two, inverse_two, gain_two.astype(jnp.float32)
    )
    grad_second = grad_two.astype(jnp.bfloat16)
    grad_b_down = jnp.sum(grad_second.astype(jnp.float32), axis=0)
    second_all = lax.all_gather(grad_second, "tensor", axis=0, tiled=True)
    grad_w_down = jnp.einsum("tf,td->fd", active, second_all, preferred_element_type=jnp.float32)
    grad_active = jnp.einsum("td,fd->tf", second_all, w_down, preferred_element_type=jnp.float32)
    _, gelu_pull = jax.vjp(gelu_exact, hidden)
    grad_hidden = gelu_pull(grad_active)[0].astype(jnp.bfloat16)
    grad_b_in = jnp.sum(grad_hidden.astype(jnp.float32), axis=0)
    grad_w_in = jnp.einsum("td,tf->df", normed_all, grad_hidden, preferred_element_type=jnp.float32)
    segment = grad_hidden
    grad_normed = grad_two + lax.psum_scatter(
        jnp.einsum("tf,df->td", segment, w_in, preferred_element_type=jnp.float32).astype(
            jnp.bfloat16
        ),
        "tensor",
        scatter_dimension=0,
        tiled=True,
    ).astype(jnp.float32)
    grad_first, grad_gain_one, grad_shift_one = norm_backward(
        grad_normed, scaled_one, inverse_one, gain_one.astype(jnp.float32)
    )
    grad_branch = grad_first.astype(jnp.bfloat16)
    grad_b_out = jnp.sum(grad_branch.astype(jnp.float32), axis=0)
    branch_all = lax.all_gather(grad_branch, "tensor", axis=0, tiled=True)
    grad_w_out = jnp.einsum("tf,td->fd", context, branch_all, preferred_element_type=jnp.float32)
    grad_context = jnp.einsum(
        "td,fd->tf", branch_all, w_out, preferred_element_type=jnp.float32
    ).astype(jnp.bfloat16)
    heads_dev = width_dev // HEAD
    shaped = projected.reshape(SEQ_DEV, SEQ, 3, heads_dev, HEAD)
    grad_shaped = grad_context.reshape(SEQ_DEV, SEQ, heads_dev, HEAD)
    grad_proj = lax.map(
        attend_backward,
        (shaped[:, :, 0], shaped[:, :, 1], shaped[:, :, 2], lengths, log_total, grad_shaped),
    )
    grad_proj = grad_proj.reshape(SEQ_DEV * SEQ, 3, width_dev)
    grad_w_qkv = jnp.einsum("td,tcf->dcf", gathered, grad_proj, preferred_element_type=jnp.float32)
    grad_b_qv = jnp.sum(grad_proj[:, 0::2].astype(jnp.float32), axis=0)
    segment = grad_proj
    grad_inputs = (
        grad_first
        + lax.psum_scatter(
            jnp.einsum("tcf,dcf->td", segment, w_qkv, preferred_element_type=jnp.float32).astype(
                jnp.bfloat16
            ),
            "tensor",
            scatter_dimension=0,
            tiled=True,
        ).astype(jnp.float32)
    ).astype(jnp.bfloat16)
    small_terms = jnp.stack(
        [grad_gain_one, grad_shift_one, grad_b_out, grad_gain_two, grad_shift_two, grad_b_down]
    )
    grad_w_qkv, grad_b_qv, grad_w_out, grad_w_in, grad_b_in, grad_w_down, small_terms = (
        lax.psum(grad_w_qkv.astype(jnp.bfloat16), "dp").astype(jnp.float32),
        lax.psum(grad_b_qv.astype(jnp.bfloat16), "dp").astype(jnp.float32),
        lax.psum(grad_w_out.astype(jnp.bfloat16), "dp").astype(jnp.float32),
        lax.psum(grad_w_in.astype(jnp.bfloat16), "dp").astype(jnp.float32),
        lax.psum(grad_b_in.astype(jnp.bfloat16), "dp").astype(jnp.float32),
        lax.psum(grad_w_down.astype(jnp.bfloat16), "dp").astype(jnp.float32),
        lax.psum(small_terms.astype(jnp.bfloat16), "dp").astype(jnp.float32),
    )
    small_sums = lax.psum(small_terms, "tensor")
    return (
        output,
        grad_inputs,
        grad_w_qkv,
        grad_b_qv,
        grad_w_out,
        small_sums[2],
        small_sums[0],
        small_sums[1],
        grad_w_in,
        grad_b_in,
        grad_w_down,
        small_sums[5],
        small_sums[3],
        small_sums[4],
    )


def place():
    dp = lax.axis_index("dp")
    return dp // (2 * N_X), (dp // 2) % N_X, dp % 2, lax.axis_index("tensor")


def at(z, x, c, y):
    return ((z * N_X + x) * 2 + c, y)


def greet(peers):
    barrier = pltpu.get_barrier_semaphore()
    for peer in peers:
        pl.semaphore_signal(barrier, inc=1, device_id=peer, device_id_type=MESH)
    pl.semaphore_wait(barrier, len(peers))


def copy_to(src, dst, send_sem, recv_sem, peer):
    return pltpu.make_async_remote_copy(
        src_ref=src, dst_ref=dst, send_sem=send_sem, recv_sem=recv_sem,
        device_id=peer, device_id_type=MESH,
    )


CHUNKS = 24
RING = 4
BF, F32 = jnp.bfloat16, jnp.float32
ROWS_AT_ONCE = 128


def dot(a, b, ca, cb):
    return lax.dot_general(a, b, (((ca,), (cb,)), ((), ())), preferred_element_type=F32)


def span(index, size):
    return pl.ds(pl.multiple_of(index * size, size), size)


def tile_place(k):
    if k < 8:
        return 0, (slice(k // 2 * TILE, (k // 2 + 1) * TILE), slice(k % 2 * TILE, (k % 2 + 1) * TILE))
    if k < 16:
        k -= 8
        return 1, (slice(k % 2 * TILE, (k % 2 + 1) * TILE), slice(k // 2 * TILE, (k // 2 + 1) * TILE))
    if k < 18:
        k -= 16
        return 2, (slice(0, TILE), slice(k * TILE, (k + 1) * TILE))
    k -= 18
    return 3, (k // 2, slice(k % 2 * TILE, (k % 2 + 1) * TILE), slice(0, TILE))


def layer_kernel(
    lengths, x_hbm, cot_hbm, wq_own, wo_own, wi_own, wd_own, in1, in2, in3, in4, in5, in6, in_qv, in_hidden,
    out_ref, gin_ref, oth, small_out, wq_oth, wo_oth, wi_oth, wd_oth, e_hbm,
    xv, nlow, gsec, gctx, ctx, qkv, inv, xhat, rs1, acc, u1, u2, own, r1, ry, rx, rz,
    ring_a, ring_b, vec, bias_own, bias_oth, small, s0, s1, s2, s3, s4,
    load_sem, w_sem, a_sem, b_sem, e_sem, g_send, g_recv, send, recv, small_send, small_recv,
):
    z, x, c, y = place()
    zb = z % 2
    z_of = [(z + d) % N_Z for d in (1, 2, 3)]
    to_c, to_y, to_x = at(z, x, 1 - c, y), at(z, x, c, 1 - y), at(z, 1 - x, c, y)
    to_z = [at(v, x, c, y) for v in z_of]
    to_zp, to_zq = at(z + 1 - 2 * zb, x, c, y), at((z + 2) % N_Z, x, c, y)
    seq, width = xv.shape
    half_w = width // 2

    load_x = pltpu.make_async_copy(x_hbm, xv, load_sem.at[0])
    load_cot = pltpu.make_async_copy(cot_hbm, gsec, load_sem.at[1])
    load_x.start()
    load_cot.start()
    for row, ref in enumerate((in1, in2, in3, in4, in5, in6)):
        vec[row : row + 1, :] = ref[...].astype(F32).reshape(1, width)
    bias_own[0:2, :] = in_qv[...].astype(F32)
    bias_own[2:6, :] = in_hidden[...].astype(F32).reshape(4, TILE)

    def fetch_qkv(h, i):
        source = (wq_own, wq_oth)[h]
        return pltpu.make_async_copy(source.at[i], ring_b.at[i], b_sem.at[i])

    def fetch_out(h):
        return pltpu.make_async_copy((wo_own, wo_oth)[h], ring_a.at[h], a_sem.at[h])

    def fetch_in(h, f, slot):
        return pltpu.make_async_copy((wi_own, wi_oth)[h].at[:, span(f, TILE)], ring_b.at[slot], b_sem.at[slot])

    def fetch_down(h, f, slot):
        return pltpu.make_async_copy((wd_own, wd_oth)[h].at[span(f, TILE)], ring_a.at[slot], a_sem.at[slot])

    def weight_load(h, k):
        which, where = tile_place(k)
        source = ((wd_own, wi_own, wo_own, wq_own), (wd_oth, wi_oth, wo_oth, wq_oth))[h][which]
        return pltpu.make_async_copy(source.at[where], (own, oth)[h].at[k], w_sem.at[h, k])

    for k in (*range(18, 24), *range(8, 16), *range(0, 8), 16, 17):
        weight_load(0, k).start()

    greet([to_c, to_y, to_x] + to_z)

    cut = wi_own.shape[1] // 2
    deep = wd_own.shape[0] // 2
    arrays = [(wq_own.at[i], wq_oth.at[i]) for i in range(3)] + [(wo_own, wo_oth)]
    arrays += [(wi_own.at[:, j * cut : (j + 1) * cut], wi_oth.at[:, j * cut : (j + 1) * cut]) for j in range(2)]
    arrays += [(wd_own.at[j * deep : (j + 1) * deep], wd_oth.at[j * deep : (j + 1) * deep]) for j in range(2)]
    loads_of = [(18, 19), (20, 21), (22, 23), (16, 17), (8, 9, 10, 11), (12, 13, 14, 15), (0, 1, 2, 3), (4, 5, 6, 7)]
    count = len(arrays)

    def gather_message(n, kind):
        size = arrays[n][0].shape[0] // 2
        size_part = size // 8 - (8 if n >= 4 else 0)
        near_a, near_b = 2 * zb, 4 + 2 * x
        far_a, far_b = 2 * (1 - zb), 4 + 2 * (1 - x)
        one_a, one_b = 2 * zb + x, 4 + 2 * x + zb
        first, parts, peer = [
            (one_a, 1, to_y), (one_b, 1, to_y), (one_a, 1, to_x), (one_b, 1, to_zp),
            (near_a, 2, to_zp), (near_b, 2, to_x), (near_a, 2, to_c), (near_b, 2, to_c), (far_a, 2, to_c), (far_b, 2, to_c),
            (8, 0, to_y), (8, 0, to_c),
        ][kind]
        length_rows = parts * size_part if parts else size - 8 * size_part
        rows = pl.ds(pl.multiple_of(c * size + first * size_part, 8), length_rows)
        source = arrays[n][0 if kind in (0, 1, 10) else 1]
        return copy_to(source.at[rows], arrays[n][1].at[rows], g_send.at[n, kind], g_recv.at[n, kind], peer)

    def gather_stage(n, step):
        if step == 0:
            gather_message(n, 0).wait_recv()
            gather_message(n, 2).start()
            gather_message(n, 1).wait_recv()
            gather_message(n, 3).start()
        if step == 1:
            gather_message(n, 2).wait_recv()
            gather_message(n, 4).start()
            gather_message(n, 6).start()
            gather_message(n, 3).wait_recv()
            gather_message(n, 5).start()
            gather_message(n, 7).start()
        if step == 2:
            gather_message(n, 4).wait_recv()
            gather_message(n, 8).start()
            gather_message(n, 5).wait_recv()
            gather_message(n, 9).start()
            if n >= 4:
                gather_message(n, 10).wait_recv()
                gather_message(n, 11).start()
        if step == 3:
            kinds = range(12 if n >= 4 else 10)
            for kind in kinds:
                if kind >= 6 and kind != 10:
                    gather_message(n, kind).wait_recv()
            for k in loads_of[n]:
                weight_load(1, k).start()
            for kind in kinds:
                gather_message(n, kind).wait_send()

    def progress(slot):
        for step in range(4):
            if 0 <= slot - step < count:
                gather_stage(slot - step, step)

    send_bias = copy_to(bias_own, bias_oth, g_send.at[count, 0], g_recv.at[count, 0], to_y)
    send_bias.start()
    for n in (0, 1, 2, 3, 4, 5, -4, 6, -5, 7, -6, -7):
        for kind in (0, 1) if n >= 0 else (10,):
            gather_message(abs(n), kind).start()

    length = lengths[y]
    key_fill = jnp.where(lax.broadcasted_iota(jnp.int32, (1, seq), 1) < length, 0.0, NEG_FILL)
    low_lanes = lax.broadcasted_iota(jnp.int32, (1, 128), 1) < HEAD
    one, zero = jnp.ones((), BF), jnp.zeros((), BF)
    scale = HEAD ** (-0.5)
    pairs = half_w // 128

    def project(h):
        bias = (bias_own, bias_oth)[h]
        for i in range(3):
            for k in (18 + 2 * i, 19 + 2 * i):
                weight_load(h, k).wait()
            value = dot(xv[...], (own, oth)[h][18 + 2 * i : 20 + 2 * i].reshape(width, TILE), 1, 0)
            if i == 0:
                qkv[h, 0] = (value + bias[0:1, :]).astype(BF) * jnp.asarray(scale, BF)
            if i == 1:
                qkv[h, 1] = value.astype(BF)
            if i == 2:
                qkv[h, 2] = (value + bias[1:2, :]).astype(BF)

    def attend(h, p, e_ref):
        lanes = span(p, 128)
        q2, k2, v2 = qkv[h, 0, :, lanes], qkv[h, 1, :, lanes], qkv[h, 2, :, lanes]
        parts = []
        for head in range(2):
            mine = low_lanes if head == 0 else jnp.logical_not(low_lanes)
            scores = dot(jnp.where(mine, q2, zero), k2, 1, 1) + key_fill
            peak = jnp.max(scores, axis=-1, keepdims=True)
            e = jnp.exp(scores - peak).astype(BF)
            e_ref[2 * p + head] = e
            parts.append(dot(e, jnp.where(mine, v2, one), 1, 0))
        total = pltpu.roll(jnp.where(low_lanes, parts[1], parts[0]), HEAD, 1)
        inverse = 1.0 / total
        inv[h, :, lanes] = inverse
        ctx[:, span(h * pairs + p, 128)] = (jnp.where(low_lanes, parts[0], parts[1]) * inverse).astype(BF)

    def attend_half(h, slots):
        def body(p, _):
            attend(h, p, (u1, u2)[h])
            for at_pair, slot in slots:
                @pl.when(p == at_pair)
                def _():
                    progress(slot)
            return 0
        lax.fori_loop(0, pairs, body, 0)

    def e_copy(h, back):
        ref, buf = e_hbm.at[pl.ds(h * 8, 8)], (u1 if back else (u1, u2)[h])
        return pltpu.make_async_copy(ref, buf, e_sem.at[h]) if back else pltpu.make_async_copy(buf, ref, e_sem.at[h])

    def out_project(h):
        for d in range(2):
            weight_load(h, 16 + d).wait()
            term = dot(ctx[:, h * half_w : (h + 1) * half_w], (own, oth)[h][16 + d], 1, 0)
            lanes = slice(d * TILE, (d + 1) * TILE)
            acc[:, lanes] = term if h == 0 else acc[:, lanes] + term

    load_x.wait()
    project(0)
    attend_half(0, ((1, 0), (3, 1)))
    e_copy(0, False).start()
    out_project(0)
    for slot in (2, 3, 4, 5):
        progress(slot)
    send_bias.wait()
    project(1)
    attend_half(1, ((1, 6),))
    e_copy(1, False).start()
    out_project(1)

    def blocks(body):
        def run(b, _):
            body(span(b, ROWS_AT_ONCE), b)
            return 0
        lax.fori_loop(0, seq // ROWS_AT_ONCE, run, 0)

    def mean(v):
        return jnp.sum(v, axis=-1, keepdims=True) * (1.0 / width)

    small[...] = jnp.zeros_like(small)
    b_out, gain1, shift1 = vec[0:1, :], vec[1:2, :], vec[2:3, :]
    b_down, gain2, shift2 = vec[3:4, :], vec[4:5, :], vec[5:6, :]

    def norm_one(r, b):
        v = xv[r, :].astype(F32) + (acc[r, :] + b_out)
        center = v - mean(v)
        inverse = lax.rsqrt(mean(center * center) + EPSILON)
        hat = center * inverse
        xhat[r, :] = hat
        rs1[r, :] = jnp.broadcast_to(inverse, (ROWS_AT_ONCE, 128))
        nlow[r, :] = (hat * gain1 + shift1).astype(BF)
    blocks(norm_one)
    e_copy(0, False).wait()
    e_copy(1, False).wait()
    progress(7)

    def hidden_half(h, slots):
        bias, weights = (bias_own, bias_oth)[h], (own, oth)[h]
        for f in range(4):
            for k in (8 + 2 * f, 9 + 2 * f):
                weight_load(h, k).wait()
            hidden = dot(nlow[...], weights[8 + 2 * f : 10 + 2 * f].reshape(width, TILE), 1, 0) + bias[2 + f : 3 + f, :]
            cdf = 0.5 + 0.5 * lax.erf(hidden * 0.7071067811865476)
            u1[4 * h + f] = (hidden * cdf).astype(BF)
            u2[4 * h + f] = (cdf + hidden * (jnp.exp(hidden * hidden * -0.5) * 0.3989422804014327)).astype(BF)
            if f in slots:
                progress(slots[f])

    def down_half(h, tiles, clear=False):
        for f in tiles:
            for d in range(2):
                weight_load(h, 2 * f + d).wait()
                term = dot(u1[4 * h + f], (own, oth)[h][2 * f + d], 1, 0)
                lanes = slice(d * TILE, (d + 1) * TILE)
                acc[:, lanes] = term if clear and f == tiles[0] else acc[:, lanes] + term

    hidden_half(0, {})
    down_half(0, (0, 1), True)
    progress(8)
    down_half(0, (2, 3))
    hidden_half(1, {3: 9})
    down_half(1, (0, 1))
    progress(10)
    down_half(1, (2, 3))

    load_cot.wait()
    valid_limit = lengths[y]

    def norm_two(r, b):
        normed = xhat[r, :] * gain1 + shift1
        v = normed + (acc[r, :] + b_down)
        center = v - mean(v)
        inverse = lax.rsqrt(mean(center * center) + EPSILON)
        hat = center * inverse
        out_ref[r, :] = (hat * gain2 + shift2).astype(BF)
        position = b * ROWS_AT_ONCE + lax.broadcasted_iota(jnp.int32, (ROWS_AT_ONCE, 1), 0)
        g_out = jnp.where(position < valid_limit, gsec[r, :].astype(F32), 0.0)
        scaled = g_out * gain2
        g_two = inverse * (scaled - mean(scaled) - hat * mean(scaled * hat))
        low = g_two.astype(BF)
        acc[r, :] = g_two
        gsec[r, :] = low
        small[3:4, :] += jnp.sum(g_out * hat, axis=0, keepdims=True)
        small[4:5, :] += jnp.sum(g_out, axis=0, keepdims=True)
        small[5:6, :] += jnp.sum(low.astype(F32), axis=0, keepdims=True)
    blocks(norm_two)

    half, quarter, part = TILE // 2, TILE // 4, TILE // 16
    c_rows = span(c, half)
    cn_rows = span(1 - c, half)
    x_rows = pl.ds(pl.multiple_of(c * half + x * quarter, quarter), quarter)
    xn_rows = pl.ds(pl.multiple_of(c * half + (1 - x) * quarter, quarter), quarter)

    def z_rows(v):
        return pl.ds(pl.multiple_of(c * half + x * quarter + v * part, part), part)

    def message(k, kind):
        slot = k % RING
        if kind == 0: src, dst, peer = own.at[k, cn_rows], r1.at[slot, 0], to_c
        if kind == 1: src, dst, peer = oth.at[k, cn_rows], r1.at[slot, 1], to_c
        if kind == 2: src, dst, peer = oth.at[k, c_rows], ry.at[slot], to_y
        if kind == 3: src, dst, peer = own.at[k, xn_rows], rx.at[slot], to_x
        if 4 <= kind < 7: src, dst, peer = own.at[k, z_rows(z_of[kind - 4])], rz.at[slot, kind - 4], to_z[kind - 4]
        if 7 <= kind < 10: src, dst, peer = oth.at[k, z_rows(z)], oth.at[k, z_rows(z)], to_z[kind - 7]
        if kind == 10: src, dst, peer = oth.at[k, x_rows], oth.at[k, x_rows], to_x
        if kind == 11: src, dst, peer = oth.at[k, c_rows], oth.at[k, c_rows], to_c
        return copy_to(src, dst, send.at[slot, kind], recv.at[slot, kind], peer)

    def add_into(dst, src, n):
        def body(i, _):
            r = span(i, 64)
            dst[r, :] = dst[r, :] + src[r, :]
            return 0
        lax.fori_loop(0, n // 64, body, 0)

    def wait(k, kinds):
        for kind in kinds:
            message(k, kind).wait()

    def reduce_stage(k, s):
        slot = k % RING
        if s == 0:
            message(k, 0).start()
            message(k, 1).start()
        if s == 1:
            wait(k, (0, 1))
            add_into(oth.at[k, c_rows], r1.at[slot, 1], half)
            message(k, 2).start()
            add_into(own.at[k, c_rows], r1.at[slot, 0], half)
        if s == 2:
            wait(k, (2,))
            add_into(own.at[k, c_rows], ry.at[slot], half)
            message(k, 3).start()
        if s == 3:
            wait(k, (3,))
            add_into(own.at[k, x_rows], rx.at[slot], quarter)
            for kind in (4, 5, 6):
                message(k, kind).start()
        if s == 4:
            wait(k, (4, 5, 6))
            total = own[k, z_rows(z), :].astype(F32)
            for d in range(3):
                total = total + rz[slot, d].astype(F32)
            oth[k, z_rows(z), :] = total.astype(BF)
            for kind in (7, 8, 9):
                message(k, kind).start()
        if s == 5:
            wait(k, (7, 8, 9))
            message(k, 10).start()
        if s == 6:
            wait(k, (10,))
            message(k, 11).start()
        if s == 7:
            wait(k, (11,))

    def reduce_step(t):
        for s in range(8):
            @pl.when((t >= s) & (t - s < CHUNKS))
            def _():
                reduce_stage(t - s, s)

    def small_messages(i):
        if i == 0:
            return [copy_to(small, s0, small_send.at[0], small_recv.at[0], to_c)]
        if i == 1:
            return [
                copy_to(small.at[pl.ds(0, 8)], s1.at[pl.ds(0, 8)], small_send.at[1], small_recv.at[1], to_y),
                copy_to(small.at[pl.ds(16, 8)], s1.at[pl.ds(8, 8)], small_send.at[2], small_recv.at[2], to_y),
            ]
        got, peer = ((s2, to_x), (s3, to_zp), (s4, to_zq))[i - 2]
        return [copy_to(small.at[pl.ds(0, 16)], got, small_send.at[i + 1], small_recv.at[i + 1], peer)]

    def small_step(i):
        if i > 0:
            for m in small_messages(i - 1):
                m.wait()
            if i == 1:
                small[...] = small[...] + s0[...]
            else:
                small[0:16, :] = small[0:16, :] + (s1, s2, s3, s4)[i - 2][...]
        if i < 5:
            for m in small_messages(i):
                m.start()

    def fetch_ffn(t, start):
        for h in range(2):
            @pl.when((t >= 4 * h) & (t < 4 * h + 4))
            def _():
                b, a = fetch_in(h, t - 4 * h, t % 3), fetch_down(h, t - 4 * h, t % 2)
                if start:
                    b.start()
                    a.start()
                else:
                    b.wait()
                    a.wait()

    def down_tiles(k):
        g = gsec[:, span(k % 2, TILE)]
        own[k] = dot(u1[k // 2], g, 0, 0).astype(BF)
        oth[k] = dot(u1[4 + k // 2], g, 0, 0).astype(BF)

    def hidden_back(t):
        fetch_ffn(t, False)
        g_active = dot(gsec[...], ring_a[t % 2], 1, 1)
        g_hidden = (g_active * u2[t].astype(F32)).astype(BF)
        u2[t] = g_hidden
        total = jnp.sum(g_hidden.astype(F32), axis=0, keepdims=True)
        small[pl.ds(9 + 8 * (t // 4) + (t % 4) // 2, 1), span(t % 2, TILE)] = total
        acc[...] += dot(g_hidden, ring_b[t % 3], 1, 1)

    def in_tiles(k):
        j = k - 8
        a = nlow[:, span(j % 2, TILE)]
        own[k] = dot(a, u2[j // 2], 0, 0).astype(BF)
        oth[k] = dot(a, u2[4 + j // 2], 0, 0).astype(BF)

    def norm_one_back(r, b):
        g_normed, hat = acc[r, :], xhat[r, :]
        scaled = g_normed * gain1
        g_first = rs1[r, 0:1] * (scaled - mean(scaled) - hat * mean(scaled * hat))
        low = g_first.astype(BF)
        acc[r, :] = g_first
        gsec[r, :] = low
        small[0:1, :] += jnp.sum(g_normed * hat, axis=0, keepdims=True)
        small[1:2, :] += jnp.sum(g_normed, axis=0, keepdims=True)
        small[2:3, :] += jnp.sum(low.astype(F32), axis=0, keepdims=True)

    def attend_back(h, p):
        lanes = span(p, 128)
        wide = span(h * pairs + p, 128)
        q2, k2, v2 = qkv[h, 0, :, lanes], qkv[h, 1, :, lanes], qkv[h, 2, :, lanes]
        g = gctx[:, wide].astype(F32) * inv[h, :, lanes]
        low = g.astype(BF)
        less = pltpu.roll(-(g * ctx[:, wide].astype(F32)), HEAD, 1).astype(BF)
        g_q, g_k, g_v = [], [], []
        for head in range(2):
            mine = low_lanes if head == 0 else jnp.logical_not(low_lanes)
            e = u1[2 * p + head]
            g_scores = (dot(jnp.where(mine, low, less), jnp.where(mine, v2, one), 1, 1) * e.astype(F32)).astype(BF)
            g_q.append(dot(g_scores, k2, 1, 0))
            rows = slice(head * HEAD, head * HEAD + HEAD)
            g_k.append(dot(q2, g_scores, 0, 0)[rows])
            g_v.append(dot(low, e, 0, 0)[rows])
        qkv[h, 0, :, lanes] = (jnp.where(low_lanes, g_q[0], g_q[1]) * scale).astype(BF)
        qkv[h, 1, :, lanes] = jnp.concatenate(g_k, axis=0).T.astype(BF)
        qkv[h, 2, :, lanes] = jnp.concatenate(g_v, axis=0).T.astype(BF)

    fetch_ffn(0, True)

    def iteration(t, _):
        @pl.when(t < 8)
        def _():
            down_tiles(t)
        @pl.when((t >= 8) & (t < 16))
        def _():
            in_tiles(t)
        @pl.when((t >= 16) & (t < 18))
        def _():
            g = gsec[:, span(t - 16, TILE)]
            own[t] = dot(ctx[:, :half_w], g, 0, 0).astype(BF)
            oth[t] = dot(ctx[:, half_w:], g, 0, 0).astype(BF)
        @pl.when((t >= 18) & (t < 24))
        def _():
            j = t - 18
            a = xv[:, span(j % 2, TILE)]
            own[t] = dot(a, qkv[0, j // 2], 0, 0).astype(BF)
            oth[t] = dot(a, qkv[1, j // 2], 0, 0).astype(BF)
        reduce_step(t)
        @pl.when(t < 8)
        def _():
            @pl.when(t < 7)
            def _():
                fetch_ffn(t + 1, True)
            hidden_back(t)
        @pl.when(t == 8)
        def _():
            e_copy(0, True).start()
            fetch_out(0).start()
            fetch_out(1).start()
            blocks(norm_one_back)
        @pl.when(t == 9)
        def _():
            for h in range(2):
                fetch_out(h).wait()
                gctx[:, h * half_w : (h + 1) * half_w] = dot(gsec[...], ring_a[h], 1, 1).astype(BF)
            e_copy(0, True).wait()
        for first, h in ((10, 0), (13, 1)):
            @pl.when((t >= first) & (t < first + 2))
            def _():
                def body(p, _):
                    attend_back(h, 2 * (t - first) + p)
                    return 0
                lax.fori_loop(0, 2, body, 0)
            @pl.when(t == first + 1)
            def _():
                if h == 0:
                    e_copy(1, True).start()
                for i in (0, 2):
                    total = jnp.sum(qkv[h, i].astype(F32), axis=0, keepdims=True)
                    small[8 + 8 * h : 9 + 8 * h, (i // 2) * TILE : (i // 2 + 1) * TILE] = total
        @pl.when(t == 12)
        def _():
            e_copy(1, True).wait()
        for h in range(2):
            first = 15 + 2 * h
            @pl.when(t == first)
            def _():
                for i in range(3):
                    fetch_qkv(h, i).start()
            @pl.when(t == first + 1)
            def _():
                for i in range(3):
                    fetch_qkv(h, i).wait()
                    acc[...] += dot(qkv[h, i], ring_b[i], 1, 1)
        @pl.when(t == 19)
        def _():
            def last(r, b):
                gin_ref[r, :] = acc[r, :].astype(BF)
            blocks(last)
        for i in range(6):
            @pl.when(t == 16 + i)
            def _():
                small_step(i)
        return 0

    lax.fori_loop(0, CHUNKS + 7, iteration, 0)
    small_out[...] = small[0:16, :]


def layer(lengths, inputs, cotangent, wq, w_out, w_in, w_down, vectors):
    seq, width = inputs.shape
    half = TILE // 2
    vm, dma = pltpu.VMEM, pltpu.SemaphoreType.DMA
    anywhere, inside = pl.BlockSpec(memory_space=pl.ANY), pl.BlockSpec(memory_space=pltpu.VMEM)
    like = lambda a: jax.ShapeDtypeStruct(a.shape, a.dtype)
    tile_shape = (TILE, TILE)
    return pl.pallas_call(
        layer_kernel,
        out_shape=[
            pltpu.VMEM(inputs.shape, BF), pltpu.VMEM(inputs.shape, BF), pltpu.VMEM((CHUNKS,) + tile_shape, BF),
            pltpu.VMEM((16, width), F32),
            like(wq), like(w_out), like(w_in), like(w_down),
            jax.ShapeDtypeStruct((16,) + tile_shape, BF),
        ],
        in_specs=[pl.BlockSpec(memory_space=pltpu.SMEM)] + [anywhere] * 6 + [inside] * 8,
        out_specs=[inside] * 4 + [anywhere] * 5,
        scratch_shapes=[
            vm((seq, width), BF), vm((seq, width), BF), vm((seq, width), BF), vm((seq, width), BF), vm((seq, width), BF),
            vm((2, 3) + tile_shape, BF), vm((2,) + tile_shape, F32),
            vm((seq, width), F32), vm((seq, 128), F32), vm((seq, width), F32),
            vm((8,) + tile_shape, BF), vm((8,) + tile_shape, BF),
            vm((CHUNKS,) + tile_shape, BF),
            vm((RING, 2, half, TILE), BF), vm((RING, half, TILE), BF),
            vm((RING, half // 2, TILE), BF), vm((RING, 3, half // 8, TILE), BF),
            vm((2, TILE, width), BF), vm((3, width, TILE), BF),
            vm((8, width), F32), vm((8, TILE), F32), vm((8, TILE), F32), vm((24, width), F32), vm((24, width), F32),
            vm((16, width), F32), vm((16, width), F32), vm((16, width), F32), vm((16, width), F32),
            dma((2,)), dma((2, CHUNKS)), dma((2,)), dma((3,)), dma((2,)),
            dma((9, 12)), dma((9, 12)), dma((RING, MESSAGES)), dma((RING, MESSAGES)), dma((6,)), dma((6,)),
        ],
        compiler_params=pltpu.CompilerParams(
            collective_id=1, has_side_effects=True, vmem_limit_bytes=47 << 20
        ),
    )(lengths, inputs, cotangent, wq, w_out, w_in, w_down, *vectors)


def widen_kernel(
    tiles, out_in, gin_in, sums, down, within, out, three, out_out, gin_out,
    b_qv, b_out, gain1, shift1, b_in, b_down, gain2, shift2, wide, out_sem, pass_sem,
):
    leave = [pltpu.make_async_copy(ref, to, pass_sem.at[i]) for i, (ref, to) in enumerate(((out_in, out_out), (gin_in, gin_out)))]
    for copy in leave:
        copy.start()
    width, half = sums.shape[1], b_qv.shape[1]
    for ref, row in ((gain1, 0), (shift1, 1), (b_out, 2), (gain2, 3), (shift2, 4), (b_down, 5)):
        ref[...] = sums[row, :]
    for i in range(2):
        b_qv[i : i + 1, :] = sums[8:9, i * half : (i + 1) * half]
        b_in[i * width : (i + 1) * width] = sums[9 + i, :]

    def store(k):
        which, where = tile_place(k)
        return pltpu.make_async_copy(wide.at[k % RING], (down, within, out, three)[which].at[where], out_sem.at[k % RING])

    stores = [store(k) for k in range(CHUNKS)]
    for k in range(CHUNKS):
        if k >= RING:
            stores[k - RING].wait()
        def body(i, _):
            r = span(i, 32)
            wide[k % RING, r, :] = tiles[k, r, :].astype(F32)
            return 0
        lax.fori_loop(0, TILE // 32, body, 0)
        stores[k].start()
    for copy in stores[CHUNKS - RING :] + leave:
        copy.wait()


def widen(tiles, output, grad_inputs, sums, half_hidden, width, half_width):
    tile, vm, dma = (TILE, TILE), pltpu.VMEM, pltpu.SemaphoreType.DMA
    anywhere, inside = pl.BlockSpec(memory_space=pl.ANY), pl.BlockSpec(memory_space=pltpu.VMEM)
    wide = lambda *shape: jax.ShapeDtypeStruct(shape, F32)
    return pl.pallas_call(
        widen_kernel,
        out_shape=[
            wide(half_hidden, width), wide(width, half_hidden), wide(half_width, width), wide(3, width, half_width),
            jax.ShapeDtypeStruct(output.shape, output.dtype), jax.ShapeDtypeStruct(output.shape, output.dtype),
            wide(2, half_width), wide(width), wide(width), wide(width), wide(half_hidden), wide(width), wide(width), wide(width),
        ],
        in_specs=[inside] * 4,
        out_specs=[anywhere] * 6 + [inside] * 8,
        scratch_shapes=[
            vm((RING,) + tile, F32), dma((RING,)), dma((2,)),
        ],
        compiler_params=pltpu.CompilerParams(vmem_limit_bytes=16 << 20),
    )(tiles, output, grad_inputs, sums)


def split_by_sequence(
    inputs, lengths, w_qkv, b_qv, w_out, b_out, gain_one, shift_one, w_in, b_in, w_down, b_down, gain_two, shift_two,
    cotangent,
):
    rows, width = inputs.shape
    half_width, half_hidden = w_qkv.shape[2], w_in.shape[1]
    wq = w_qkv.transpose(1, 0, 2)
    vectors = (b_out, gain_one, shift_one, b_down, gain_two, shift_two, b_qv, b_in)
    made = layer(lengths, inputs, cotangent, wq, w_out, w_in, w_down, vectors)
    output, grad_inputs, tiles, sums = made[:4]
    (
        g_w_down, g_w_in, g_w_out, g_w_qkv, output, grad_inputs,
        g_b_qv, g_b_out, g_gain_one, g_shift_one, g_b_in, g_b_down, g_gain_two, g_shift_two,
    ) = widen(tiles, output, grad_inputs, sums, half_hidden, width, half_width)
    return (
        output, grad_inputs, g_w_qkv.transpose(1, 0, 2), g_b_qv, g_w_out, g_b_out, g_gain_one, g_shift_one,
        g_w_in, g_b_in, g_w_down, g_b_down, g_gain_two, g_shift_two,
    )


def solution(mesh):
    small_mesh = mesh.shape["tensor"] == 2 and mesh.shape["dp"] == 2 * N_X * N_Z
    step = split_by_sequence if small_mesh else general
    in_specs = (
        P(("dp", "tensor"), None),
        P("dp"),
        P(None, None, "tensor"),
        P(None, "tensor"),
        P("tensor", None),
        P(),
        P(),
        P(),
        P(None, "tensor"),
        P("tensor"),
        P("tensor", None),
        P(),
        P(),
        P(),
        P(("dp", "tensor"), None),
    )
    out_specs = (
        P(("dp", "tensor"), None),
        P(("dp", "tensor"), None),
        P(None, None, "tensor"),
        P(None, "tensor"),
        P("tensor", None),
        P(),
        P(),
        P(),
        P(None, "tensor"),
        P("tensor"),
        P("tensor", None),
        P(),
        P(),
        P(),
    )
    return jax.shard_map(step, mesh=mesh, in_specs=in_specs, out_specs=out_specs, check_vma=False)
```

```python
import jax
import jax.numpy as jnp
from jax import lax
from jax.experimental import pallas as pl
from jax.experimental.pallas import tpu as pltpu
from jax.sharding import PartitionSpec as P

MESH = pl.DeviceIdType.MESH
N_Z, N_X = 4, 2
TILE = 512
MESSAGES = 12
VMEM_BYTES = 63 << 20

HEAD = 64
SEQ = 512
SEQ_DEV = 2


EPSILON = 1e-12
NEG_FILL = -1000000000.0


def gelu_exact(values):
    return jax.nn.gelu(values, approximate=False)


def norm_forward(values, gain_vec, shift_vec):
    center = values - jnp.mean(values, axis=-1, keepdims=True)
    spread = jnp.mean(center * center, axis=-1, keepdims=True)
    inverse = lax.rsqrt(spread + EPSILON)
    scaled = center * inverse
    return (scaled * gain_vec + shift_vec, scaled, inverse)


def norm_backward(grad_out, scaled, inverse, gain_vec):
    grad_scaled = grad_out * gain_vec
    mean_one = jnp.mean(grad_scaled, axis=-1, keepdims=True)
    mean_two = jnp.mean(grad_scaled * scaled, axis=-1, keepdims=True)
    grad_in = inverse * (grad_scaled - mean_one - scaled * mean_two)
    return (grad_in, jnp.sum(grad_out * scaled, axis=0), jnp.sum(grad_out, axis=0))


def masked_scores(queries, key_rows, length):
    score_scale = HEAD ** (-0.5)
    scores = (
        jnp.einsum("qhe,khe->hqk", queries, key_rows, preferred_element_type=jnp.float32)
        * score_scale
    )
    key_valid = (jnp.arange(SEQ) < length)[None, None, :]
    return jnp.where(key_valid, scores, NEG_FILL)


def attend_forward(element):
    queries, key_rows, value_rows, length = element
    scores = masked_scores(queries, key_rows, length)
    peak_score = jnp.max(scores, axis=-1, keepdims=True)
    shifted_exp = jnp.exp(scores - peak_score)
    denominator = jnp.sum(shifted_exp, axis=-1, keepdims=True)
    probability = (shifted_exp / denominator).astype(jnp.bfloat16)
    context = jnp.einsum(
        "hqk,khe->qhe", probability, value_rows, preferred_element_type=jnp.float32
    )
    return (context.astype(jnp.bfloat16), (peak_score + jnp.log(denominator))[..., 0])


def attend_backward(element):
    queries, key_rows, value_rows, length, log_total, grad_context = element
    score_scale = HEAD ** (-0.5)
    scores = masked_scores(queries, key_rows, length)
    probability = jnp.exp(scores - log_total[..., None])
    grad_prob = jnp.einsum(
        "qhe,khe->hqk", grad_context, value_rows, preferred_element_type=jnp.float32
    )
    grad_value = jnp.einsum(
        "hqk,qhe->khe",
        probability.astype(jnp.bfloat16),
        grad_context,
        preferred_element_type=jnp.float32,
    )
    grad_scores = probability * (
        grad_prob - jnp.sum(probability * grad_prob, axis=-1, keepdims=True)
    )
    grad_scores = grad_scores.astype(jnp.bfloat16)
    grad_query = (
        jnp.einsum("hqk,khe->qhe", grad_scores, key_rows, preferred_element_type=jnp.float32)
        * score_scale
    )
    grad_key = (
        jnp.einsum("hqk,qhe->khe", grad_scores, queries, preferred_element_type=jnp.float32)
        * score_scale
    )
    return jnp.stack([grad_query, grad_key, grad_value], axis=1).astype(jnp.bfloat16)


def row_mask(lengths, rows_dev):
    places = lax.axis_index("tensor") * rows_dev + jnp.arange(rows_dev)
    sequence_of = places // SEQ
    offset = places % SEQ
    matches = sequence_of[:, None] == jnp.arange(lengths.shape[0])[None, :]
    limit_rows = jnp.sum(jnp.where(matches, lengths[None, :], 0), axis=1)
    return (offset < limit_rows).astype(jnp.float32)[:, None]


def forward_pass(inputs, lengths, weights):
    (
        w_qkv,
        b_qv,
        w_out,
        b_out,
        gain_one,
        shift_one,
        w_in,
        b_in,
        w_down,
        b_down,
        gain_two,
        shift_two,
    ) = weights
    width_dev = w_qkv.shape[2]
    gathered = lax.all_gather(inputs, "tensor", axis=0, tiled=True)
    bias_three = jnp.stack([b_qv[0], jnp.zeros_like(b_qv[0]), b_qv[1]]).astype(jnp.float32)
    projected = (
        jnp.einsum("td,dcf->tcf", gathered, w_qkv, preferred_element_type=jnp.float32) + bias_three
    ).astype(jnp.bfloat16)
    shaped = projected.reshape(SEQ_DEV, SEQ, 3, width_dev // HEAD, HEAD)
    context, log_total = lax.map(
        attend_forward, (shaped[:, :, 0], shaped[:, :, 1], shaped[:, :, 2], lengths)
    )
    context = context.reshape(SEQ_DEV * SEQ, width_dev)
    segment = context
    branch = lax.psum_scatter(
        jnp.dot(segment, w_out, preferred_element_type=jnp.float32).astype(jnp.bfloat16),
        "tensor",
        scatter_dimension=0,
        tiled=True,
    ).astype(jnp.float32) + b_out.astype(jnp.float32)
    normed, scaled_one, inverse_one = norm_forward(
        inputs.astype(jnp.float32) + branch,
        gain_one.astype(jnp.float32),
        shift_one.astype(jnp.float32),
    )
    normed_all = lax.all_gather(normed.astype(jnp.bfloat16), "tensor", axis=0, tiled=True)
    hidden = jnp.dot(normed_all, w_in, preferred_element_type=jnp.float32) + b_in.astype(
        jnp.float32
    )
    active = gelu_exact(hidden).astype(jnp.bfloat16)
    segment = active
    second = lax.psum_scatter(
        jnp.dot(segment, w_down, preferred_element_type=jnp.float32).astype(jnp.bfloat16),
        "tensor",
        scatter_dimension=0,
        tiled=True,
    ).astype(jnp.float32) + b_down.astype(jnp.float32)
    output, scaled_two, inverse_two = norm_forward(
        normed + second, gain_two.astype(jnp.float32), shift_two.astype(jnp.float32)
    )
    return (
        gathered,
        projected,
        context,
        log_total,
        scaled_one,
        inverse_one,
        normed_all,
        hidden,
        active,
        scaled_two,
        inverse_two,
        output,
    )


def general(
    inputs,
    lengths,
    w_qkv,
    b_qv,
    w_out,
    b_out,
    gain_one,
    shift_one,
    w_in,
    b_in,
    w_down,
    b_down,
    gain_two,
    shift_two,
    cotangent,
):
    weights = (
        w_qkv,
        b_qv,
        w_out,
        b_out,
        gain_one,
        shift_one,
        w_in,
        b_in,
        w_down,
        b_down,
        gain_two,
        shift_two,
    )
    first_pass = forward_pass(inputs, lengths, weights)
    output = first_pass[11].astype(jnp.bfloat16)
    recorded = forward_pass(inputs, lengths, weights)
    (
        gathered,
        projected,
        context,
        log_total,
        scaled_one,
        inverse_one,
        normed_all,
        hidden,
        active,
        scaled_two,
        inverse_two,
        _,
    ) = recorded
    rows_dev = inputs.shape[0]
    width_dev = w_qkv.shape[2]
    grad_out = cotangent.astype(jnp.float32) * row_mask(lengths, rows_dev)
    grad_two, grad_gain_two, grad_shift_two = norm_backward(
        grad_out, scaled_two, inverse_two, gain_two.astype(jnp.float32)
    )
    grad_second = grad_two.astype(jnp.bfloat16)
    grad_b_down = jnp.sum(grad_second.astype(jnp.float32), axis=0)
    second_all = lax.all_gather(grad_second, "tensor", axis=0, tiled=True)
    grad_w_down = jnp.einsum("tf,td->fd", active, second_all, preferred_element_type=jnp.float32)
    grad_active = jnp.einsum("td,fd->tf", second_all, w_down, preferred_element_type=jnp.float32)
    _, gelu_pull = jax.vjp(gelu_exact, hidden)
    grad_hidden = gelu_pull(grad_active)[0].astype(jnp.bfloat16)
    grad_b_in = jnp.sum(grad_hidden.astype(jnp.float32), axis=0)
    grad_w_in = jnp.einsum("td,tf->df", normed_all, grad_hidden, preferred_element_type=jnp.float32)
    segment = grad_hidden
    grad_normed = grad_two + lax.psum_scatter(
        jnp.einsum("tf,df->td", segment, w_in, preferred_element_type=jnp.float32).astype(
            jnp.bfloat16
        ),
        "tensor",
        scatter_dimension=0,
        tiled=True,
    ).astype(jnp.float32)
    grad_first, grad_gain_one, grad_shift_one = norm_backward(
        grad_normed, scaled_one, inverse_one, gain_one.astype(jnp.float32)
    )
    grad_branch = grad_first.astype(jnp.bfloat16)
    grad_b_out = jnp.sum(grad_branch.astype(jnp.float32), axis=0)
    branch_all = lax.all_gather(grad_branch, "tensor", axis=0, tiled=True)
    grad_w_out = jnp.einsum("tf,td->fd", context, branch_all, preferred_element_type=jnp.float32)
    grad_context = jnp.einsum(
        "td,fd->tf", branch_all, w_out, preferred_element_type=jnp.float32
    ).astype(jnp.bfloat16)
    heads_dev = width_dev // HEAD
    shaped = projected.reshape(SEQ_DEV, SEQ, 3, heads_dev, HEAD)
    grad_shaped = grad_context.reshape(SEQ_DEV, SEQ, heads_dev, HEAD)
    grad_proj = lax.map(
        attend_backward,
        (shaped[:, :, 0], shaped[:, :, 1], shaped[:, :, 2], lengths, log_total, grad_shaped),
    )
    grad_proj = grad_proj.reshape(SEQ_DEV * SEQ, 3, width_dev)
    grad_w_qkv = jnp.einsum("td,tcf->dcf", gathered, grad_proj, preferred_element_type=jnp.float32)
    grad_b_qv = jnp.sum(grad_proj[:, 0::2].astype(jnp.float32), axis=0)
    segment = grad_proj
    grad_inputs = (
        grad_first
        + lax.psum_scatter(
            jnp.einsum("tcf,dcf->td", segment, w_qkv, preferred_element_type=jnp.float32).astype(
                jnp.bfloat16
            ),
            "tensor",
            scatter_dimension=0,
            tiled=True,
        ).astype(jnp.float32)
    ).astype(jnp.bfloat16)
    small_terms = jnp.stack(
        [grad_gain_one, grad_shift_one, grad_b_out, grad_gain_two, grad_shift_two, grad_b_down]
    )
    grad_w_qkv, grad_b_qv, grad_w_out, grad_w_in, grad_b_in, grad_w_down, small_terms = (
        lax.psum(grad_w_qkv.astype(jnp.bfloat16), "dp").astype(jnp.float32),
        lax.psum(grad_b_qv.astype(jnp.bfloat16), "dp").astype(jnp.float32),
        lax.psum(grad_w_out.astype(jnp.bfloat16), "dp").astype(jnp.float32),
        lax.psum(grad_w_in.astype(jnp.bfloat16), "dp").astype(jnp.float32),
        lax.psum(grad_b_in.astype(jnp.bfloat16), "dp").astype(jnp.float32),
        lax.psum(grad_w_down.astype(jnp.bfloat16), "dp").astype(jnp.float32),
        lax.psum(small_terms.astype(jnp.bfloat16), "dp").astype(jnp.float32),
    )
    small_sums = lax.psum(small_terms, "tensor")
    return (
        output,
        grad_inputs,
        grad_w_qkv,
        grad_b_qv,
        grad_w_out,
        small_sums[2],
        small_sums[0],
        small_sums[1],
        grad_w_in,
        grad_b_in,
        grad_w_down,
        small_sums[5],
        small_sums[3],
        small_sums[4],
    )


def place():
    dp = lax.axis_index("dp")
    return dp // (2 * N_X), (dp // 2) % N_X, dp % 2, lax.axis_index("tensor")


def at(z, x, c, y):
    return ((z * N_X + x) * 2 + c, y)


def greet(peers):
    barrier = pltpu.get_barrier_semaphore()
    for peer in peers:
        pl.semaphore_signal(barrier, inc=1, device_id=peer, device_id_type=MESH)
    pl.semaphore_wait(barrier, len(peers))


def copy_to(src, dst, send_sem, recv_sem, peer):
    return pltpu.make_async_remote_copy(
        src_ref=src, dst_ref=dst, send_sem=send_sem, recv_sem=recv_sem,
        device_id=peer, device_id_type=MESH,
    )


CHUNKS = 24
RING = 4
BF, F32 = jnp.bfloat16, jnp.float32
ROWS_AT_ONCE = 128


def dot(a, b, ca, cb):
    return lax.dot_general(a, b, (((ca,), (cb,)), ((), ())), preferred_element_type=F32)


def span(index, size):
    return pl.ds(pl.multiple_of(index * size, size), size)


def tile_place(k):
    if k < 8:
        return 0, (slice(k // 2 * TILE, (k // 2 + 1) * TILE), slice(k % 2 * TILE, (k % 2 + 1) * TILE))
    if k < 16:
        k -= 8
        return 1, (slice(k % 2 * TILE, (k % 2 + 1) * TILE), slice(k // 2 * TILE, (k // 2 + 1) * TILE))
    if k < 18:
        k -= 16
        return 2, (slice(0, TILE), slice(k * TILE, (k + 1) * TILE))
    k -= 18
    return 3, (k // 2, slice(k % 2 * TILE, (k % 2 + 1) * TILE), slice(0, TILE))


def layer_kernel(
    lengths, x_hbm, cot_hbm, wq_own, wo_own, wi_own, wd_own, in1, in2, in3, in4, in5, in6, in_qv, in_hidden,
    out_ref, gin_ref, oth, small_out, wq_oth, wo_oth, wi_oth, wd_oth, e_hbm,
    xv, nlow, gsec, gctx, ctx, qkv, inv, xhat, rs1, acc, u1, u2, own, r1, ry, rx, rz,
    ring_a, ring_b, vec, bias_own, bias_oth, small, s0, s1, s2, s3, s4,
    load_sem, w_sem, a_sem, b_sem, e_sem, g_send, g_recv, send, recv, small_send, small_recv,
):
    z, x, c, y = place()
    zb = z % 2
    z_of = [(z + d) % N_Z for d in (1, 2, 3)]
    to_c, to_y, to_x = at(z, x, 1 - c, y), at(z, x, c, 1 - y), at(z, 1 - x, c, y)
    to_z = [at(v, x, c, y) for v in z_of]
    to_zp, to_zq = at(z + 1 - 2 * zb, x, c, y), at((z + 2) % N_Z, x, c, y)
    seq, width = xv.shape
    half_w = width // 2

    load_x = pltpu.make_async_copy(x_hbm, xv, load_sem.at[0])
    load_cot = pltpu.make_async_copy(cot_hbm, gsec, load_sem.at[1])
    load_x.start()
    load_cot.start()
    for row, ref in enumerate((in1, in2, in3, in4, in5, in6)):
        vec[row : row + 1, :] = ref[...].astype(F32).reshape(1, width)
    bias_own[0:2, :] = in_qv[...].astype(F32)
    bias_own[2:6, :] = in_hidden[...].astype(F32).reshape(4, TILE)

    def fetch_qkv(h, i):
        source = (wq_own, wq_oth)[h]
        return pltpu.make_async_copy(source.at[i], ring_b.at[i], b_sem.at[i])

    def fetch_out(h):
        return pltpu.make_async_copy((wo_own, wo_oth)[h], ring_a.at[h], a_sem.at[h])

    def fetch_in(h, f, slot):
        return pltpu.make_async_copy((wi_own, wi_oth)[h].at[:, span(f, TILE)], ring_b.at[slot], b_sem.at[slot])

    def fetch_down(h, f, slot):
        return pltpu.make_async_copy((wd_own, wd_oth)[h].at[span(f, TILE)], ring_a.at[slot], a_sem.at[slot])

    def weight_load(h, k):
        which, where = tile_place(k)
        source = ((wd_own, wi_own, wo_own, wq_own), (wd_oth, wi_oth, wo_oth, wq_oth))[h][which]
        return pltpu.make_async_copy(source.at[where], (own, oth)[h].at[k], w_sem.at[h, k])

    for k in (*range(18, 24), *range(8, 16), *range(0, 8), 16, 17):
        weight_load(0, k).start()

    greet([to_c, to_y, to_x] + to_z)

    cut = wi_own.shape[1] // 2
    deep = wd_own.shape[0] // 2
    arrays = [(wq_own.at[i], wq_oth.at[i]) for i in range(3)] + [(wo_own, wo_oth)]
    arrays += [(wi_own.at[:, j * cut : (j + 1) * cut], wi_oth.at[:, j * cut : (j + 1) * cut]) for j in range(2)]
    arrays += [(wd_own.at[j * deep : (j + 1) * deep], wd_oth.at[j * deep : (j + 1) * deep]) for j in range(2)]
    loads_of = [(18, 19), (20, 21), (22, 23), (16, 17), (8, 9, 10, 11), (12, 13, 14, 15), (0, 1, 2, 3), (4, 5, 6, 7)]
    count = len(arrays)

    def gather_message(n, kind):
        size = arrays[n][0].shape[0] // 2
        size_part = size // 8 - (8 if n >= 4 else 0)
        near_a, near_b = 2 * zb, 4 + 2 * x
        far_a, far_b = 2 * (1 - zb), 4 + 2 * (1 - x)
        one_a, one_b = 2 * zb + x, 4 + 2 * x + zb
        first, parts, peer = [
            (one_a, 1, to_y), (one_b, 1, to_y), (one_a, 1, to_x), (one_b, 1, to_zp),
            (near_a, 2, to_zp), (near_b, 2, to_x), (near_a, 2, to_c), (near_b, 2, to_c), (far_a, 2, to_c), (far_b, 2, to_c),
            (8, 0, to_y), (8, 0, to_c),
        ][kind]
        length_rows = parts * size_part if parts else size - 8 * size_part
        rows = pl.ds(pl.multiple_of(c * size + first * size_part, 8), length_rows)
        source = arrays[n][0 if kind in (0, 1, 10) else 1]
        return copy_to(source.at[rows], arrays[n][1].at[rows], g_send.at[n, kind], g_recv.at[n, kind], peer)

    def gather_stage(n, step):
        if step == 0:
            gather_message(n, 0).wait_recv()
            gather_message(n, 2).start()
            gather_message(n, 1).wait_recv()
            gather_message(n, 3).start()
        if step == 1:
            gather_message(n, 2).wait_recv()
            gather_message(n, 4).start()
            gather_message(n, 6).start()
            gather_message(n, 3).wait_recv()
            gather_message(n, 5).start()
            gather_message(n, 7).start()
        if step == 2:
            gather_message(n, 4).wait_recv()
            gather_message(n, 8).start()
            gather_message(n, 5).wait_recv()
            gather_message(n, 9).start()
            if n >= 4:
                gather_message(n, 10).wait_recv()
                gather_message(n, 11).start()
        if step == 3:
            kinds = range(12 if n >= 4 else 10)
            for kind in kinds:
                if kind >= 6 and kind != 10:
                    gather_message(n, kind).wait_recv()
            for k in loads_of[n]:
                weight_load(1, k).start()
            for kind in kinds:
                gather_message(n, kind).wait_send()

    def progress(slot):
        for step in range(4):
            if 0 <= slot - step < count:
                gather_stage(slot - step, step)

    send_bias = copy_to(bias_own, bias_oth, g_send.at[count, 0], g_recv.at[count, 0], to_y)
    send_bias.start()
    for n in (0, 1, 2, 3, 4, 5, -4, 6, -5, 7, -6, -7):
        for kind in (0, 1) if n >= 0 else (10,):
            gather_message(abs(n), kind).start()

    length = lengths[y]
    key_fill = jnp.where(lax.broadcasted_iota(jnp.int32, (1, seq), 1) < length, 0.0, NEG_FILL)
    low_lanes = lax.broadcasted_iota(jnp.int32, (1, 128), 1) < HEAD
    one, zero = jnp.ones((), BF), jnp.zeros((), BF)
    scale = HEAD ** (-0.5)
    pairs = half_w // 128

    def project(h):
        bias = (bias_own, bias_oth)[h]
        for i in range(3):
            for k in (18 + 2 * i, 19 + 2 * i):
                weight_load(h, k).wait()
            value = dot(xv[...], (own, oth)[h][18 + 2 * i : 20 + 2 * i].reshape(width, TILE), 1, 0)
            if i == 0:
                qkv[h, 0] = (value + bias[0:1, :]).astype(BF) * jnp.asarray(scale, BF)
            if i == 1:
                qkv[h, 1] = value.astype(BF)
            if i == 2:
                qkv[h, 2] = (value + bias[1:2, :]).astype(BF)

    def attend(h, p, e_ref):
        lanes = span(p, 128)
        q2, k2, v2 = qkv[h, 0, :, lanes], qkv[h, 1, :, lanes], qkv[h, 2, :, lanes]
        parts = []
        for head in range(2):
            mine = low_lanes if head == 0 else jnp.logical_not(low_lanes)
            scores = dot(jnp.where(mine, q2, zero), k2, 1, 1) + key_fill
            peak = jnp.max(scores, axis=-1, keepdims=True)
            e = jnp.exp(scores - peak).astype(BF)
            e_ref[2 * p + head] = e
            parts.append(dot(e, jnp.where(mine, v2, one), 1, 0))
        total = pltpu.roll(jnp.where(low_lanes, parts[1], parts[0]), HEAD, 1)
        inverse = 1.0 / total
        inv[h, :, lanes] = inverse
        ctx[:, span(h * pairs + p, 128)] = (jnp.where(low_lanes, parts[0], parts[1]) * inverse).astype(BF)

    def attend_half(h, slots):
        def body(p, _):
            attend(h, p, (u1, u2)[h])
            for at_pair, slot in slots:
                @pl.when(p == at_pair)
                def _():
                    progress(slot)
            return 0
        lax.fori_loop(0, pairs, body, 0)

    def e_copy(h, back):
        ref, buf = e_hbm.at[pl.ds(h * 8, 8)], (u1 if back else (u1, u2)[h])
        return pltpu.make_async_copy(ref, buf, e_sem.at[h]) if back else pltpu.make_async_copy(buf, ref, e_sem.at[h])

    def out_project(h):
        for d in range(2):
            weight_load(h, 16 + d).wait()
            term = dot(ctx[:, h * half_w : (h + 1) * half_w], (own, oth)[h][16 + d], 1, 0)
            lanes = slice(d * TILE, (d + 1) * TILE)
            acc[:, lanes] = term if h == 0 else acc[:, lanes] + term

    load_x.wait()
    project(0)
    attend_half(0, ((1, 0), (3, 1)))
    e_copy(0, False).start()
    out_project(0)
    for slot in (2, 3, 4, 5):
        progress(slot)
    send_bias.wait()
    project(1)
    attend_half(1, ((1, 6),))
    e_copy(1, False).start()
    out_project(1)

    def blocks(body):
        def run(b, _):
            body(span(b, ROWS_AT_ONCE), b)
            return 0
        lax.fori_loop(0, seq // ROWS_AT_ONCE, run, 0)

    def mean(v):
        return jnp.sum(v, axis=-1, keepdims=True) * (1.0 / width)

    small[...] = jnp.zeros_like(small)
    b_out, gain1, shift1 = vec[0:1, :], vec[1:2, :], vec[2:3, :]
    b_down, gain2, shift2 = vec[3:4, :], vec[4:5, :], vec[5:6, :]

    def norm_one(r, b):
        v = xv[r, :].astype(F32) + (acc[r, :] + b_out)
        center = v - mean(v)
        inverse = lax.rsqrt(mean(center * center) + EPSILON)
        hat = center * inverse
        xhat[r, :] = hat
        rs1[r, :] = jnp.broadcast_to(inverse, (ROWS_AT_ONCE, 128))
        nlow[r, :] = (hat * gain1 + shift1).astype(BF)
    blocks(norm_one)
    e_copy(0, False).wait()
    e_copy(1, False).wait()
    progress(7)

    def hidden_half(h, slots):
        bias, weights = (bias_own, bias_oth)[h], (own, oth)[h]
        for f in range(4):
            for k in (8 + 2 * f, 9 + 2 * f):
                weight_load(h, k).wait()
            hidden = dot(nlow[...], weights[8 + 2 * f : 10 + 2 * f].reshape(width, TILE), 1, 0) + bias[2 + f : 3 + f, :]
            cdf = 0.5 + 0.5 * lax.erf(hidden * 0.7071067811865476)
            u1[4 * h + f] = (hidden * cdf).astype(BF)
            u2[4 * h + f] = (cdf + hidden * (jnp.exp(hidden * hidden * -0.5) * 0.3989422804014327)).astype(BF)
            if f in slots:
                progress(slots[f])

    def down_half(h, tiles, clear=False):
        for f in tiles:
            for d in range(2):
                weight_load(h, 2 * f + d).wait()
                term = dot(u1[4 * h + f], (own, oth)[h][2 * f + d], 1, 0)
                lanes = slice(d * TILE, (d + 1) * TILE)
                acc[:, lanes] = term if clear and f == tiles[0] else acc[:, lanes] + term

    hidden_half(0, {})
    down_half(0, (0, 1), True)
    progress(8)
    down_half(0, (2, 3))
    hidden_half(1, {3: 9})
    down_half(1, (0, 1))
    progress(10)
    down_half(1, (2, 3))

    load_cot.wait()
    valid_limit = lengths[y]

    def norm_two(r, b):
        normed = xhat[r, :] * gain1 + shift1
        v = normed + (acc[r, :] + b_down)
        center = v - mean(v)
        inverse = lax.rsqrt(mean(center * center) + EPSILON)
        hat = center * inverse
        out_ref[r, :] = (hat * gain2 + shift2).astype(BF)
        position = b * ROWS_AT_ONCE + lax.broadcasted_iota(jnp.int32, (ROWS_AT_ONCE, 1), 0)
        g_out = jnp.where(position < valid_limit, gsec[r, :].astype(F32), 0.0)
        scaled = g_out * gain2
        g_two = inverse * (scaled - mean(scaled) - hat * mean(scaled * hat))
        low = g_two.astype(BF)
        acc[r, :] = g_two
        gsec[r, :] = low
        small[3:4, :] += jnp.sum(g_out * hat, axis=0, keepdims=True)
        small[4:5, :] += jnp.sum(g_out, axis=0, keepdims=True)
        small[5:6, :] += jnp.sum(low.astype(F32), axis=0, keepdims=True)
    blocks(norm_two)

    half, quarter, part = TILE // 2, TILE // 4, TILE // 16
    c_rows = span(c, half)
    cn_rows = span(1 - c, half)
    x_rows = pl.ds(pl.multiple_of(c * half + x * quarter, quarter), quarter)
    xn_rows = pl.ds(pl.multiple_of(c * half + (1 - x) * quarter, quarter), quarter)

    def z_rows(v):
        return pl.ds(pl.multiple_of(c * half + x * quarter + v * part, part), part)

    def message(k, kind):
        slot = k % RING
        if kind == 0: src, dst, peer = own.at[k, cn_rows], r1.at[slot, 0], to_c
        if kind == 1: src, dst, peer = oth.at[k, cn_rows], r1.at[slot, 1], to_c
        if kind == 2: src, dst, peer = oth.at[k, c_rows], ry.at[slot], to_y
        if kind == 3: src, dst, peer = own.at[k, xn_rows], rx.at[slot], to_x
        if 4 <= kind < 7: src, dst, peer = own.at[k, z_rows(z_of[kind - 4])], rz.at[slot, kind - 4], to_z[kind - 4]
        if 7 <= kind < 10: src, dst, peer = oth.at[k, z_rows(z)], oth.at[k, z_rows(z)], to_z[kind - 7]
        if kind == 10: src, dst, peer = oth.at[k, x_rows], oth.at[k, x_rows], to_x
        if kind == 11: src, dst, peer = oth.at[k, c_rows], oth.at[k, c_rows], to_c
        return copy_to(src, dst, send.at[slot, kind], recv.at[slot, kind], peer)

    def add_into(dst, src, n):
        def body(i, _):
            r = span(i, 64)
            dst[r, :] = dst[r, :] + src[r, :]
            return 0
        lax.fori_loop(0, n // 64, body, 0)

    def wait(k, kinds):
        for kind in kinds:
            message(k, kind).wait()

    def reduce_stage(k, s):
        slot = k % RING
        if s == 0:
            message(k, 0).start()
            message(k, 1).start()
        if s == 1:
            wait(k, (0, 1))
            add_into(oth.at[k, c_rows], r1.at[slot, 1], half)
            message(k, 2).start()
            add_into(own.at[k, c_rows], r1.at[slot, 0], half)
        if s == 2:
            wait(k, (2,))
            add_into(own.at[k, c_rows], ry.at[slot], half)
            message(k, 3).start()
        if s == 3:
            wait(k, (3,))
            add_into(own.at[k, x_rows], rx.at[slot], quarter)
            for kind in (4, 5, 6):
                message(k, kind).start()
        if s == 4:
            wait(k, (4, 5, 6))
            total = own[k, z_rows(z), :].astype(F32)
            for d in range(3):
                total = total + rz[slot, d].astype(F32)
            oth[k, z_rows(z), :] = total.astype(BF)
            for kind in (7, 8, 9):
                message(k, kind).start()
        if s == 5:
            wait(k, (7, 8, 9))
            message(k, 10).start()
        if s == 6:
            wait(k, (10,))
            message(k, 11).start()
        if s == 7:
            wait(k, (11,))

    def reduce_step(t, stages):
        for s in stages:
            @pl.when((t >= s) & (t - s < CHUNKS))
            def _():
                reduce_stage(t - s, s)

    def small_messages(i):
        if i == 0:
            return [copy_to(small, s0, small_send.at[0], small_recv.at[0], to_c)]
        if i == 1:
            return [
                copy_to(small.at[pl.ds(0, 8)], s1.at[pl.ds(0, 8)], small_send.at[1], small_recv.at[1], to_y),
                copy_to(small.at[pl.ds(16, 8)], s1.at[pl.ds(8, 8)], small_send.at[2], small_recv.at[2], to_y),
            ]
        got, peer = ((s2, to_x), (s3, to_zp), (s4, to_zq))[i - 2]
        return [copy_to(small.at[pl.ds(0, 16)], got, small_send.at[i + 1], small_recv.at[i + 1], peer)]

    def small_step(i):
        if i > 0:
            for m in small_messages(i - 1):
                m.wait()
            if i == 1:
                small[...] = small[...] + s0[...]
            else:
                small[0:16, :] = small[0:16, :] + (s1, s2, s3, s4)[i - 2][...]
        if i < 5:
            for m in small_messages(i):
                m.start()

    def fetch_ffn(t, start):
        for h in range(2):
            @pl.when((t >= 4 * h) & (t < 4 * h + 4))
            def _():
                b, a = fetch_in(h, t - 4 * h, t % 3), fetch_down(h, t - 4 * h, t % 2)
                if start:
                    b.start()
                    a.start()
                else:
                    b.wait()
                    a.wait()

    def down_tiles(k):
        g = gsec[:, span(k % 2, TILE)]
        own[k] = dot(u1[k // 2], g, 0, 0).astype(BF)
        oth[k] = dot(u1[4 + k // 2], g, 0, 0).astype(BF)

    def hidden_back(t):
        fetch_ffn(t, False)
        g_active = dot(gsec[...], ring_a[t % 2], 1, 1)
        g_hidden = (g_active * u2[t].astype(F32)).astype(BF)
        u2[t] = g_hidden
        total = jnp.sum(g_hidden.astype(F32), axis=0, keepdims=True)
        small[pl.ds(9 + 8 * (t // 4) + (t % 4) // 2, 1), span(t % 2, TILE)] = total
        acc[...] += dot(g_hidden, ring_b[t % 3], 1, 1)

    def in_tiles(k):
        j = k - 8
        a = nlow[:, span(j % 2, TILE)]
        own[k] = dot(a, u2[j // 2], 0, 0).astype(BF)
        oth[k] = dot(a, u2[4 + j // 2], 0, 0).astype(BF)

    def norm_one_back(r, b):
        g_normed, hat = acc[r, :], xhat[r, :]
        scaled = g_normed * gain1
        g_first = rs1[r, 0:1] * (scaled - mean(scaled) - hat * mean(scaled * hat))
        low = g_first.astype(BF)
        acc[r, :] = g_first
        gsec[r, :] = low
        small[0:1, :] += jnp.sum(g_normed * hat, axis=0, keepdims=True)
        small[1:2, :] += jnp.sum(g_normed, axis=0, keepdims=True)
        small[2:3, :] += jnp.sum(low.astype(F32), axis=0, keepdims=True)

    def attend_back(h, p):
        lanes = span(p, 128)
        wide = span(h * pairs + p, 128)
        q2, k2, v2 = qkv[h, 0, :, lanes], qkv[h, 1, :, lanes], qkv[h, 2, :, lanes]
        g = gctx[:, wide].astype(F32) * inv[h, :, lanes]
        low = g.astype(BF)
        less = pltpu.roll(-(g * ctx[:, wide].astype(F32)), HEAD, 1).astype(BF)
        g_q, g_k, g_v = [], [], []
        for head in range(2):
            mine = low_lanes if head == 0 else jnp.logical_not(low_lanes)
            e = u1[2 * p + head]
            g_scores = (dot(jnp.where(mine, low, less), jnp.where(mine, v2, one), 1, 1) * e.astype(F32)).astype(BF)
            g_q.append(dot(g_scores, k2, 1, 0))
            rows = slice(head * HEAD, head * HEAD + HEAD)
            g_k.append(dot(q2, g_scores, 0, 0)[rows])
            g_v.append(dot(low, e, 0, 0)[rows])
        qkv[h, 0, :, lanes] = (jnp.where(low_lanes, g_q[0], g_q[1]) * scale).astype(BF)
        qkv[h, 1, :, lanes] = jnp.concatenate(g_k, axis=0).T.astype(BF)
        qkv[h, 2, :, lanes] = jnp.concatenate(g_v, axis=0).T.astype(BF)

    fetch_ffn(0, True)

    def iteration(t, _):
        @pl.when(t < 8)
        def _():
            down_tiles(t)
        @pl.when((t >= 8) & (t < 16))
        def _():
            in_tiles(t)
        @pl.when((t >= 16) & (t < 18))
        def _():
            g = gsec[:, span(t - 16, TILE)]
            own[t] = dot(ctx[:, :half_w], g, 0, 0).astype(BF)
            oth[t] = dot(ctx[:, half_w:], g, 0, 0).astype(BF)
        @pl.when((t >= 18) & (t < 24))
        def _():
            j = t - 18
            a = xv[:, span(j % 2, TILE)]
            own[t] = dot(a, qkv[0, j // 2], 0, 0).astype(BF)
            oth[t] = dot(a, qkv[1, j // 2], 0, 0).astype(BF)
        reduce_step(t, (0, 1, 2, 3))
        @pl.when(t < 8)
        def _():
            @pl.when(t < 7)
            def _():
                fetch_ffn(t + 1, True)
            hidden_back(t)
        @pl.when(t == 8)
        def _():
            e_copy(0, True).start()
            fetch_out(0).start()
            fetch_out(1).start()
            blocks(norm_one_back)
        @pl.when(t == 9)
        def _():
            for h in range(2):
                fetch_out(h).wait()
                gctx[:, h * half_w : (h + 1) * half_w] = dot(gsec[...], ring_a[h], 1, 1).astype(BF)
            e_copy(0, True).wait()
        for first, h in ((10, 0), (13, 1)):
            @pl.when((t >= first) & (t < first + 2))
            def _():
                def body(p, _):
                    attend_back(h, 2 * (t - first) + p)
                    return 0
                lax.fori_loop(0, 2, body, 0)
            @pl.when(t == first + 1)
            def _():
                if h == 0:
                    e_copy(1, True).start()
                for i in (0, 2):
                    total = jnp.sum(qkv[h, i].astype(F32), axis=0, keepdims=True)
                    small[8 + 8 * h : 9 + 8 * h, (i // 2) * TILE : (i // 2 + 1) * TILE] = total
        @pl.when(t == 12)
        def _():
            e_copy(1, True).wait()
        for h in range(2):
            first = 15 + 2 * h
            @pl.when(t == first)
            def _():
                for i in range(3):
                    fetch_qkv(h, i).start()
            @pl.when(t == first + 1)
            def _():
                for i in range(3):
                    fetch_qkv(h, i).wait()
                    acc[...] += dot(qkv[h, i], ring_b[i], 1, 1)
        @pl.when(t == 19)
        def _():
            def last(r, b):
                gin_ref[r, :] = acc[r, :].astype(BF)
            blocks(last)
        for i in range(6):
            @pl.when(t == 16 + i)
            def _():
                small_step(i)
        reduce_step(t, range(4, 8))
        return 0

    lax.fori_loop(0, CHUNKS + 7, iteration, 0)
    small_out[...] = small[0:16, :]


def layer(lengths, inputs, cotangent, wq, w_out, w_in, w_down, vectors):
    seq, width = inputs.shape
    half = TILE // 2
    vm, dma = pltpu.VMEM, pltpu.SemaphoreType.DMA
    anywhere, inside = pl.BlockSpec(memory_space=pl.ANY), pl.BlockSpec(memory_space=pltpu.VMEM)
    like = lambda a: jax.ShapeDtypeStruct(a.shape, a.dtype)
    tile_shape = (TILE, TILE)
    return pl.pallas_call(
        layer_kernel,
        out_shape=[
            pltpu.VMEM(inputs.shape, BF), pltpu.VMEM(inputs.shape, BF), pltpu.VMEM((CHUNKS,) + tile_shape, BF),
            pltpu.VMEM((16, width), F32),
            like(wq), like(w_out), like(w_in), like(w_down),
            jax.ShapeDtypeStruct((16,) + tile_shape, BF),
        ],
        in_specs=[pl.BlockSpec(memory_space=pltpu.SMEM)] + [anywhere] * 6 + [inside] * 8,
        out_specs=[inside] * 4 + [anywhere] * 5,
        scratch_shapes=[
            vm((seq, width), BF), vm((seq, width), BF), vm((seq, width), BF), vm((seq, width), BF), vm((seq, width), BF),
            vm((2, 3) + tile_shape, BF), vm((2,) + tile_shape, F32),
            vm((seq, width), F32), vm((seq, 128), F32), vm((seq, width), F32),
            vm((8,) + tile_shape, BF), vm((8,) + tile_shape, BF),
            vm((CHUNKS,) + tile_shape, BF),
            vm((RING, 2, half, TILE), BF), vm((RING, half, TILE), BF),
            vm((RING, half // 2, TILE), BF), vm((RING, 3, half // 8, TILE), BF),
            vm((2, TILE, width), BF), vm((3, width, TILE), BF),
            vm((8, width), F32), vm((8, TILE), F32), vm((8, TILE), F32), vm((24, width), F32), vm((24, width), F32),
            vm((16, width), F32), vm((16, width), F32), vm((16, width), F32), vm((16, width), F32),
            dma((2,)), dma((2, CHUNKS)), dma((2,)), dma((3,)), dma((2,)),
            dma((9, 12)), dma((9, 12)), dma((RING, MESSAGES)), dma((RING, MESSAGES)), dma((6,)), dma((6,)),
        ],
        compiler_params=pltpu.CompilerParams(
            collective_id=1, has_side_effects=True, vmem_limit_bytes=47 << 20
        ),
    )(lengths, inputs, cotangent, wq, w_out, w_in, w_down, *vectors)


def widen_kernel(
    tiles, out_in, gin_in, sums, down, within, out, three, out_out, gin_out,
    b_qv, b_out, gain1, shift1, b_in, b_down, gain2, shift2, wide, out_sem, pass_sem,
):
    leave = [pltpu.make_async_copy(ref, to, pass_sem.at[i]) for i, (ref, to) in enumerate(((out_in, out_out), (gin_in, gin_out)))]
    for copy in leave:
        copy.start()
    width, half = sums.shape[1], b_qv.shape[1]
    for ref, row in ((gain1, 0), (shift1, 1), (b_out, 2), (gain2, 3), (shift2, 4), (b_down, 5)):
        ref[...] = sums[row, :]
    for i in range(2):
        b_qv[i : i + 1, :] = sums[8:9, i * half : (i + 1) * half]
        b_in[i * width : (i + 1) * width] = sums[9 + i, :]

    def store(k):
        which, where = tile_place(k)
        return pltpu.make_async_copy(wide.at[k % RING], (down, within, out, three)[which].at[where], out_sem.at[k % RING])

    stores = [store(k) for k in range(CHUNKS)]
    for k in range(CHUNKS):
        if k >= RING:
            stores[k - RING].wait()
        def body(i, _):
            r = span(i, 32)
            wide[k % RING, r, :] = tiles[k, r, :].astype(F32)
            return 0
        lax.fori_loop(0, TILE // 32, body, 0)
        stores[k].start()
    for copy in stores[CHUNKS - RING :] + leave:
        copy.wait()


def widen(tiles, output, grad_inputs, sums, half_hidden, width, half_width):
    tile, vm, dma = (TILE, TILE), pltpu.VMEM, pltpu.SemaphoreType.DMA
    anywhere, inside = pl.BlockSpec(memory_space=pl.ANY), pl.BlockSpec(memory_space=pltpu.VMEM)
    wide = lambda *shape: jax.ShapeDtypeStruct(shape, F32)
    return pl.pallas_call(
        widen_kernel,
        out_shape=[
            wide(half_hidden, width), wide(width, half_hidden), wide(half_width, width), wide(3, width, half_width),
            jax.ShapeDtypeStruct(output.shape, output.dtype), jax.ShapeDtypeStruct(output.shape, output.dtype),
            wide(2, half_width), wide(width), wide(width), wide(width), wide(half_hidden), wide(width), wide(width), wide(width),
        ],
        in_specs=[inside] * 4,
        out_specs=[anywhere] * 6 + [inside] * 8,
        scratch_shapes=[
            vm((RING,) + tile, F32), dma((RING,)), dma((2,)),
        ],
        compiler_params=pltpu.CompilerParams(vmem_limit_bytes=16 << 20),
    )(tiles, output, grad_inputs, sums)


def split_by_sequence(
    inputs, lengths, w_qkv, b_qv, w_out, b_out, gain_one, shift_one, w_in, b_in, w_down, b_down, gain_two, shift_two,
    cotangent,
):
    rows, width = inputs.shape
    half_width, half_hidden = w_qkv.shape[2], w_in.shape[1]
    wq = w_qkv.transpose(1, 0, 2)
    vectors = (b_out, gain_one, shift_one, b_down, gain_two, shift_two, b_qv, b_in)
    made = layer(lengths, inputs, cotangent, wq, w_out, w_in, w_down, vectors)
    output, grad_inputs, tiles, sums = made[:4]
    (
        g_w_down, g_w_in, g_w_out, g_w_qkv, output, grad_inputs,
        g_b_qv, g_b_out, g_gain_one, g_shift_one, g_b_in, g_b_down, g_gain_two, g_shift_two,
    ) = widen(tiles, output, grad_inputs, sums, half_hidden, width, half_width)
    return (
        output, grad_inputs, g_w_qkv.transpose(1, 0, 2), g_b_qv, g_w_out, g_b_out, g_gain_one, g_shift_one,
        g_w_in, g_b_in, g_w_down, g_b_down, g_gain_two, g_shift_two,
    )


def solution(mesh):
    small_mesh = mesh.shape["tensor"] == 2 and mesh.shape["dp"] == 2 * N_X * N_Z
    step = split_by_sequence if small_mesh else general
    in_specs = (
        P(("dp", "tensor"), None),
        P("dp"),
        P(None, None, "tensor"),
        P(None, "tensor"),
        P("tensor", None),
        P(),
        P(),
        P(),
        P(None, "tensor"),
        P("tensor"),
        P("tensor", None),
        P(),
        P(),
        P(),
        P(("dp", "tensor"), None),
    )
    out_specs = (
        P(("dp", "tensor"), None),
        P(("dp", "tensor"), None),
        P(None, None, "tensor"),
        P(None, "tensor"),
        P("tensor", None),
        P(),
        P(),
        P(),
        P(None, "tensor"),
        P("tensor"),
        P("tensor", None),
        P(),
        P(),
        P(),
    )
    return jax.shard_map(step, mesh=mesh, in_specs=in_specs, out_specs=out_specs, check_vma=False)
```

```python
import jax
import jax.numpy as jnp
from jax import lax
from jax.experimental import pallas as pl
from jax.experimental.pallas import tpu as pltpu
from jax.sharding import PartitionSpec as P

MESH = pl.DeviceIdType.MESH
N_Z, N_X = 4, 2
TILE = 512
MESSAGES = 12
VMEM_BYTES = 63 << 20

HEAD = 64
SEQ = 512
SEQ_DEV = 2


EPSILON = 1e-12
NEG_FILL = -1000000000.0


def gelu_exact(values):
    return jax.nn.gelu(values, approximate=False)


def norm_forward(values, gain_vec, shift_vec):
    center = values - jnp.mean(values, axis=-1, keepdims=True)
    spread = jnp.mean(center * center, axis=-1, keepdims=True)
    inverse = lax.rsqrt(spread + EPSILON)
    scaled = center * inverse
    return (scaled * gain_vec + shift_vec, scaled, inverse)


def norm_backward(grad_out, scaled, inverse, gain_vec):
    grad_scaled = grad_out * gain_vec
    mean_one = jnp.mean(grad_scaled, axis=-1, keepdims=True)
    mean_two = jnp.mean(grad_scaled * scaled, axis=-1, keepdims=True)
    grad_in = inverse * (grad_scaled - mean_one - scaled * mean_two)
    return (grad_in, jnp.sum(grad_out * scaled, axis=0), jnp.sum(grad_out, axis=0))


def masked_scores(queries, key_rows, length):
    score_scale = HEAD ** (-0.5)
    scores = (
        jnp.einsum("qhe,khe->hqk", queries, key_rows, preferred_element_type=jnp.float32)
        * score_scale
    )
    key_valid = (jnp.arange(SEQ) < length)[None, None, :]
    return jnp.where(key_valid, scores, NEG_FILL)


def attend_forward(element):
    queries, key_rows, value_rows, length = element
    scores = masked_scores(queries, key_rows, length)
    peak_score = jnp.max(scores, axis=-1, keepdims=True)
    shifted_exp = jnp.exp(scores - peak_score)
    denominator = jnp.sum(shifted_exp, axis=-1, keepdims=True)
    probability = (shifted_exp / denominator).astype(jnp.bfloat16)
    context = jnp.einsum(
        "hqk,khe->qhe", probability, value_rows, preferred_element_type=jnp.float32
    )
    return (context.astype(jnp.bfloat16), (peak_score + jnp.log(denominator))[..., 0])


def attend_backward(element):
    queries, key_rows, value_rows, length, log_total, grad_context = element
    score_scale = HEAD ** (-0.5)
    scores = masked_scores(queries, key_rows, length)
    probability = jnp.exp(scores - log_total[..., None])
    grad_prob = jnp.einsum(
        "qhe,khe->hqk", grad_context, value_rows, preferred_element_type=jnp.float32
    )
    grad_value = jnp.einsum(
        "hqk,qhe->khe",
        probability.astype(jnp.bfloat16),
        grad_context,
        preferred_element_type=jnp.float32,
    )
    grad_scores = probability * (
        grad_prob - jnp.sum(probability * grad_prob, axis=-1, keepdims=True)
    )
    grad_scores = grad_scores.astype(jnp.bfloat16)
    grad_query = (
        jnp.einsum("hqk,khe->qhe", grad_scores, key_rows, preferred_element_type=jnp.float32)
        * score_scale
    )
    grad_key = (
        jnp.einsum("hqk,qhe->khe", grad_scores, queries, preferred_element_type=jnp.float32)
        * score_scale
    )
    return jnp.stack([grad_query, grad_key, grad_value], axis=1).astype(jnp.bfloat16)


def row_mask(lengths, rows_dev):
    places = lax.axis_index("tensor") * rows_dev + jnp.arange(rows_dev)
    sequence_of = places // SEQ
    offset = places % SEQ
    matches = sequence_of[:, None] == jnp.arange(lengths.shape[0])[None, :]
    limit_rows = jnp.sum(jnp.where(matches, lengths[None, :], 0), axis=1)
    return (offset < limit_rows).astype(jnp.float32)[:, None]


def forward_pass(inputs, lengths, weights):
    (
        w_qkv,
        b_qv,
        w_out,
        b_out,
        gain_one,
        shift_one,
        w_in,
        b_in,
        w_down,
        b_down,
        gain_two,
        shift_two,
    ) = weights
    width_dev = w_qkv.shape[2]
    gathered = lax.all_gather(inputs, "tensor", axis=0, tiled=True)
    bias_three = jnp.stack([b_qv[0], jnp.zeros_like(b_qv[0]), b_qv[1]]).astype(jnp.float32)
    projected = (
        jnp.einsum("td,dcf->tcf", gathered, w_qkv, preferred_element_type=jnp.float32) + bias_three
    ).astype(jnp.bfloat16)
    shaped = projected.reshape(SEQ_DEV, SEQ, 3, width_dev // HEAD, HEAD)
    context, log_total = lax.map(
        attend_forward, (shaped[:, :, 0], shaped[:, :, 1], shaped[:, :, 2], lengths)
    )
    context = context.reshape(SEQ_DEV * SEQ, width_dev)
    segment = context
    branch = lax.psum_scatter(
        jnp.dot(segment, w_out, preferred_element_type=jnp.float32).astype(jnp.bfloat16),
        "tensor",
        scatter_dimension=0,
        tiled=True,
    ).astype(jnp.float32) + b_out.astype(jnp.float32)
    normed, scaled_one, inverse_one = norm_forward(
        inputs.astype(jnp.float32) + branch,
        gain_one.astype(jnp.float32),
        shift_one.astype(jnp.float32),
    )
    normed_all = lax.all_gather(normed.astype(jnp.bfloat16), "tensor", axis=0, tiled=True)
    hidden = jnp.dot(normed_all, w_in, preferred_element_type=jnp.float32) + b_in.astype(
        jnp.float32
    )
    active = gelu_exact(hidden).astype(jnp.bfloat16)
    segment = active
    second = lax.psum_scatter(
        jnp.dot(segment, w_down, preferred_element_type=jnp.float32).astype(jnp.bfloat16),
        "tensor",
        scatter_dimension=0,
        tiled=True,
    ).astype(jnp.float32) + b_down.astype(jnp.float32)
    output, scaled_two, inverse_two = norm_forward(
        normed + second, gain_two.astype(jnp.float32), shift_two.astype(jnp.float32)
    )
    return (
        gathered,
        projected,
        context,
        log_total,
        scaled_one,
        inverse_one,
        normed_all,
        hidden,
        active,
        scaled_two,
        inverse_two,
        output,
    )


def general(
    inputs,
    lengths,
    w_qkv,
    b_qv,
    w_out,
    b_out,
    gain_one,
    shift_one,
    w_in,
    b_in,
    w_down,
    b_down,
    gain_two,
    shift_two,
    cotangent,
):
    weights = (
        w_qkv,
        b_qv,
        w_out,
        b_out,
        gain_one,
        shift_one,
        w_in,
        b_in,
        w_down,
        b_down,
        gain_two,
        shift_two,
    )
    first_pass = forward_pass(inputs, lengths, weights)
    output = first_pass[11].astype(jnp.bfloat16)
    recorded = forward_pass(inputs, lengths, weights)
    (
        gathered,
        projected,
        context,
        log_total,
        scaled_one,
        inverse_one,
        normed_all,
        hidden,
        active,
        scaled_two,
        inverse_two,
        _,
    ) = recorded
    rows_dev = inputs.shape[0]
    width_dev = w_qkv.shape[2]
    grad_out = cotangent.astype(jnp.float32) * row_mask(lengths, rows_dev)
    grad_two, grad_gain_two, grad_shift_two = norm_backward(
        grad_out, scaled_two, inverse_two, gain_two.astype(jnp.float32)
    )
    grad_second = grad_two.astype(jnp.bfloat16)
    grad_b_down = jnp.sum(grad_second.astype(jnp.float32), axis=0)
    second_all = lax.all_gather(grad_second, "tensor", axis=0, tiled=True)
    grad_w_down = jnp.einsum("tf,td->fd", active, second_all, preferred_element_type=jnp.float32)
    grad_active = jnp.einsum("td,fd->tf", second_all, w_down, preferred_element_type=jnp.float32)
    _, gelu_pull = jax.vjp(gelu_exact, hidden)
    grad_hidden = gelu_pull(grad_active)[0].astype(jnp.bfloat16)
    grad_b_in = jnp.sum(grad_hidden.astype(jnp.float32), axis=0)
    grad_w_in = jnp.einsum("td,tf->df", normed_all, grad_hidden, preferred_element_type=jnp.float32)
    segment = grad_hidden
    grad_normed = grad_two + lax.psum_scatter(
        jnp.einsum("tf,df->td", segment, w_in, preferred_element_type=jnp.float32).astype(
            jnp.bfloat16
        ),
        "tensor",
        scatter_dimension=0,
        tiled=True,
    ).astype(jnp.float32)
    grad_first, grad_gain_one, grad_shift_one = norm_backward(
        grad_normed, scaled_one, inverse_one, gain_one.astype(jnp.float32)
    )
    grad_branch = grad_first.astype(jnp.bfloat16)
    grad_b_out = jnp.sum(grad_branch.astype(jnp.float32), axis=0)
    branch_all = lax.all_gather(grad_branch, "tensor", axis=0, tiled=True)
    grad_w_out = jnp.einsum("tf,td->fd", context, branch_all, preferred_element_type=jnp.float32)
    grad_context = jnp.einsum(
        "td,fd->tf", branch_all, w_out, preferred_element_type=jnp.float32
    ).astype(jnp.bfloat16)
    heads_dev = width_dev // HEAD
    shaped = projected.reshape(SEQ_DEV, SEQ, 3, heads_dev, HEAD)
    grad_shaped = grad_context.reshape(SEQ_DEV, SEQ, heads_dev, HEAD)
    grad_proj = lax.map(
        attend_backward,
        (shaped[:, :, 0], shaped[:, :, 1], shaped[:, :, 2], lengths, log_total, grad_shaped),
    )
    grad_proj = grad_proj.reshape(SEQ_DEV * SEQ, 3, width_dev)
    grad_w_qkv = jnp.einsum("td,tcf->dcf", gathered, grad_proj, preferred_element_type=jnp.float32)
    grad_b_qv = jnp.sum(grad_proj[:, 0::2].astype(jnp.float32), axis=0)
    segment = grad_proj
    grad_inputs = (
        grad_first
        + lax.psum_scatter(
            jnp.einsum("tcf,dcf->td", segment, w_qkv, preferred_element_type=jnp.float32).astype(
                jnp.bfloat16
            ),
            "tensor",
            scatter_dimension=0,
            tiled=True,
        ).astype(jnp.float32)
    ).astype(jnp.bfloat16)
    small_terms = jnp.stack(
        [grad_gain_one, grad_shift_one, grad_b_out, grad_gain_two, grad_shift_two, grad_b_down]
    )
    grad_w_qkv, grad_b_qv, grad_w_out, grad_w_in, grad_b_in, grad_w_down, small_terms = (
        lax.psum(grad_w_qkv.astype(jnp.bfloat16), "dp").astype(jnp.float32),
        lax.psum(grad_b_qv.astype(jnp.bfloat16), "dp").astype(jnp.float32),
        lax.psum(grad_w_out.astype(jnp.bfloat16), "dp").astype(jnp.float32),
        lax.psum(grad_w_in.astype(jnp.bfloat16), "dp").astype(jnp.float32),
        lax.psum(grad_b_in.astype(jnp.bfloat16), "dp").astype(jnp.float32),
        lax.psum(grad_w_down.astype(jnp.bfloat16), "dp").astype(jnp.float32),
        lax.psum(small_terms.astype(jnp.bfloat16), "dp").astype(jnp.float32),
    )
    small_sums = lax.psum(small_terms, "tensor")
    return (
        output,
        grad_inputs,
        grad_w_qkv,
        grad_b_qv,
        grad_w_out,
        small_sums[2],
        small_sums[0],
        small_sums[1],
        grad_w_in,
        grad_b_in,
        grad_w_down,
        small_sums[5],
        small_sums[3],
        small_sums[4],
    )


def place():
    dp = lax.axis_index("dp")
    return dp // (2 * N_X), (dp // 2) % N_X, dp % 2, lax.axis_index("tensor")


def at(z, x, c, y):
    return ((z * N_X + x) * 2 + c, y)


def greet(peers):
    barrier = pltpu.get_barrier_semaphore()
    for peer in peers:
        pl.semaphore_signal(barrier, inc=1, device_id=peer, device_id_type=MESH)
    pl.semaphore_wait(barrier, len(peers))


def copy_to(src, dst, send_sem, recv_sem, peer):
    return pltpu.make_async_remote_copy(
        src_ref=src, dst_ref=dst, send_sem=send_sem, recv_sem=recv_sem,
        device_id=peer, device_id_type=MESH,
    )


CHUNKS = 24
RING = 4
BF, F32 = jnp.bfloat16, jnp.float32
ROWS_AT_ONCE = 128


def dot(a, b, ca, cb):
    return lax.dot_general(a, b, (((ca,), (cb,)), ((), ())), preferred_element_type=F32)


def span(index, size):
    return pl.ds(pl.multiple_of(index * size, size), size)


def tile_place(k):
    if k < 8:
        return 0, (slice(k // 2 * TILE, (k // 2 + 1) * TILE), slice(k % 2 * TILE, (k % 2 + 1) * TILE))
    if k < 16:
        k -= 8
        return 1, (slice(k % 2 * TILE, (k % 2 + 1) * TILE), slice(k // 2 * TILE, (k // 2 + 1) * TILE))
    if k < 18:
        k -= 16
        return 2, (slice(0, TILE), slice(k * TILE, (k + 1) * TILE))
    k -= 18
    return 3, (k // 2, slice(k % 2 * TILE, (k % 2 + 1) * TILE), slice(0, TILE))


def layer_kernel(
    lengths, x_hbm, cot_hbm, wq_own, wo_own, wi_own, wd_own, in1, in2, in3, in4, in5, in6, in_qv, in_hidden,
    out_ref, gin_ref, oth, small_out, wq_oth, wo_oth, wi_oth, wd_oth, e_hbm,
    xv, nlow, gsec, gctx, ctx, qkv, inv, xhat, rs1, acc, u1, u2, own, r1, ry, rx, rz,
    ring_a, ring_b, vec, bias_own, bias_oth, small, s0, s1, s2, s3, s4,
    load_sem, w_sem, a_sem, b_sem, e_sem, g_send, g_recv, send, recv, small_send, small_recv,
):
    z, x, c, y = place()
    zb = z % 2
    z_of = [(z + d) % N_Z for d in (1, 2, 3)]
    to_c, to_y, to_x = at(z, x, 1 - c, y), at(z, x, c, 1 - y), at(z, 1 - x, c, y)
    to_z = [at(v, x, c, y) for v in z_of]
    to_zp, to_zq = at(z + 1 - 2 * zb, x, c, y), at((z + 2) % N_Z, x, c, y)
    seq, width = xv.shape
    half_w = width // 2

    load_x = pltpu.make_async_copy(x_hbm, xv, load_sem.at[0])
    load_cot = pltpu.make_async_copy(cot_hbm, gsec, load_sem.at[1])
    load_x.start()
    load_cot.start()
    for row, ref in enumerate((in1, in2, in3, in4, in5, in6)):
        vec[row : row + 1, :] = ref[...].astype(F32).reshape(1, width)
    bias_own[0:2, :] = in_qv[...].astype(F32)
    bias_own[2:6, :] = in_hidden[...].astype(F32).reshape(4, TILE)

    def fetch_qkv(h, i):
        source = (wq_own, wq_oth)[h]
        return pltpu.make_async_copy(source.at[i], ring_b.at[i], b_sem.at[i])

    def fetch_out(h):
        return pltpu.make_async_copy((wo_own, wo_oth)[h], ring_a.at[h], a_sem.at[h])

    def fetch_in(h, f, slot):
        return pltpu.make_async_copy((wi_own, wi_oth)[h].at[:, span(f, TILE)], ring_b.at[slot], b_sem.at[slot])

    def fetch_down(h, f, slot):
        return pltpu.make_async_copy((wd_own, wd_oth)[h].at[span(f, TILE)], ring_a.at[slot], a_sem.at[slot])

    def weight_load(h, k):
        which, where = tile_place(k)
        source = ((wd_own, wi_own, wo_own, wq_own), (wd_oth, wi_oth, wo_oth, wq_oth))[h][which]
        return pltpu.make_async_copy(source.at[where], (own, oth)[h].at[k], w_sem.at[h, k])

    for k in (*range(18, 24), *range(8, 16), *range(0, 8), 16, 17):
        weight_load(0, k).start()

    greet([to_c, to_y, to_x] + to_z)

    cut = wi_own.shape[1] // 2
    deep = wd_own.shape[0] // 2
    arrays = [(wq_own.at[i], wq_oth.at[i]) for i in range(3)] + [(wo_own, wo_oth)]
    arrays += [(wi_own.at[:, j * cut : (j + 1) * cut], wi_oth.at[:, j * cut : (j + 1) * cut]) for j in range(2)]
    arrays += [(wd_own.at[j * deep : (j + 1) * deep], wd_oth.at[j * deep : (j + 1) * deep]) for j in range(2)]
    loads_of = [(18, 19), (20, 21), (22, 23), (16, 17), (8, 9, 10, 11), (12, 13, 14, 15), (0, 1, 2, 3), (4, 5, 6, 7)]
    count = len(arrays)

    def gather_message(n, kind):
        size = arrays[n][0].shape[0] // 2
        size_part = size // 8 - (16 if n >= 4 else 0)
        near_a, near_b = 2 * zb, 4 + 2 * x
        far_a, far_b = 2 * (1 - zb), 4 + 2 * (1 - x)
        one_a, one_b = 2 * zb + x, 4 + 2 * x + zb
        first, parts, peer = [
            (one_a, 1, to_y), (one_b, 1, to_y), (one_a, 1, to_x), (one_b, 1, to_zp),
            (near_a, 2, to_zp), (near_b, 2, to_x), (near_a, 2, to_c), (near_b, 2, to_c), (far_a, 2, to_c), (far_b, 2, to_c),
            (8, 0, to_y), (8, 0, to_c),
        ][kind]
        length_rows = parts * size_part if parts else size - 8 * size_part
        rows = pl.ds(pl.multiple_of(c * size + first * size_part, 8), length_rows)
        source = arrays[n][0 if kind in (0, 1, 10) else 1]
        return copy_to(source.at[rows], arrays[n][1].at[rows], g_send.at[n, kind], g_recv.at[n, kind], peer)

    def gather_stage(n, step):
        if step == 0:
            gather_message(n, 0).wait_recv()
            gather_message(n, 2).start()
            gather_message(n, 1).wait_recv()
            gather_message(n, 3).start()
        if step == 1:
            gather_message(n, 2).wait_recv()
            gather_message(n, 4).start()
            gather_message(n, 6).start()
            gather_message(n, 3).wait_recv()
            gather_message(n, 5).start()
            gather_message(n, 7).start()
        if step == 2:
            gather_message(n, 4).wait_recv()
            gather_message(n, 8).start()
            gather_message(n, 5).wait_recv()
            gather_message(n, 9).start()
            if n >= 4:
                gather_message(n, 10).wait_recv()
                gather_message(n, 11).start()
        if step == 3:
            kinds = range(12 if n >= 4 else 10)
            for kind in kinds:
                if kind >= 6 and kind != 10:
                    gather_message(n, kind).wait_recv()
            for k in loads_of[n]:
                weight_load(1, k).start()
            for kind in kinds:
                gather_message(n, kind).wait_send()

    def progress(slot):
        for step in range(4):
            if 0 <= slot - step < count:
                gather_stage(slot - step, step)

    send_bias = copy_to(bias_own, bias_oth, g_send.at[count, 0], g_recv.at[count, 0], to_y)
    send_bias.start()
    for n in (0, 1, 2, 3, 4, 5, -4, 6, -5, 7, -6, -7):
        for kind in (0, 1) if n >= 0 else (10,):
            gather_message(abs(n), kind).start()

    length = lengths[y]
    key_fill = jnp.where(lax.broadcasted_iota(jnp.int32, (1, seq), 1) < length, 0.0, NEG_FILL)
    low_lanes = lax.broadcasted_iota(jnp.int32, (1, 128), 1) < HEAD
    one, zero = jnp.ones((), BF), jnp.zeros((), BF)
    scale = HEAD ** (-0.5)
    pairs = half_w // 128

    def project(h):
        bias = (bias_own, bias_oth)[h]
        for i in range(3):
            for k in (18 + 2 * i, 19 + 2 * i):
                weight_load(h, k).wait()
            value = dot(xv[...], (own, oth)[h][18 + 2 * i : 20 + 2 * i].reshape(width, TILE), 1, 0)
            if i == 0:
                qkv[h, 0] = (value + bias[0:1, :]).astype(BF) * jnp.asarray(scale, BF)
            if i == 1:
                qkv[h, 1] = value.astype(BF)
            if i == 2:
                qkv[h, 2] = (value + bias[1:2, :]).astype(BF)

    def attend(h, p, e_ref):
        lanes = span(p, 128)
        q2, k2, v2 = qkv[h, 0, :, lanes], qkv[h, 1, :, lanes], qkv[h, 2, :, lanes]
        parts = []
        for head in range(2):
            mine = low_lanes if head == 0 else jnp.logical_not(low_lanes)
            scores = dot(jnp.where(mine, q2, zero), k2, 1, 1) + key_fill
            peak = jnp.max(scores, axis=-1, keepdims=True)
            e = jnp.exp(scores - peak).astype(BF)
            e_ref[2 * p + head] = e
            parts.append(dot(e, jnp.where(mine, v2, one), 1, 0))
        total = pltpu.roll(jnp.where(low_lanes, parts[1], parts[0]), HEAD, 1)
        inverse = 1.0 / total
        inv[h, :, lanes] = inverse
        ctx[:, span(h * pairs + p, 128)] = (jnp.where(low_lanes, parts[0], parts[1]) * inverse).astype(BF)

    def attend_half(h, slots):
        def body(p, _):
            attend(h, p, (u1, u2)[h])
            for at_pair, slot in slots:
                @pl.when(p == at_pair)
                def _():
                    progress(slot)
            return 0
        lax.fori_loop(0, pairs, body, 0)

    def e_copy(h, back):
        ref, buf = e_hbm.at[pl.ds(h * 8, 8)], (u1 if back else (u1, u2)[h])
        return pltpu.make_async_copy(ref, buf, e_sem.at[h]) if back else pltpu.make_async_copy(buf, ref, e_sem.at[h])

    def out_project(h):
        for d in range(2):
            weight_load(h, 16 + d).wait()
            term = dot(ctx[:, h * half_w : (h + 1) * half_w], (own, oth)[h][16 + d], 1, 0)
            lanes = slice(d * TILE, (d + 1) * TILE)
            acc[:, lanes] = term if h == 0 else acc[:, lanes] + term

    load_x.wait()
    project(0)
    attend_half(0, ((1, 0), (3, 1)))
    e_copy(0, False).start()
    out_project(0)
    for slot in (2, 3, 4, 5):
        progress(slot)
    send_bias.wait()
    project(1)
    attend_half(1, ((1, 6),))
    e_copy(1, False).start()
    out_project(1)

    def blocks(body):
        def run(b, _):
            body(span(b, ROWS_AT_ONCE), b)
            return 0
        lax.fori_loop(0, seq // ROWS_AT_ONCE, run, 0)

    def mean(v):
        return jnp.sum(v, axis=-1, keepdims=True) * (1.0 / width)

    small[...] = jnp.zeros_like(small)
    b_out, gain1, shift1 = vec[0:1, :], vec[1:2, :], vec[2:3, :]
    b_down, gain2, shift2 = vec[3:4, :], vec[4:5, :], vec[5:6, :]

    def norm_one(r, b):
        v = xv[r, :].astype(F32) + (acc[r, :] + b_out)
        center = v - mean(v)
        inverse = lax.rsqrt(mean(center * center) + EPSILON)
        hat = center * inverse
        xhat[r, :] = hat
        rs1[r, :] = jnp.broadcast_to(inverse, (ROWS_AT_ONCE, 128))
        nlow[r, :] = (hat * gain1 + shift1).astype(BF)
    blocks(norm_one)
    e_copy(0, False).wait()
    e_copy(1, False).wait()
    progress(7)

    def hidden_half(h, slots):
        bias, weights = (bias_own, bias_oth)[h], (own, oth)[h]
        for f in range(4):
            for k in (8 + 2 * f, 9 + 2 * f):
                weight_load(h, k).wait()
            hidden = dot(nlow[...], weights[8 + 2 * f : 10 + 2 * f].reshape(width, TILE), 1, 0) + bias[2 + f : 3 + f, :]
            cdf = 0.5 + 0.5 * lax.erf(hidden * 0.7071067811865476)
            u1[4 * h + f] = (hidden * cdf).astype(BF)
            u2[4 * h + f] = (cdf + hidden * (jnp.exp(hidden * hidden * -0.5) * 0.3989422804014327)).astype(BF)
            if f in slots:
                progress(slots[f])

    def down_half(h, tiles, clear=False):
        for f in tiles:
            for d in range(2):
                weight_load(h, 2 * f + d).wait()
                term = dot(u1[4 * h + f], (own, oth)[h][2 * f + d], 1, 0)
                lanes = slice(d * TILE, (d + 1) * TILE)
                acc[:, lanes] = term if clear and f == tiles[0] else acc[:, lanes] + term

    hidden_half(0, {})
    down_half(0, (0, 1), True)
    progress(8)
    down_half(0, (2, 3))
    hidden_half(1, {3: 9})
    down_half(1, (0, 1))
    progress(10)
    down_half(1, (2, 3))

    load_cot.wait()
    valid_limit = lengths[y]

    def norm_two(r, b):
        normed = xhat[r, :] * gain1 + shift1
        v = normed + (acc[r, :] + b_down)
        center = v - mean(v)
        inverse = lax.rsqrt(mean(center * center) + EPSILON)
        hat = center * inverse
        out_ref[r, :] = (hat * gain2 + shift2).astype(BF)
        position = b * ROWS_AT_ONCE + lax.broadcasted_iota(jnp.int32, (ROWS_AT_ONCE, 1), 0)
        g_out = jnp.where(position < valid_limit, gsec[r, :].astype(F32), 0.0)
        scaled = g_out * gain2
        g_two = inverse * (scaled - mean(scaled) - hat * mean(scaled * hat))
        low = g_two.astype(BF)
        acc[r, :] = g_two
        gsec[r, :] = low
        small[3:4, :] += jnp.sum(g_out * hat, axis=0, keepdims=True)
        small[4:5, :] += jnp.sum(g_out, axis=0, keepdims=True)
        small[5:6, :] += jnp.sum(low.astype(F32), axis=0, keepdims=True)
    blocks(norm_two)

    half, quarter, part = TILE // 2, TILE // 4, TILE // 16
    c_rows = span(c, half)
    cn_rows = span(1 - c, half)
    x_rows = pl.ds(pl.multiple_of(c * half + x * quarter, quarter), quarter)
    xn_rows = pl.ds(pl.multiple_of(c * half + (1 - x) * quarter, quarter), quarter)

    def z_rows(v):
        return pl.ds(pl.multiple_of(c * half + x * quarter + v * part, part), part)

    def message(k, kind):
        slot = k % RING
        if kind == 0: src, dst, peer = own.at[k, cn_rows], r1.at[slot, 0], to_c
        if kind == 1: src, dst, peer = oth.at[k, cn_rows], r1.at[slot, 1], to_c
        if kind == 2: src, dst, peer = oth.at[k, c_rows], ry.at[slot], to_y
        if kind == 3: src, dst, peer = own.at[k, xn_rows], rx.at[slot], to_x
        if 4 <= kind < 7: src, dst, peer = own.at[k, z_rows(z_of[kind - 4])], rz.at[slot, kind - 4], to_z[kind - 4]
        if 7 <= kind < 10: src, dst, peer = oth.at[k, z_rows(z)], oth.at[k, z_rows(z)], to_z[kind - 7]
        if kind == 10: src, dst, peer = oth.at[k, x_rows], oth.at[k, x_rows], to_x
        if kind == 11: src, dst, peer = oth.at[k, c_rows], oth.at[k, c_rows], to_c
        return copy_to(src, dst, send.at[slot, kind], recv.at[slot, kind], peer)

    def add_into(dst, src, n):
        def body(i, _):
            r = span(i, 64)
            dst[r, :] = dst[r, :] + src[r, :]
            return 0
        lax.fori_loop(0, n // 64, body, 0)

    def wait(k, kinds):
        for kind in kinds:
            message(k, kind).wait()

    def reduce_stage(k, s):
        slot = k % RING
        if s == 0:
            message(k, 0).start()
            message(k, 1).start()
        if s == 1:
            wait(k, (0, 1))
            add_into(oth.at[k, c_rows], r1.at[slot, 1], half)
            message(k, 2).start()
            add_into(own.at[k, c_rows], r1.at[slot, 0], half)
        if s == 2:
            wait(k, (2,))
            add_into(own.at[k, c_rows], ry.at[slot], half)
            message(k, 3).start()
        if s == 3:
            wait(k, (3,))
            add_into(own.at[k, x_rows], rx.at[slot], quarter)
            for kind in (4, 5, 6):
                message(k, kind).start()
        if s == 4:
            wait(k, (4, 5, 6))
            total = own[k, z_rows(z), :].astype(F32)
            for d in range(3):
                total = total + rz[slot, d].astype(F32)
            oth[k, z_rows(z), :] = total.astype(BF)
            for kind in (7, 8, 9):
                message(k, kind).start()
        if s == 5:
            wait(k, (7, 8, 9))
            message(k, 10).start()
        if s == 6:
            wait(k, (10,))
            message(k, 11).start()
        if s == 7:
            wait(k, (11,))

    def reduce_step(t, stages):
        for s in stages:
            @pl.when((t >= s) & (t - s < CHUNKS))
            def _():
                reduce_stage(t - s, s)

    def small_messages(i):
        if i == 0:
            return [copy_to(small, s0, small_send.at[0], small_recv.at[0], to_c)]
        if i == 1:
            return [
                copy_to(small.at[pl.ds(0, 8)], s1.at[pl.ds(0, 8)], small_send.at[1], small_recv.at[1], to_y),
                copy_to(small.at[pl.ds(16, 8)], s1.at[pl.ds(8, 8)], small_send.at[2], small_recv.at[2], to_y),
            ]
        got, peer = ((s2, to_x), (s3, to_zp), (s4, to_zq))[i - 2]
        return [copy_to(small.at[pl.ds(0, 16)], got, small_send.at[i + 1], small_recv.at[i + 1], peer)]

    def small_step(i):
        if i > 0:
            for m in small_messages(i - 1):
                m.wait()
            if i == 1:
                small[...] = small[...] + s0[...]
            else:
                small[0:16, :] = small[0:16, :] + (s1, s2, s3, s4)[i - 2][...]
        if i < 5:
            for m in small_messages(i):
                m.start()

    def fetch_ffn(t, start):
        for h in range(2):
            @pl.when((t >= 4 * h) & (t < 4 * h + 4))
            def _():
                b, a = fetch_in(h, t - 4 * h, t % 3), fetch_down(h, t - 4 * h, t % 2)
                if start:
                    b.start()
                    a.start()
                else:
                    b.wait()
                    a.wait()

    def down_tiles(k):
        g = gsec[:, span(k % 2, TILE)]
        own[k] = dot(u1[k // 2], g, 0, 0).astype(BF)
        oth[k] = dot(u1[4 + k // 2], g, 0, 0).astype(BF)

    def hidden_back(t):
        fetch_ffn(t, False)
        g_active = dot(gsec[...], ring_a[t % 2], 1, 1)
        g_hidden = (g_active * u2[t].astype(F32)).astype(BF)
        u2[t] = g_hidden
        total = jnp.sum(g_hidden.astype(F32), axis=0, keepdims=True)
        small[pl.ds(9 + 8 * (t // 4) + (t % 4) // 2, 1), span(t % 2, TILE)] = total
        acc[...] += dot(g_hidden, ring_b[t % 3], 1, 1)

    def in_tiles(k):
        j = k - 8
        a = nlow[:, span(j % 2, TILE)]
        own[k] = dot(a, u2[j // 2], 0, 0).astype(BF)
        oth[k] = dot(a, u2[4 + j // 2], 0, 0).astype(BF)

    def norm_one_back(r, b):
        g_normed, hat = acc[r, :], xhat[r, :]
        scaled = g_normed * gain1
        g_first = rs1[r, 0:1] * (scaled - mean(scaled) - hat * mean(scaled * hat))
        low = g_first.astype(BF)
        acc[r, :] = g_first
        gsec[r, :] = low
        small[0:1, :] += jnp.sum(g_normed * hat, axis=0, keepdims=True)
        small[1:2, :] += jnp.sum(g_normed, axis=0, keepdims=True)
        small[2:3, :] += jnp.sum(low.astype(F32), axis=0, keepdims=True)

    def attend_back(h, p):
        lanes = span(p, 128)
        wide = span(h * pairs + p, 128)
        q2, k2, v2 = qkv[h, 0, :, lanes], qkv[h, 1, :, lanes], qkv[h, 2, :, lanes]
        g = gctx[:, wide].astype(F32) * inv[h, :, lanes]
        low = g.astype(BF)
        less = pltpu.roll(-(g * ctx[:, wide].astype(F32)), HEAD, 1).astype(BF)
        g_q, g_k, g_v = [], [], []
        for head in range(2):
            mine = low_lanes if head == 0 else jnp.logical_not(low_lanes)
            e = u1[2 * p + head]
            g_scores = (dot(jnp.where(mine, low, less), jnp.where(mine, v2, one), 1, 1) * e.astype(F32)).astype(BF)
            g_q.append(dot(g_scores, k2, 1, 0))
            rows = slice(head * HEAD, head * HEAD + HEAD)
            g_k.append(dot(q2, g_scores, 0, 0)[rows])
            g_v.append(dot(low, e, 0, 0)[rows])
        qkv[h, 0, :, lanes] = (jnp.where(low_lanes, g_q[0], g_q[1]) * scale).astype(BF)
        qkv[h, 1, :, lanes] = jnp.concatenate(g_k, axis=0).T.astype(BF)
        qkv[h, 2, :, lanes] = jnp.concatenate(g_v, axis=0).T.astype(BF)

    fetch_ffn(0, True)

    def iteration(t, _):
        @pl.when(t < 8)
        def _():
            down_tiles(t)
        @pl.when((t >= 8) & (t < 16))
        def _():
            in_tiles(t)
        @pl.when((t >= 16) & (t < 18))
        def _():
            g = gsec[:, span(t - 16, TILE)]
            own[t] = dot(ctx[:, :half_w], g, 0, 0).astype(BF)
            oth[t] = dot(ctx[:, half_w:], g, 0, 0).astype(BF)
        @pl.when((t >= 18) & (t < 24))
        def _():
            j = t - 18
            a = xv[:, span(j % 2, TILE)]
            own[t] = dot(a, qkv[0, j // 2], 0, 0).astype(BF)
            oth[t] = dot(a, qkv[1, j // 2], 0, 0).astype(BF)
        reduce_step(t, (0, 1, 2, 3))
        @pl.when(t < 8)
        def _():
            @pl.when(t < 7)
            def _():
                fetch_ffn(t + 1, True)
            hidden_back(t)
        @pl.when(t == 8)
        def _():
            e_copy(0, True).start()
            fetch_out(0).start()
            fetch_out(1).start()
            blocks(norm_one_back)
        @pl.when(t == 9)
        def _():
            for h in range(2):
                fetch_out(h).wait()
                gctx[:, h * half_w : (h + 1) * half_w] = dot(gsec[...], ring_a[h], 1, 1).astype(BF)
            e_copy(0, True).wait()
        for first, h in ((10, 0), (13, 1)):
            @pl.when((t >= first) & (t < first + 2))
            def _():
                def body(p, _):
                    attend_back(h, 2 * (t - first) + p)
                    return 0
                lax.fori_loop(0, 2, body, 0)
            @pl.when(t == first + 1)
            def _():
                if h == 0:
                    e_copy(1, True).start()
                for i in (0, 2):
                    total = jnp.sum(qkv[h, i].astype(F32), axis=0, keepdims=True)
                    small[8 + 8 * h : 9 + 8 * h, (i // 2) * TILE : (i // 2 + 1) * TILE] = total
        @pl.when(t == 12)
        def _():
            e_copy(1, True).wait()
        for h in range(2):
            first = 15 + 2 * h
            @pl.when(t == first)
            def _():
                for i in range(3):
                    fetch_qkv(h, i).start()
            @pl.when(t == first + 1)
            def _():
                for i in range(3):
                    fetch_qkv(h, i).wait()
                    acc[...] += dot(qkv[h, i], ring_b[i], 1, 1)
        @pl.when(t == 19)
        def _():
            def last(r, b):
                gin_ref[r, :] = acc[r, :].astype(BF)
            blocks(last)
        for i in range(6):
            @pl.when(t == 16 + i)
            def _():
                small_step(i)
        reduce_step(t, range(4, 8))
        return 0

    lax.fori_loop(0, CHUNKS + 7, iteration, 0)
    small_out[...] = small[0:16, :]


def layer(lengths, inputs, cotangent, wq, w_out, w_in, w_down, vectors):
    seq, width = inputs.shape
    half = TILE // 2
    vm, dma = pltpu.VMEM, pltpu.SemaphoreType.DMA
    anywhere, inside = pl.BlockSpec(memory_space=pl.ANY), pl.BlockSpec(memory_space=pltpu.VMEM)
    like = lambda a: jax.ShapeDtypeStruct(a.shape, a.dtype)
    tile_shape = (TILE, TILE)
    return pl.pallas_call(
        layer_kernel,
        out_shape=[
            pltpu.VMEM(inputs.shape, BF), pltpu.VMEM(inputs.shape, BF), pltpu.VMEM((CHUNKS,) + tile_shape, BF),
            pltpu.VMEM((16, width), F32),
            like(wq), like(w_out), like(w_in), like(w_down),
            jax.ShapeDtypeStruct((16,) + tile_shape, BF),
        ],
        in_specs=[pl.BlockSpec(memory_space=pltpu.SMEM)] + [anywhere] * 6 + [inside] * 8,
        out_specs=[inside] * 4 + [anywhere] * 5,
        scratch_shapes=[
            vm((seq, width), BF), vm((seq, width), BF), vm((seq, width), BF), vm((seq, width), BF), vm((seq, width), BF),
            vm((2, 3) + tile_shape, BF), vm((2,) + tile_shape, F32),
            vm((seq, width), F32), vm((seq, 128), F32), vm((seq, width), F32),
            vm((8,) + tile_shape, BF), vm((8,) + tile_shape, BF),
            vm((CHUNKS,) + tile_shape, BF),
            vm((RING, 2, half, TILE), BF), vm((RING, half, TILE), BF),
            vm((RING, half // 2, TILE), BF), vm((RING, 3, half // 8, TILE), BF),
            vm((2, TILE, width), BF), vm((3, width, TILE), BF),
            vm((8, width), F32), vm((8, TILE), F32), vm((8, TILE), F32), vm((24, width), F32), vm((24, width), F32),
            vm((16, width), F32), vm((16, width), F32), vm((16, width), F32), vm((16, width), F32),
            dma((2,)), dma((2, CHUNKS)), dma((2,)), dma((3,)), dma((2,)),
            dma((9, 12)), dma((9, 12)), dma((RING, MESSAGES)), dma((RING, MESSAGES)), dma((6,)), dma((6,)),
        ],
        compiler_params=pltpu.CompilerParams(
            collective_id=1, has_side_effects=True, vmem_limit_bytes=47 << 20
        ),
    )(lengths, inputs, cotangent, wq, w_out, w_in, w_down, *vectors)


def widen_kernel(
    tiles, out_in, gin_in, sums, down, within, out, three, out_out, gin_out,
    b_qv, b_out, gain1, shift1, b_in, b_down, gain2, shift2, wide, out_sem, pass_sem,
):
    leave = [pltpu.make_async_copy(ref, to, pass_sem.at[i]) for i, (ref, to) in enumerate(((out_in, out_out), (gin_in, gin_out)))]
    for copy in leave:
        copy.start()
    width, half = sums.shape[1], b_qv.shape[1]
    for ref, row in ((gain1, 0), (shift1, 1), (b_out, 2), (gain2, 3), (shift2, 4), (b_down, 5)):
        ref[...] = sums[row, :]
    for i in range(2):
        b_qv[i : i + 1, :] = sums[8:9, i * half : (i + 1) * half]
        b_in[i * width : (i + 1) * width] = sums[9 + i, :]

    def store(k):
        which, where = tile_place(k)
        return pltpu.make_async_copy(wide.at[k % RING], (down, within, out, three)[which].at[where], out_sem.at[k % RING])

    stores = [store(k) for k in range(CHUNKS)]
    for k in range(CHUNKS):
        if k >= RING:
            stores[k - RING].wait()
        def body(i, _):
            r = span(i, 32)
            wide[k % RING, r, :] = tiles[k, r, :].astype(F32)
            return 0
        lax.fori_loop(0, TILE // 32, body, 0)
        stores[k].start()
    for copy in stores[CHUNKS - RING :] + leave:
        copy.wait()


def widen(tiles, output, grad_inputs, sums, half_hidden, width, half_width):
    tile, vm, dma = (TILE, TILE), pltpu.VMEM, pltpu.SemaphoreType.DMA
    anywhere, inside = pl.BlockSpec(memory_space=pl.ANY), pl.BlockSpec(memory_space=pltpu.VMEM)
    wide = lambda *shape: jax.ShapeDtypeStruct(shape, F32)
    return pl.pallas_call(
        widen_kernel,
        out_shape=[
            wide(half_hidden, width), wide(width, half_hidden), wide(half_width, width), wide(3, width, half_width),
            jax.ShapeDtypeStruct(output.shape, output.dtype), jax.ShapeDtypeStruct(output.shape, output.dtype),
            wide(2, half_width), wide(width), wide(width), wide(width), wide(half_hidden), wide(width), wide(width), wide(width),
        ],
        in_specs=[inside] * 4,
        out_specs=[anywhere] * 6 + [inside] * 8,
        scratch_shapes=[
            vm((RING,) + tile, F32), dma((RING,)), dma((2,)),
        ],
        compiler_params=pltpu.CompilerParams(vmem_limit_bytes=16 << 20),
    )(tiles, output, grad_inputs, sums)


def split_by_sequence(
    inputs, lengths, w_qkv, b_qv, w_out, b_out, gain_one, shift_one, w_in, b_in, w_down, b_down, gain_two, shift_two,
    cotangent,
):
    rows, width = inputs.shape
    half_width, half_hidden = w_qkv.shape[2], w_in.shape[1]
    wq = w_qkv.transpose(1, 0, 2)
    vectors = (b_out, gain_one, shift_one, b_down, gain_two, shift_two, b_qv, b_in)
    made = layer(lengths, inputs, cotangent, wq, w_out, w_in, w_down, vectors)
    output, grad_inputs, tiles, sums = made[:4]
    (
        g_w_down, g_w_in, g_w_out, g_w_qkv, output, grad_inputs,
        g_b_qv, g_b_out, g_gain_one, g_shift_one, g_b_in, g_b_down, g_gain_two, g_shift_two,
    ) = widen(tiles, output, grad_inputs, sums, half_hidden, width, half_width)
    return (
        output, grad_inputs, g_w_qkv.transpose(1, 0, 2), g_b_qv, g_w_out, g_b_out, g_gain_one, g_shift_one,
        g_w_in, g_b_in, g_w_down, g_b_down, g_gain_two, g_shift_two,
    )


def solution(mesh):
    small_mesh = mesh.shape["tensor"] == 2 and mesh.shape["dp"] == 2 * N_X * N_Z
    step = split_by_sequence if small_mesh else general
    in_specs = (
        P(("dp", "tensor"), None),
        P("dp"),
        P(None, None, "tensor"),
        P(None, "tensor"),
        P("tensor", None),
        P(),
        P(),
        P(),
        P(None, "tensor"),
        P("tensor"),
        P("tensor", None),
        P(),
        P(),
        P(),
        P(("dp", "tensor"), None),
    )
    out_specs = (
        P(("dp", "tensor"), None),
        P(("dp", "tensor"), None),
        P(None, None, "tensor"),
        P(None, "tensor"),
        P("tensor", None),
        P(),
        P(),
        P(),
        P(None, "tensor"),
        P("tensor"),
        P("tensor", None),
        P(),
        P(),
        P(),
    )
    return jax.shard_map(step, mesh=mesh, in_specs=in_specs, out_specs=out_specs, check_vma=False)
```

```python
import jax
import jax.numpy as jnp
from jax import lax
from jax.experimental import pallas as pl
from jax.experimental.pallas import tpu as pltpu
from jax.sharding import PartitionSpec as P

MESH = pl.DeviceIdType.MESH
N_Z, N_X = 4, 2
TILE = 512
MESSAGES = 12
VMEM_BYTES = 63 << 20

HEAD = 64
SEQ = 512
SEQ_DEV = 2


EPSILON = 1e-12
NEG_FILL = -1000000000.0


def gelu_exact(values):
    return jax.nn.gelu(values, approximate=False)


def norm_forward(values, gain_vec, shift_vec):
    center = values - jnp.mean(values, axis=-1, keepdims=True)
    spread = jnp.mean(center * center, axis=-1, keepdims=True)
    inverse = lax.rsqrt(spread + EPSILON)
    scaled = center * inverse
    return (scaled * gain_vec + shift_vec, scaled, inverse)


def norm_backward(grad_out, scaled, inverse, gain_vec):
    grad_scaled = grad_out * gain_vec
    mean_one = jnp.mean(grad_scaled, axis=-1, keepdims=True)
    mean_two = jnp.mean(grad_scaled * scaled, axis=-1, keepdims=True)
    grad_in = inverse * (grad_scaled - mean_one - scaled * mean_two)
    return (grad_in, jnp.sum(grad_out * scaled, axis=0), jnp.sum(grad_out, axis=0))


def masked_scores(queries, key_rows, length):
    score_scale = HEAD ** (-0.5)
    scores = (
        jnp.einsum("qhe,khe->hqk", queries, key_rows, preferred_element_type=jnp.float32)
        * score_scale
    )
    key_valid = (jnp.arange(SEQ) < length)[None, None, :]
    return jnp.where(key_valid, scores, NEG_FILL)


def attend_forward(element):
    queries, key_rows, value_rows, length = element
    scores = masked_scores(queries, key_rows, length)
    peak_score = jnp.max(scores, axis=-1, keepdims=True)
    shifted_exp = jnp.exp(scores - peak_score)
    denominator = jnp.sum(shifted_exp, axis=-1, keepdims=True)
    probability = (shifted_exp / denominator).astype(jnp.bfloat16)
    context = jnp.einsum(
        "hqk,khe->qhe", probability, value_rows, preferred_element_type=jnp.float32
    )
    return (context.astype(jnp.bfloat16), (peak_score + jnp.log(denominator))[..., 0])


def attend_backward(element):
    queries, key_rows, value_rows, length, log_total, grad_context = element
    score_scale = HEAD ** (-0.5)
    scores = masked_scores(queries, key_rows, length)
    probability = jnp.exp(scores - log_total[..., None])
    grad_prob = jnp.einsum(
        "qhe,khe->hqk", grad_context, value_rows, preferred_element_type=jnp.float32
    )
    grad_value = jnp.einsum(
        "hqk,qhe->khe",
        probability.astype(jnp.bfloat16),
        grad_context,
        preferred_element_type=jnp.float32,
    )
    grad_scores = probability * (
        grad_prob - jnp.sum(probability * grad_prob, axis=-1, keepdims=True)
    )
    grad_scores = grad_scores.astype(jnp.bfloat16)
    grad_query = (
        jnp.einsum("hqk,khe->qhe", grad_scores, key_rows, preferred_element_type=jnp.float32)
        * score_scale
    )
    grad_key = (
        jnp.einsum("hqk,qhe->khe", grad_scores, queries, preferred_element_type=jnp.float32)
        * score_scale
    )
    return jnp.stack([grad_query, grad_key, grad_value], axis=1).astype(jnp.bfloat16)


def row_mask(lengths, rows_dev):
    places = lax.axis_index("tensor") * rows_dev + jnp.arange(rows_dev)
    sequence_of = places // SEQ
    offset = places % SEQ
    matches = sequence_of[:, None] == jnp.arange(lengths.shape[0])[None, :]
    limit_rows = jnp.sum(jnp.where(matches, lengths[None, :], 0), axis=1)
    return (offset < limit_rows).astype(jnp.float32)[:, None]


def forward_pass(inputs, lengths, weights):
    (
        w_qkv,
        b_qv,
        w_out,
        b_out,
        gain_one,
        shift_one,
        w_in,
        b_in,
        w_down,
        b_down,
        gain_two,
        shift_two,
    ) = weights
    width_dev = w_qkv.shape[2]
    gathered = lax.all_gather(inputs, "tensor", axis=0, tiled=True)
    bias_three = jnp.stack([b_qv[0], jnp.zeros_like(b_qv[0]), b_qv[1]]).astype(jnp.float32)
    projected = (
        jnp.einsum("td,dcf->tcf", gathered, w_qkv, preferred_element_type=jnp.float32) + bias_three
    ).astype(jnp.bfloat16)
    shaped = projected.reshape(SEQ_DEV, SEQ, 3, width_dev // HEAD, HEAD)
    context, log_total = lax.map(
        attend_forward, (shaped[:, :, 0], shaped[:, :, 1], shaped[:, :, 2], lengths)
    )
    context = context.reshape(SEQ_DEV * SEQ, width_dev)
    segment = context
    branch = lax.psum_scatter(
        jnp.dot(segment, w_out, preferred_element_type=jnp.float32).astype(jnp.bfloat16),
        "tensor",
        scatter_dimension=0,
        tiled=True,
    ).astype(jnp.float32) + b_out.astype(jnp.float32)
    normed, scaled_one, inverse_one = norm_forward(
        inputs.astype(jnp.float32) + branch,
        gain_one.astype(jnp.float32),
        shift_one.astype(jnp.float32),
    )
    normed_all = lax.all_gather(normed.astype(jnp.bfloat16), "tensor", axis=0, tiled=True)
    hidden = jnp.dot(normed_all, w_in, preferred_element_type=jnp.float32) + b_in.astype(
        jnp.float32
    )
    active = gelu_exact(hidden).astype(jnp.bfloat16)
    segment = active
    second = lax.psum_scatter(
        jnp.dot(segment, w_down, preferred_element_type=jnp.float32).astype(jnp.bfloat16),
        "tensor",
        scatter_dimension=0,
        tiled=True,
    ).astype(jnp.float32) + b_down.astype(jnp.float32)
    output, scaled_two, inverse_two = norm_forward(
        normed + second, gain_two.astype(jnp.float32), shift_two.astype(jnp.float32)
    )
    return (
        gathered,
        projected,
        context,
        log_total,
        scaled_one,
        inverse_one,
        normed_all,
        hidden,
        active,
        scaled_two,
        inverse_two,
        output,
    )


def general(
    inputs,
    lengths,
    w_qkv,
    b_qv,
    w_out,
    b_out,
    gain_one,
    shift_one,
    w_in,
    b_in,
    w_down,
    b_down,
    gain_two,
    shift_two,
    cotangent,
):
    weights = (
        w_qkv,
        b_qv,
        w_out,
        b_out,
        gain_one,
        shift_one,
        w_in,
        b_in,
        w_down,
        b_down,
        gain_two,
        shift_two,
    )
    first_pass = forward_pass(inputs, lengths, weights)
    output = first_pass[11].astype(jnp.bfloat16)
    recorded = forward_pass(inputs, lengths, weights)
    (
        gathered,
        projected,
        context,
        log_total,
        scaled_one,
        inverse_one,
        normed_all,
        hidden,
        active,
        scaled_two,
        inverse_two,
        _,
    ) = recorded
    rows_dev = inputs.shape[0]
    width_dev = w_qkv.shape[2]
    grad_out = cotangent.astype(jnp.float32) * row_mask(lengths, rows_dev)
    grad_two, grad_gain_two, grad_shift_two = norm_backward(
        grad_out, scaled_two, inverse_two, gain_two.astype(jnp.float32)
    )
    grad_second = grad_two.astype(jnp.bfloat16)
    grad_b_down = jnp.sum(grad_second.astype(jnp.float32), axis=0)
    second_all = lax.all_gather(grad_second, "tensor", axis=0, tiled=True)
    grad_w_down = jnp.einsum("tf,td->fd", active, second_all, preferred_element_type=jnp.float32)
    grad_active = jnp.einsum("td,fd->tf", second_all, w_down, preferred_element_type=jnp.float32)
    _, gelu_pull = jax.vjp(gelu_exact, hidden)
    grad_hidden = gelu_pull(grad_active)[0].astype(jnp.bfloat16)
    grad_b_in = jnp.sum(grad_hidden.astype(jnp.float32), axis=0)
    grad_w_in = jnp.einsum("td,tf->df", normed_all, grad_hidden, preferred_element_type=jnp.float32)
    segment = grad_hidden
    grad_normed = grad_two + lax.psum_scatter(
        jnp.einsum("tf,df->td", segment, w_in, preferred_element_type=jnp.float32).astype(
            jnp.bfloat16
        ),
        "tensor",
        scatter_dimension=0,
        tiled=True,
    ).astype(jnp.float32)
    grad_first, grad_gain_one, grad_shift_one = norm_backward(
        grad_normed, scaled_one, inverse_one, gain_one.astype(jnp.float32)
    )
    grad_branch = grad_first.astype(jnp.bfloat16)
    grad_b_out = jnp.sum(grad_branch.astype(jnp.float32), axis=0)
    branch_all = lax.all_gather(grad_branch, "tensor", axis=0, tiled=True)
    grad_w_out = jnp.einsum("tf,td->fd", context, branch_all, preferred_element_type=jnp.float32)
    grad_context = jnp.einsum(
        "td,fd->tf", branch_all, w_out, preferred_element_type=jnp.float32
    ).astype(jnp.bfloat16)
    heads_dev = width_dev // HEAD
    shaped = projected.reshape(SEQ_DEV, SEQ, 3, heads_dev, HEAD)
    grad_shaped = grad_context.reshape(SEQ_DEV, SEQ, heads_dev, HEAD)
    grad_proj = lax.map(
        attend_backward,
        (shaped[:, :, 0], shaped[:, :, 1], shaped[:, :, 2], lengths, log_total, grad_shaped),
    )
    grad_proj = grad_proj.reshape(SEQ_DEV * SEQ, 3, width_dev)
    grad_w_qkv = jnp.einsum("td,tcf->dcf", gathered, grad_proj, preferred_element_type=jnp.float32)
    grad_b_qv = jnp.sum(grad_proj[:, 0::2].astype(jnp.float32), axis=0)
    segment = grad_proj
    grad_inputs = (
        grad_first
        + lax.psum_scatter(
            jnp.einsum("tcf,dcf->td", segment, w_qkv, preferred_element_type=jnp.float32).astype(
                jnp.bfloat16
            ),
            "tensor",
            scatter_dimension=0,
            tiled=True,
        ).astype(jnp.float32)
    ).astype(jnp.bfloat16)
    small_terms = jnp.stack(
        [grad_gain_one, grad_shift_one, grad_b_out, grad_gain_two, grad_shift_two, grad_b_down]
    )
    grad_w_qkv, grad_b_qv, grad_w_out, grad_w_in, grad_b_in, grad_w_down, small_terms = (
        lax.psum(grad_w_qkv.astype(jnp.bfloat16), "dp").astype(jnp.float32),
        lax.psum(grad_b_qv.astype(jnp.bfloat16), "dp").astype(jnp.float32),
        lax.psum(grad_w_out.astype(jnp.bfloat16), "dp").astype(jnp.float32),
        lax.psum(grad_w_in.astype(jnp.bfloat16), "dp").astype(jnp.float32),
        lax.psum(grad_b_in.astype(jnp.bfloat16), "dp").astype(jnp.float32),
        lax.psum(grad_w_down.astype(jnp.bfloat16), "dp").astype(jnp.float32),
        lax.psum(small_terms.astype(jnp.bfloat16), "dp").astype(jnp.float32),
    )
    small_sums = lax.psum(small_terms, "tensor")
    return (
        output,
        grad_inputs,
        grad_w_qkv,
        grad_b_qv,
        grad_w_out,
        small_sums[2],
        small_sums[0],
        small_sums[1],
        grad_w_in,
        grad_b_in,
        grad_w_down,
        small_sums[5],
        small_sums[3],
        small_sums[4],
    )


def place():
    dp = lax.axis_index("dp")
    return dp // (2 * N_X), (dp // 2) % N_X, dp % 2, lax.axis_index("tensor")


def at(z, x, c, y):
    return ((z * N_X + x) * 2 + c, y)


def greet(peers):
    barrier = pltpu.get_barrier_semaphore()
    for peer in peers:
        pl.semaphore_signal(barrier, inc=1, device_id=peer, device_id_type=MESH)
    pl.semaphore_wait(barrier, len(peers))


def copy_to(src, dst, send_sem, recv_sem, peer):
    return pltpu.make_async_remote_copy(
        src_ref=src, dst_ref=dst, send_sem=send_sem, recv_sem=recv_sem,
        device_id=peer, device_id_type=MESH,
    )


CHUNKS = 24
RING = 4
BF, F32 = jnp.bfloat16, jnp.float32
ROWS_AT_ONCE = 128


def dot(a, b, ca, cb):
    return lax.dot_general(a, b, (((ca,), (cb,)), ((), ())), preferred_element_type=F32)


def span(index, size):
    return pl.ds(pl.multiple_of(index * size, size), size)


def tile_place(k):
    if k < 8:
        return 0, (slice(k // 2 * TILE, (k // 2 + 1) * TILE), slice(k % 2 * TILE, (k % 2 + 1) * TILE))
    if k < 16:
        k -= 8
        return 1, (slice(k % 2 * TILE, (k % 2 + 1) * TILE), slice(k // 2 * TILE, (k // 2 + 1) * TILE))
    if k < 18:
        k -= 16
        return 2, (slice(0, TILE), slice(k * TILE, (k + 1) * TILE))
    k -= 18
    return 3, (k // 2, slice(k % 2 * TILE, (k % 2 + 1) * TILE), slice(0, TILE))


def layer_kernel(
    lengths, x_hbm, cot_hbm, wq_own, wo_own, wi_own, wd_own, in1, in2, in3, in4, in5, in6, in_qv, in_hidden,
    out_ref, gin_ref, oth, small_out, wq_oth, wo_oth, wi_oth, wd_oth, e_hbm,
    xv, nlow, gsec, gctx, ctx, qkv, inv, xhat, rs1, acc, u1, u2, own, r1, ry, rx, rz,
    ring_a, ring_b, vec, bias_own, bias_oth, small, s0, s1, s2, s3, s4,
    load_sem, w_sem, a_sem, b_sem, e_sem, g_send, g_recv, send, recv, small_send, small_recv,
):
    z, x, c, y = place()
    zb = z % 2
    z_of = [(z + d) % N_Z for d in (1, 2, 3)]
    to_c, to_y, to_x = at(z, x, 1 - c, y), at(z, x, c, 1 - y), at(z, 1 - x, c, y)
    to_z = [at(v, x, c, y) for v in z_of]
    to_zp, to_zq = at(z + 1 - 2 * zb, x, c, y), at((z + 2) % N_Z, x, c, y)
    seq, width = xv.shape
    half_w = width // 2

    load_x = pltpu.make_async_copy(x_hbm, xv, load_sem.at[0])
    load_cot = pltpu.make_async_copy(cot_hbm, gsec, load_sem.at[1])
    load_x.start()
    load_cot.start()
    for row, ref in enumerate((in1, in2, in3, in4, in5, in6)):
        vec[row : row + 1, :] = ref[...].astype(F32).reshape(1, width)
    bias_own[0:2, :] = in_qv[...].astype(F32)
    bias_own[2:6, :] = in_hidden[...].astype(F32).reshape(4, TILE)

    def fetch_qkv(h, i):
        source = (wq_own, wq_oth)[h]
        return pltpu.make_async_copy(source.at[i], ring_b.at[i], b_sem.at[i])

    def fetch_out(h):
        return pltpu.make_async_copy((wo_own, wo_oth)[h], ring_a.at[h], a_sem.at[h])

    def fetch_in(h, f, slot):
        return pltpu.make_async_copy((wi_own, wi_oth)[h].at[:, span(f, TILE)], ring_b.at[slot], b_sem.at[slot])

    def fetch_down(h, f, slot):
        return pltpu.make_async_copy((wd_own, wd_oth)[h].at[span(f, TILE)], ring_a.at[slot], a_sem.at[slot])

    def weight_load(h, k):
        which, where = tile_place(k)
        source = ((wd_own, wi_own, wo_own, wq_own), (wd_oth, wi_oth, wo_oth, wq_oth))[h][which]
        return pltpu.make_async_copy(source.at[where], (own, oth)[h].at[k], w_sem.at[h, k])

    for k in (*range(18, 24), *range(8, 16), *range(0, 8), 16, 17):
        weight_load(0, k).start()

    greet([to_c, to_y, to_x] + to_z)

    cut = wi_own.shape[1] // 2
    deep = wd_own.shape[0] // 2
    arrays = [(wq_own.at[i], wq_oth.at[i]) for i in range(3)] + [(wo_own, wo_oth)]
    arrays += [(wi_own.at[:, j * cut : (j + 1) * cut], wi_oth.at[:, j * cut : (j + 1) * cut]) for j in range(2)]
    arrays += [(wd_own.at[j * deep : (j + 1) * deep], wd_oth.at[j * deep : (j + 1) * deep]) for j in range(2)]
    loads_of = [(18, 19), (20, 21), (22, 23), (16, 17), (8, 9, 10, 11), (12, 13, 14, 15), (0, 1, 2, 3), (4, 5, 6, 7)]
    count = len(arrays)

    def gather_message(n, kind):
        size = arrays[n][0].shape[0] // 2
        size_part = size // 8 - (16 if n >= 4 else 0)
        near_a, near_b = 2 * zb, 4 + 2 * x
        far_a, far_b = 2 * (1 - zb), 4 + 2 * (1 - x)
        one_a, one_b = 2 * zb + x, 4 + 2 * x + zb
        first, parts, peer = [
            (one_a, 1, to_y), (one_b, 1, to_y), (one_a, 1, to_x), (one_b, 1, to_zp),
            (near_a, 2, to_zp), (near_b, 2, to_x), (near_a, 2, to_c), (near_b, 2, to_c), (far_a, 2, to_c), (far_b, 2, to_c),
            (8, 0, to_y), (8, 0, to_c),
        ][kind]
        length_rows = parts * size_part if parts else size - 8 * size_part
        rows = pl.ds(pl.multiple_of(c * size + first * size_part, 8), length_rows)
        source = arrays[n][0 if kind in (0, 1, 10) else 1]
        return copy_to(source.at[rows], arrays[n][1].at[rows], g_send.at[n, kind], g_recv.at[n, kind], peer)

    def gather_stage(n, step):
        if step == 0:
            gather_message(n, 0).wait_recv()
            gather_message(n, 2).start()
            gather_message(n, 1).wait_recv()
            gather_message(n, 3).start()
        if step == 1:
            gather_message(n, 2).wait_recv()
            gather_message(n, 4).start()
            gather_message(n, 6).start()
            gather_message(n, 3).wait_recv()
            gather_message(n, 5).start()
            gather_message(n, 7).start()
        if step == 2:
            gather_message(n, 4).wait_recv()
            gather_message(n, 8).start()
            gather_message(n, 5).wait_recv()
            gather_message(n, 9).start()
            if n >= 4:
                gather_message(n, 10).wait_recv()
                gather_message(n, 11).start()
        if step == 3:
            kinds = range(12 if n >= 4 else 10)
            for kind in kinds:
                if kind >= 6 and kind != 10:
                    gather_message(n, kind).wait_recv()
            for k in loads_of[n]:
                weight_load(1, k).start()
            for kind in kinds:
                gather_message(n, kind).wait_send()

    def progress(slot):
        for step in range(4):
            if 0 <= slot - step < count:
                gather_stage(slot - step, step)

    send_bias = copy_to(bias_own, bias_oth, g_send.at[count, 0], g_recv.at[count, 0], to_y)
    send_bias.start()
    for n in (0, 1, 2, 3, 4, 5, -4, 6, -5, 7, -6, -7):
        for kind in (0, 1) if n >= 0 else (10,):
            gather_message(abs(n), kind).start()

    length = lengths[y]
    key_fill = jnp.where(lax.broadcasted_iota(jnp.int32, (1, seq), 1) < length, 0.0, NEG_FILL)
    low_lanes = lax.broadcasted_iota(jnp.int32, (1, 128), 1) < HEAD
    one, zero = jnp.ones((), BF), jnp.zeros((), BF)
    scale = HEAD ** (-0.5)
    pairs = half_w // 128

    def project(h):
        bias = (bias_own, bias_oth)[h]
        for i in range(3):
            for k in (18 + 2 * i, 19 + 2 * i):
                weight_load(h, k).wait()
            value = dot(xv[...], (own, oth)[h][18 + 2 * i : 20 + 2 * i].reshape(width, TILE), 1, 0)
            if i == 0:
                qkv[h, 0] = (value + bias[0:1, :]).astype(BF) * jnp.asarray(scale, BF)
            if i == 1:
                qkv[h, 1] = value.astype(BF)
            if i == 2:
                qkv[h, 2] = (value + bias[1:2, :]).astype(BF)

    def attend(h, p, e_ref):
        lanes = span(p, 128)
        q2, k2, v2 = qkv[h, 0, :, lanes], qkv[h, 1, :, lanes], qkv[h, 2, :, lanes]
        parts = []
        for head in range(2):
            mine = low_lanes if head == 0 else jnp.logical_not(low_lanes)
            scores = dot(jnp.where(mine, q2, zero), k2, 1, 1) + key_fill
            peak = jnp.max(scores, axis=-1, keepdims=True)
            e = jnp.exp(scores - peak).astype(BF)
            e_ref[2 * p + head] = e
            parts.append(dot(e, jnp.where(mine, v2, one), 1, 0))
        total = pltpu.roll(jnp.where(low_lanes, parts[1], parts[0]), HEAD, 1)
        inverse = 1.0 / total
        inv[h, :, lanes] = inverse
        ctx[:, span(h * pairs + p, 128)] = (jnp.where(low_lanes, parts[0], parts[1]) * inverse).astype(BF)

    def attend_half(h, slots):
        def body(p, _):
            attend(h, p, (u1, u2)[h])
            for at_pair, slot in slots:
                @pl.when(p == at_pair)
                def _():
                    progress(slot)
            return 0
        lax.fori_loop(0, pairs, body, 0)

    def e_copy(h, back):
        ref, buf = e_hbm.at[pl.ds(h * 8, 8)], (u1 if back else (u1, u2)[h])
        return pltpu.make_async_copy(ref, buf, e_sem.at[h]) if back else pltpu.make_async_copy(buf, ref, e_sem.at[h])

    def out_project(h):
        for d in range(2):
            weight_load(h, 16 + d).wait()
            term = dot(ctx[:, h * half_w : (h + 1) * half_w], (own, oth)[h][16 + d], 1, 0)
            lanes = slice(d * TILE, (d + 1) * TILE)
            acc[:, lanes] = term if h == 0 else acc[:, lanes] + term

    load_x.wait()
    project(0)
    attend_half(0, ((1, 0), (3, 1)))
    e_copy(0, False).start()
    out_project(0)
    for slot in (2, 3, 4, 5):
        progress(slot)
    send_bias.wait()
    project(1)
    attend_half(1, ((1, 6),))
    e_copy(1, False).start()
    out_project(1)

    def blocks(body):
        def run(b, _):
            body(span(b, ROWS_AT_ONCE), b)
            return 0
        lax.fori_loop(0, seq // ROWS_AT_ONCE, run, 0)

    def mean(v):
        return jnp.sum(v, axis=-1, keepdims=True) * (1.0 / width)

    small[...] = jnp.zeros_like(small)
    b_out, gain1, shift1 = vec[0:1, :], vec[1:2, :], vec[2:3, :]
    b_down, gain2, shift2 = vec[3:4, :], vec[4:5, :], vec[5:6, :]

    def norm_one(r, b):
        v = xv[r, :].astype(F32) + (acc[r, :] + b_out)
        center = v - mean(v)
        inverse = lax.rsqrt(mean(center * center) + EPSILON)
        hat = center * inverse
        xhat[r, :] = hat
        rs1[r, :] = jnp.broadcast_to(inverse, (ROWS_AT_ONCE, 128))
        nlow[r, :] = (hat * gain1 + shift1).astype(BF)
    blocks(norm_one)
    e_copy(0, False).wait()
    e_copy(1, False).wait()
    progress(7)

    def hidden_half(h, slots):
        bias, weights = (bias_own, bias_oth)[h], (own, oth)[h]
        for f in range(4):
            for k in (8 + 2 * f, 9 + 2 * f):
                weight_load(h, k).wait()
            hidden = dot(nlow[...], weights[8 + 2 * f : 10 + 2 * f].reshape(width, TILE), 1, 0) + bias[2 + f : 3 + f, :]
            cdf = 0.5 + 0.5 * lax.erf(hidden * 0.7071067811865476)
            u1[4 * h + f] = (hidden * cdf).astype(BF)
            u2[4 * h + f] = (cdf + hidden * (jnp.exp(hidden * hidden * -0.5) * 0.3989422804014327)).astype(BF)
            if f in slots:
                progress(slots[f])

    def down_half(h, tiles, clear=False):
        for f in tiles:
            for d in range(2):
                weight_load(h, 2 * f + d).wait()
                term = dot(u1[4 * h + f], (own, oth)[h][2 * f + d], 1, 0)
                lanes = slice(d * TILE, (d + 1) * TILE)
                acc[:, lanes] = term if clear and f == tiles[0] else acc[:, lanes] + term

    hidden_half(0, {})
    down_half(0, (0, 1), True)
    progress(8)
    down_half(0, (2, 3))
    hidden_half(1, {3: 9})
    down_half(1, (0, 1))
    progress(10)
    down_half(1, (2, 3))

    load_cot.wait()
    valid_limit = lengths[y]

    def norm_two(r, b):
        normed = xhat[r, :] * gain1 + shift1
        v = normed + (acc[r, :] + b_down)
        center = v - mean(v)
        inverse = lax.rsqrt(mean(center * center) + EPSILON)
        hat = center * inverse
        out_ref[r, :] = (hat * gain2 + shift2).astype(BF)
        position = b * ROWS_AT_ONCE + lax.broadcasted_iota(jnp.int32, (ROWS_AT_ONCE, 1), 0)
        g_out = jnp.where(position < valid_limit, gsec[r, :].astype(F32), 0.0)
        scaled = g_out * gain2
        g_two = inverse * (scaled - mean(scaled) - hat * mean(scaled * hat))
        low = g_two.astype(BF)
        acc[r, :] = g_two
        gsec[r, :] = low
        small[3:4, :] += jnp.sum(g_out * hat, axis=0, keepdims=True)
        small[4:5, :] += jnp.sum(g_out, axis=0, keepdims=True)
        small[5:6, :] += jnp.sum(low.astype(F32), axis=0, keepdims=True)
    blocks(norm_two)

    half, quarter, part = TILE // 2, TILE // 4, TILE // 16
    c_rows = span(c, half)
    cn_rows = span(1 - c, half)
    x_rows = pl.ds(pl.multiple_of(c * half + x * quarter, quarter), quarter)
    xn_rows = pl.ds(pl.multiple_of(c * half + (1 - x) * quarter, quarter), quarter)

    def z_rows(v):
        return pl.ds(pl.multiple_of(c * half + x * quarter + v * part, part), part)

    def message(k, kind):
        slot = k % RING
        if kind == 0: src, dst, peer = own.at[k, cn_rows], r1.at[slot, 0], to_c
        if kind == 1: src, dst, peer = oth.at[k, cn_rows], r1.at[slot, 1], to_c
        if kind == 2: src, dst, peer = oth.at[k, c_rows], ry.at[slot], to_y
        if kind == 3: src, dst, peer = own.at[k, xn_rows], rx.at[slot], to_x
        if 4 <= kind < 7: src, dst, peer = own.at[k, z_rows(z_of[kind - 4])], rz.at[slot, kind - 4], to_z[kind - 4]
        if 7 <= kind < 10: src, dst, peer = oth.at[k, z_rows(z)], oth.at[k, z_rows(z)], to_z[kind - 7]
        if kind == 10: src, dst, peer = oth.at[k, x_rows], oth.at[k, x_rows], to_x
        if kind == 11: src, dst, peer = oth.at[k, c_rows], oth.at[k, c_rows], to_c
        return copy_to(src, dst, send.at[slot, kind], recv.at[slot, kind], peer)

    def add_into(dst, src, n):
        def body(i, _):
            r = span(i, 64)
            dst[r, :] = dst[r, :] + src[r, :]
            return 0
        lax.fori_loop(0, n // 64, body, 0)

    def wait(k, kinds):
        for kind in kinds:
            message(k, kind).wait()

    def reduce_stage(k, s):
        slot = k % RING
        if s == 0:
            message(k, 0).start()
            message(k, 1).start()
        if s == 1:
            wait(k, (0, 1))
            add_into(oth.at[k, c_rows], r1.at[slot, 1], half)
            message(k, 2).start()
            add_into(own.at[k, c_rows], r1.at[slot, 0], half)
        if s == 2:
            wait(k, (2,))
            add_into(own.at[k, c_rows], ry.at[slot], half)
            message(k, 3).start()
        if s == 3:
            wait(k, (3,))
            add_into(own.at[k, x_rows], rx.at[slot], quarter)
            for kind in (4, 5, 6):
                message(k, kind).start()
        if s == 4:
            wait(k, (4, 5, 6))
            total = own[k, z_rows(z), :].astype(F32)
            for d in range(3):
                total = total + rz[slot, d].astype(F32)
            oth[k, z_rows(z), :] = total.astype(BF)
            for kind in (7, 8, 9):
                message(k, kind).start()
        if s == 5:
            wait(k, (7, 8, 9))
            message(k, 10).start()
        if s == 6:
            wait(k, (10,))
            message(k, 11).start()
        if s == 7:
            wait(k, (11,))

    def reduce_step(t, stages):
        for s in stages:
            @pl.when((t >= s) & (t - s < CHUNKS))
            def _():
                reduce_stage(t - s, s)

    def small_messages(i):
        if i == 0:
            return [copy_to(small, s0, small_send.at[0], small_recv.at[0], to_c)]
        if i == 1:
            return [
                copy_to(small.at[pl.ds(0, 8)], s1.at[pl.ds(0, 8)], small_send.at[1], small_recv.at[1], to_y),
                copy_to(small.at[pl.ds(16, 8)], s1.at[pl.ds(8, 8)], small_send.at[2], small_recv.at[2], to_y),
            ]
        got, peer = ((s2, to_x), (s3, to_zp), (s4, to_zq))[i - 2]
        return [copy_to(small.at[pl.ds(0, 16)], got, small_send.at[i + 1], small_recv.at[i + 1], peer)]

    def small_step(i):
        if i > 0:
            for m in small_messages(i - 1):
                m.wait()
            if i == 1:
                small[...] = small[...] + s0[...]
            else:
                small[0:16, :] = small[0:16, :] + (s1, s2, s3, s4)[i - 2][...]
        if i < 5:
            for m in small_messages(i):
                m.start()

    def fetch_ffn(t, start):
        for h in range(2):
            @pl.when((t >= 4 * h) & (t < 4 * h + 4))
            def _():
                b, a = fetch_in(h, t - 4 * h, t % 3), fetch_down(h, t - 4 * h, t % 2)
                if start:
                    b.start()
                    a.start()
                else:
                    b.wait()
                    a.wait()

    def down_tiles(k):
        g = gsec[:, span(k % 2, TILE)]
        own[k] = dot(u1[k // 2], g, 0, 0).astype(BF)
        oth[k] = dot(u1[4 + k // 2], g, 0, 0).astype(BF)

    def hidden_back(t):
        fetch_ffn(t, False)
        g_active = dot(gsec[...], ring_a[t % 2], 1, 1)
        g_hidden = (g_active * u2[t].astype(F32)).astype(BF)
        u2[t] = g_hidden
        total = jnp.sum(g_hidden.astype(F32), axis=0, keepdims=True)
        small[pl.ds(9 + 8 * (t // 4) + (t % 4) // 2, 1), span(t % 2, TILE)] = total
        acc[...] += dot(g_hidden, ring_b[t % 3], 1, 1)

    def in_tiles(k):
        j = k - 8
        a = nlow[:, span(j % 2, TILE)]
        own[k] = dot(a, u2[j // 2], 0, 0).astype(BF)
        oth[k] = dot(a, u2[4 + j // 2], 0, 0).astype(BF)

    def norm_one_back(r, b):
        g_normed, hat = acc[r, :], xhat[r, :]
        scaled = g_normed * gain1
        g_first = rs1[r, 0:1] * (scaled - mean(scaled) - hat * mean(scaled * hat))
        low = g_first.astype(BF)
        acc[r, :] = g_first
        gsec[r, :] = low
        small[0:1, :] += jnp.sum(g_normed * hat, axis=0, keepdims=True)
        small[1:2, :] += jnp.sum(g_normed, axis=0, keepdims=True)
        small[2:3, :] += jnp.sum(low.astype(F32), axis=0, keepdims=True)

    def attend_back(h, p):
        lanes = span(p, 128)
        wide = span(h * pairs + p, 128)
        q2, k2, v2 = qkv[h, 0, :, lanes], qkv[h, 1, :, lanes], qkv[h, 2, :, lanes]
        g = gctx[:, wide].astype(F32) * inv[h, :, lanes]
        low = g.astype(BF)
        less = pltpu.roll(-(g * ctx[:, wide].astype(F32)), HEAD, 1).astype(BF)
        g_q, g_k, g_v = [], [], []
        for head in range(2):
            mine = low_lanes if head == 0 else jnp.logical_not(low_lanes)
            e = u1[2 * p + head]
            g_scores = (dot(jnp.where(mine, low, less), jnp.where(mine, v2, one), 1, 1) * e.astype(F32)).astype(BF)
            g_q.append(dot(g_scores, k2, 1, 0))
            rows = slice(head * HEAD, head * HEAD + HEAD)
            g_k.append(dot(q2, g_scores, 0, 0)[rows])
            g_v.append(dot(low, e, 0, 0)[rows])
        qkv[h, 0, :, lanes] = (jnp.where(low_lanes, g_q[0], g_q[1]) * scale).astype(BF)
        qkv[h, 1, :, lanes] = jnp.concatenate(g_k, axis=0).T.astype(BF)
        qkv[h, 2, :, lanes] = jnp.concatenate(g_v, axis=0).T.astype(BF)

    fetch_ffn(0, True)

    def iteration(t, _):
        @pl.when(t < 8)
        def _():
            down_tiles(t)
        @pl.when((t >= 8) & (t < 16))
        def _():
            in_tiles(t)
        @pl.when((t >= 16) & (t < 18))
        def _():
            g = gsec[:, span(t - 16, TILE)]
            own[t] = dot(ctx[:, :half_w], g, 0, 0).astype(BF)
            oth[t] = dot(ctx[:, half_w:], g, 0, 0).astype(BF)
        @pl.when((t >= 18) & (t < 24))
        def _():
            j = t - 18
            a = xv[:, span(j % 2, TILE)]
            own[t] = dot(a, qkv[0, j // 2], 0, 0).astype(BF)
            oth[t] = dot(a, qkv[1, j // 2], 0, 0).astype(BF)
        reduce_step(t, (0, 1, 2))
        @pl.when(t < 8)
        def _():
            @pl.when(t < 7)
            def _():
                fetch_ffn(t + 1, True)
            hidden_back(t)
        @pl.when(t == 8)
        def _():
            e_copy(0, True).start()
            fetch_out(0).start()
            fetch_out(1).start()
            blocks(norm_one_back)
        @pl.when(t == 9)
        def _():
            for h in range(2):
                fetch_out(h).wait()
                gctx[:, h * half_w : (h + 1) * half_w] = dot(gsec[...], ring_a[h], 1, 1).astype(BF)
            e_copy(0, True).wait()
        for first, h in ((10, 0), (13, 1)):
            @pl.when((t >= first) & (t < first + 2))
            def _():
                def body(p, _):
                    attend_back(h, 2 * (t - first) + p)
                    return 0
                lax.fori_loop(0, 2, body, 0)
            @pl.when(t == first + 1)
            def _():
                if h == 0:
                    e_copy(1, True).start()
                for i in (0, 2):
                    total = jnp.sum(qkv[h, i].astype(F32), axis=0, keepdims=True)
                    small[8 + 8 * h : 9 + 8 * h, (i // 2) * TILE : (i // 2 + 1) * TILE] = total
        @pl.when(t == 12)
        def _():
            e_copy(1, True).wait()
        for h in range(2):
            first = 15 + 2 * h
            @pl.when(t == first)
            def _():
                for i in range(3):
                    fetch_qkv(h, i).start()
            @pl.when(t == first + 1)
            def _():
                for i in range(3):
                    fetch_qkv(h, i).wait()
                    acc[...] += dot(qkv[h, i], ring_b[i], 1, 1)
        @pl.when(t == 19)
        def _():
            def last(r, b):
                gin_ref[r, :] = acc[r, :].astype(BF)
            blocks(last)
        for i in range(6):
            @pl.when(t == 16 + i)
            def _():
                small_step(i)
        reduce_step(t, range(3, 8))
        return 0

    lax.fori_loop(0, CHUNKS + 7, iteration, 0)
    small_out[...] = small[0:16, :]


def layer(lengths, inputs, cotangent, wq, w_out, w_in, w_down, vectors):
    seq, width = inputs.shape
    half = TILE // 2
    vm, dma = pltpu.VMEM, pltpu.SemaphoreType.DMA
    anywhere, inside = pl.BlockSpec(memory_space=pl.ANY), pl.BlockSpec(memory_space=pltpu.VMEM)
    like = lambda a: jax.ShapeDtypeStruct(a.shape, a.dtype)
    tile_shape = (TILE, TILE)
    return pl.pallas_call(
        layer_kernel,
        out_shape=[
            pltpu.VMEM(inputs.shape, BF), pltpu.VMEM(inputs.shape, BF), pltpu.VMEM((CHUNKS,) + tile_shape, BF),
            pltpu.VMEM((16, width), F32),
            like(wq), like(w_out), like(w_in), like(w_down),
            jax.ShapeDtypeStruct((16,) + tile_shape, BF),
        ],
        in_specs=[pl.BlockSpec(memory_space=pltpu.SMEM)] + [anywhere] * 6 + [inside] * 8,
        out_specs=[inside] * 4 + [anywhere] * 5,
        scratch_shapes=[
            vm((seq, width), BF), vm((seq, width), BF), vm((seq, width), BF), vm((seq, width), BF), vm((seq, width), BF),
            vm((2, 3) + tile_shape, BF), vm((2,) + tile_shape, F32),
            vm((seq, width), F32), vm((seq, 128), F32), vm((seq, width), F32),
            vm((8,) + tile_shape, BF), vm((8,) + tile_shape, BF),
            vm((CHUNKS,) + tile_shape, BF),
            vm((RING, 2, half, TILE), BF), vm((RING, half, TILE), BF),
            vm((RING, half // 2, TILE), BF), vm((RING, 3, half // 8, TILE), BF),
            vm((2, TILE, width), BF), vm((3, width, TILE), BF),
            vm((8, width), F32), vm((8, TILE), F32), vm((8, TILE), F32), vm((24, width), F32), vm((24, width), F32),
            vm((16, width), F32), vm((16, width), F32), vm((16, width), F32), vm((16, width), F32),
            dma((2,)), dma((2, CHUNKS)), dma((2,)), dma((3,)), dma((2,)),
            dma((9, 12)), dma((9, 12)), dma((RING, MESSAGES)), dma((RING, MESSAGES)), dma((6,)), dma((6,)),
        ],
        compiler_params=pltpu.CompilerParams(
            collective_id=1, has_side_effects=True, vmem_limit_bytes=47 << 20
        ),
    )(lengths, inputs, cotangent, wq, w_out, w_in, w_down, *vectors)


def widen_kernel(
    tiles, out_in, gin_in, sums, down, within, out, three, out_out, gin_out,
    b_qv, b_out, gain1, shift1, b_in, b_down, gain2, shift2, wide, out_sem, pass_sem,
):
    leave = [pltpu.make_async_copy(ref, to, pass_sem.at[i]) for i, (ref, to) in enumerate(((out_in, out_out), (gin_in, gin_out)))]
    for copy in leave:
        copy.start()
    width, half = sums.shape[1], b_qv.shape[1]
    for ref, row in ((gain1, 0), (shift1, 1), (b_out, 2), (gain2, 3), (shift2, 4), (b_down, 5)):
        ref[...] = sums[row, :]
    for i in range(2):
        b_qv[i : i + 1, :] = sums[8:9, i * half : (i + 1) * half]
        b_in[i * width : (i + 1) * width] = sums[9 + i, :]

    def store(k):
        which, where = tile_place(k)
        return pltpu.make_async_copy(wide.at[k % RING], (down, within, out, three)[which].at[where], out_sem.at[k % RING])

    stores = [store(k) for k in range(CHUNKS)]
    for k in range(CHUNKS):
        if k >= RING:
            stores[k - RING].wait()
        def body(i, _):
            r = span(i, 32)
            wide[k % RING, r, :] = tiles[k, r, :].astype(F32)
            return 0
        lax.fori_loop(0, TILE // 32, body, 0)
        stores[k].start()
    for copy in stores[CHUNKS - RING :] + leave:
        copy.wait()


def widen(tiles, output, grad_inputs, sums, half_hidden, width, half_width):
    tile, vm, dma = (TILE, TILE), pltpu.VMEM, pltpu.SemaphoreType.DMA
    anywhere, inside = pl.BlockSpec(memory_space=pl.ANY), pl.BlockSpec(memory_space=pltpu.VMEM)
    wide = lambda *shape: jax.ShapeDtypeStruct(shape, F32)
    return pl.pallas_call(
        widen_kernel,
        out_shape=[
            wide(half_hidden, width), wide(width, half_hidden), wide(half_width, width), wide(3, width, half_width),
            jax.ShapeDtypeStruct(output.shape, output.dtype), jax.ShapeDtypeStruct(output.shape, output.dtype),
            wide(2, half_width), wide(width), wide(width), wide(width), wide(half_hidden), wide(width), wide(width), wide(width),
        ],
        in_specs=[inside] * 4,
        out_specs=[anywhere] * 6 + [inside] * 8,
        scratch_shapes=[
            vm((RING,) + tile, F32), dma((RING,)), dma((2,)),
        ],
        compiler_params=pltpu.CompilerParams(vmem_limit_bytes=16 << 20),
    )(tiles, output, grad_inputs, sums)


def split_by_sequence(
    inputs, lengths, w_qkv, b_qv, w_out, b_out, gain_one, shift_one, w_in, b_in, w_down, b_down, gain_two, shift_two,
    cotangent,
):
    rows, width = inputs.shape
    half_width, half_hidden = w_qkv.shape[2], w_in.shape[1]
    wq = w_qkv.transpose(1, 0, 2)
    vectors = (b_out, gain_one, shift_one, b_down, gain_two, shift_two, b_qv, b_in)
    made = layer(lengths, inputs, cotangent, wq, w_out, w_in, w_down, vectors)
    output, grad_inputs, tiles, sums = made[:4]
    (
        g_w_down, g_w_in, g_w_out, g_w_qkv, output, grad_inputs,
        g_b_qv, g_b_out, g_gain_one, g_shift_one, g_b_in, g_b_down, g_gain_two, g_shift_two,
    ) = widen(tiles, output, grad_inputs, sums, half_hidden, width, half_width)
    return (
        output, grad_inputs, g_w_qkv.transpose(1, 0, 2), g_b_qv, g_w_out, g_b_out, g_gain_one, g_shift_one,
        g_w_in, g_b_in, g_w_down, g_b_down, g_gain_two, g_shift_two,
    )


def solution(mesh):
    small_mesh = mesh.shape["tensor"] == 2 and mesh.shape["dp"] == 2 * N_X * N_Z
    step = split_by_sequence if small_mesh else general
    in_specs = (
        P(("dp", "tensor"), None),
        P("dp"),
        P(None, None, "tensor"),
        P(None, "tensor"),
        P("tensor", None),
        P(),
        P(),
        P(),
        P(None, "tensor"),
        P("tensor"),
        P("tensor", None),
        P(),
        P(),
        P(),
        P(("dp", "tensor"), None),
    )
    out_specs = (
        P(("dp", "tensor"), None),
        P(("dp", "tensor"), None),
        P(None, None, "tensor"),
        P(None, "tensor"),
        P("tensor", None),
        P(),
        P(),
        P(),
        P(None, "tensor"),
        P("tensor"),
        P("tensor", None),
        P(),
        P(),
        P(),
    )
    return jax.shard_map(step, mesh=mesh, in_specs=in_specs, out_specs=out_specs, check_vma=False)
```
